32 devices in a mesh: ens: 2 (over y), lat: 4 (over z), lon: 4 (over x, core).
Axes of the slice: x: 2, y: 2, z: 4, core: 2. Of those that a mesh axis runs over, the one named last changes fastest.
Arguments:
- sample_quantities: bfloat16 [2, 24, 256, 512], P('ens', None, 'lat', 'lon'), may hold values from -6 to 6
- conv_weight: bfloat16 [216, 256], replicated, may hold values from -0.4375 to 0.4375
- conv_bias: float32 [256], replicated, may hold values from -3 to 3
- out_weight: bfloat16 [256, 24], replicated, may hold values from -0.375 to 0.375
- obs_index: int32 [4, 4, 256], P('lat', 'lon'), may hold values from 0 to 196607
- obs_count: int32 [4, 4], P('lat', 'lon'), may hold values from 85 to 256, as said below
- obs_value: float32 [4, 4, 256], P('lat', 'lon'), may hold values from -8 to 8
- obs_weight: float32 [4, 4, 256], P('lat', 'lon'), may hold values from 0.002 to 0.03
Outputs:
- updated_estimates: bfloat16 [2, 24, 256, 512], P('ens', None, 'lat', 'lon')
The draws below stay inside these ranges and needn't reach their ends.
Inputs may be any that keep to these rules, and one draw needn't show every extreme that they name: `obs_index`: flat index v * 64 * 128 + r * 128 + c into the own shard's block; slots at or past the shard's count are unused. `obs_count`: some shard has exactly 256 live slots.
All inputs are finite; a program needn't handle non-finite values.
Results may differ from the reference program's by a relative error of at most 0.0075.
Values may be sent and summed in bfloat16 or wider, within the bound.
No kernel may reach another device: no remote copies, remote signals or barrier semaphores. Data moves between devices by JAX's collectives and lax.ppermute only.
A program may use at most 64 MiB of HBM per device.

```python
import math
import jax
import jax.numpy as jnp
from jax import lax

EVOLVED_QUANTITY = 24
HID = 256
PARALLEL_LINES = 64
MERIDIAN_LINES = 128
OBS_DEV = 256
NS_ITERS = 20
MEMBERS = 2
NLAT = 256
NLON = 512
N_LAT = 4
N_LON = 4


def draw_obs_count(key, part):
    first, second = jax.random.split(jax.random.fold_in(key, 11))
    shards = N_LAT * N_LON
    counts = jax.random.randint(first, (shards,), OBS_DEV // 3, OBS_DEV + 1)
    chosen = jax.random.randint(second, (), 0, shards)
    counts = jnp.where(jnp.arange(shards) == chosen, OBS_DEV, counts)
    return counts.reshape(N_LAT, N_LON).astype(jnp.int32)


def with_ends(result, stream_key, smallest, top_value):
    index_at = [jax.random.randint(jax.random.fold_in(stream_key, axis), (), 0, length) for axis, length in enumerate(result.shape)]
    widest = result.shape.index(max(result.shape))
    beside = index_at[:widest] + [(index_at[widest] + 1) % result.shape[widest]] + index_at[widest + 1:]
    return result.at[tuple(index_at)].set(smallest).at[tuple(beside)].set(top_value)


def steps_of(own_key, shape, cuts, low, top_value):
    gain, own = 1.0, jax.random.fold_in(own_key, 6)
    for axis_at, shards_of in cuts:
        steps = jnp.exp(jax.random.uniform(jax.random.fold_in(own, axis_at), (shards_of,), jnp.float32, low / len(cuts), top_value / len(cuts)))
        gain = gain * jnp.repeat(steps, shape[axis_at] // shards_of).reshape([-1 if axis == axis_at else 1 for axis in range(len(shape))])
    return gain


def centred(key, shape, width, reach, cuts=(), kind=jnp.bfloat16):
    entries = jax.random.normal(key, shape, jnp.float32) * width
    if len(cuts) > 0:
        entries = steps_of(key, shape, cuts, -0.22, 0.18) * entries
    return jnp.clip(entries, min=-reach, max=reach).astype(kind)


def setup_inputs(seed: int = 0) -> dict:
    seeds = jax.random.split(jax.random.key(seed), 9)
    sample_quantities = centred(seeds[0], (MEMBERS, EVOLVED_QUANTITY, NLAT, NLON), 1.0, 6.0, ((0, 2), (2, 4), (3, 4)))
    conv_weight = centred(seeds[1], (9 * EVOLVED_QUANTITY, HID), (9 * EVOLVED_QUANTITY) ** -0.5, 0.4375)
    conv_bias = centred(seeds[2], (HID,), 0.5, 3.0, (), jnp.float32)
    out_weight = centred(seeds[3], (HID, EVOLVED_QUANTITY), HID ** -0.5, 0.375)
    obs_index = with_ends(jax.random.randint(seeds[4], (N_LAT, N_LON, OBS_DEV), 0, EVOLVED_QUANTITY * PARALLEL_LINES * MERIDIAN_LINES), jax.random.fold_in(seeds[4], 1), 0, (EVOLVED_QUANTITY * PARALLEL_LINES * MERIDIAN_LINES) - 1).astype(jnp.int32)
    obs_count = draw_obs_count(jax.random.fold_in(seeds[8], 71), 0)
    obs_value = centred(seeds[6], (N_LAT, N_LON, OBS_DEV), 1.5, 8.0, ((0, 4), (1, 4)), jnp.float32)
    obs_weight = jnp.clip(jnp.exp(math.log(0.03) - 2.70805 * jax.random.uniform(seeds[7], (N_LAT, N_LON, OBS_DEV), jnp.float32) ** steps_of(seeds[7], (N_LAT, N_LON, OBS_DEV), ((0, 4), (1, 4)), -0.2, 0.2)), 0.002, 0.03)
    return dict(sample_quantities=sample_quantities, conv_weight=conv_weight, conv_bias=conv_bias, out_weight=out_weight, obs_index=obs_index, obs_count=obs_count, obs_value=obs_value, obs_weight=obs_weight)


def substep(padded, conv_weight, conv_bias, out_weight):
    nvar = padded.shape[0]
    rows = padded.shape[1] - 2
    cols = padded.shape[2] - 2
    patches = jnp.concatenate([padded[:, a:a + rows, b:b + cols] for a in range(3) for b in range(3)], axis=0)
    patches = patches.reshape(9 * nvar, rows * cols)
    pre = lax.dot_general(conv_weight, patches, (((0,), (0,)), ((), ())), preferred_element_type=jnp.float32)
    hidden = jax.nn.gelu(pre + conv_bias[:, None]).astype(jnp.bfloat16)
    change = lax.dot_general(out_weight, hidden, (((0,), (0,)), ((), ())), preferred_element_type=jnp.float32)
    centre = padded[:, 1:-1, 1:-1].astype(jnp.float32)
    return (centre + change.reshape(nvar, rows, cols)).astype(jnp.bfloat16)

def blend_weights(gram, proj):
    entries_number = gram.shape[0]
    eye = jnp.eye(entries_number, dtype=gram.dtype)
    system = (entries_number - 1) * eye + gram
    scale = jnp.sqrt(jnp.sum(system * system))
    current = system / scale
    inverse = eye
    for turn in range(NS_ITERS):
        factor = 1.5 * eye - 0.5 * jnp.dot(inverse, current, precision=lax.Precision.HIGHEST)
        current = jnp.dot(current, factor, precision=lax.Precision.HIGHEST)
        inverse = jnp.dot(factor, inverse, precision=lax.Precision.HIGHEST)
    root_inv = inverse / jnp.sqrt(scale)
    half = jnp.dot(root_inv, proj, precision=lax.Precision.HIGHEST)
    mean_w = jnp.dot(root_inv, half, precision=lax.Precision.HIGHEST)
    full = mean_w[:, None] + math.sqrt(entries_number - 1.0) * root_inv
    return 1.0 / entries_number + full - lax.optimization_barrier(jnp.mean(full, axis=0, keepdims=True))

def reference(sample_quantities, conv_weight, conv_bias, out_weight, obs_index, obs_count, obs_value, obs_weight):

    def predicted_sample(gridded_quantity):
        for sub in range(2):
            padded = jnp.pad(gridded_quantity, ((0, 0), (1, 1), (0, 0)))
            padded = jnp.concatenate([padded[:, :, -1:], padded, padded[:, :, :1]], axis=2)
            gridded_quantity = substep(padded, conv_weight, conv_bias, out_weight)
        return gridded_quantity
    predicted_population = lax.map(predicted_sample, sample_quantities)
    entries_number = predicted_population.shape[0]
    tile_sequence = predicted_population.reshape(entries_number, EVOLVED_QUANTITY, N_LAT, PARALLEL_LINES, N_LON, MERIDIAN_LINES).transpose(0, 2, 4, 1, 3, 5)
    tile_sequence = tile_sequence.reshape(entries_number, N_LAT, N_LON, EVOLVED_QUANTITY * PARALLEL_LINES * MERIDIAN_LINES)
    where = jnp.broadcast_to(obs_index[None], (entries_number,) + obs_index.shape).astype(jnp.int32)
    values = jnp.take_along_axis(tile_sequence, where, axis=3).astype(jnp.float32)
    live = (jnp.arange(OBS_DEV, dtype=jnp.int32)[None, None, :] < obs_count[:, :, None]).astype(jnp.float32)
    weight = obs_weight * live
    mean = lax.optimization_barrier(jnp.mean(values, axis=0))
    spread = values - mean
    innov = obs_value - mean
    gram = jnp.einsum('kijo,mijo->km', spread * weight, spread, precision=lax.Precision.HIGHEST)
    proj = jnp.einsum('kijo,ijo->k', spread * weight, innov, precision=lax.Precision.HIGHEST)
    transform_weights_square = blend_weights(gram, proj)
    updated_estimates = jnp.einsum('up,urif->prif', transform_weights_square, predicted_population.astype(jnp.float32), precision=lax.Precision.HIGHEST)
    return updated_estimates.astype(jnp.bfloat16)
```

```python
import functools
import math

import jax
import jax.numpy as jnp
from jax import lax
from jax.experimental import pallas as pl
from jax.experimental.pallas import tpu as pltpu
from jax.sharding import PartitionSpec as P

NS_ITERS = 20
GELU_A = math.sqrt(2.0 / math.pi)
GELU_B = GELU_A * 0.044715
F32 = jnp.float32
BF16 = jnp.bfloat16
PAD = 8


def lanes_of(shape):
    return lax.broadcasted_iota(jnp.int32, shape, len(shape) - 1)


def rows_kernel(top_ref, bottom_ref, up_ref, down_ref, stage):
    nvar, tile, cols = top_ref.shape
    for ref, out, first in ((top_ref, up_ref, 0), (bottom_ref, down_ref, tile - 2)):
        stage[...] = ref[...].reshape(nvar * tile, cols).astype(F32)
        both = [stage[pl.ds(first + i, nvar, stride=tile), :] for i in range(2)]
        out[...] = jnp.concatenate(both, axis=0).astype(BF16)


def edge_rows(x):
    nvar, rows, cols = x.shape
    tile = 16
    last = rows // tile - 1
    out = jax.ShapeDtypeStruct((2 * nvar, cols), BF16)
    return pl.pallas_call(
        rows_kernel,
        out_shape=(out, out),
        grid=(1,),
        in_specs=[
            pl.BlockSpec((nvar, tile, cols), lambda i: (0, 0, 0)),
            pl.BlockSpec((nvar, tile, cols), lambda i: (0, last, 0)),
        ],
        out_specs=[pl.BlockSpec((2 * nvar, cols), lambda i: (0, 0))] * 2,
        scratch_shapes=[pltpu.VMEM((nvar * tile, cols), F32)],
        name="edge_rows",
    )(x, x)


def columns_kernel(x_ref, north_ref, south_ref, left_ref, right_ref, stage):
    nvar, rows, cols = x_ref.shape
    wanted = (0, 1, cols - 2, cols - 1)
    k = lax.broadcasted_iota(jnp.int32, (8, cols), 0)
    lane = lanes_of((8, cols))
    pick = jnp.zeros((8, cols), F32)
    for i, c in enumerate(wanted):
        pick = jnp.where((k == i) & (lane == c), 1.0, pick)
    pick = pick.astype(BF16)
    per = cols // rows
    flat = x_ref[...].reshape(nvar * rows, cols)
    taken = lax.dot_general(pick, flat, (((1,), (1,)), ((), ())), preferred_element_type=F32)
    for v in range(nvar):
        block = taken[:, (v // per) * cols : (v // per + 1) * cols]
        shift = (2 - (v % per) * rows) % cols
        stage[8 * v : 8 * v + 8, :] = pltpu.roll(block, shift, 1)
    lane = lanes_of((nvar, cols))
    halo = []
    for ref, first in ((north_ref, 0), (south_ref, rows + 2)):
        for i in range(2):
            halo.append((first + i, ref[i * nvar : (i + 1) * nvar, :].astype(F32)))
    outs = []
    for i, c in enumerate(wanted):
        column = stage[pl.ds(i, nvar, stride=8), :]
        column = jnp.where(lane < rows + 2, column, 0.0)
        for at, row in halo:
            column = jnp.where(lane == at, pltpu.roll(row, (at - c) % cols, 1), column)
        outs.append(column)
    left_ref[...] = jnp.concatenate(outs[:2], axis=0).astype(BF16)
    right_ref[...] = jnp.concatenate(outs[2:], axis=0).astype(BF16)


def edge_columns(x, north, south):
    nvar, rows, cols = x.shape
    out = jax.ShapeDtypeStruct((2 * nvar, cols), BF16)
    return pl.pallas_call(
        columns_kernel,
        out_shape=(out, out),
        scratch_shapes=[pltpu.VMEM((8 * nvar, cols), F32)],
        name="edge_columns",
    )(x, north, south)


def gelu2(pre):
    inner = pre * (GELU_A + GELU_B * (pre * pre))
    return pre + pre * jnp.tanh(inner)


def forecast_kernel(
    spot_ref,
    north_in_ref,
    inside_ref,
    x_ref,
    north_ref,
    south_ref,
    own_left_ref,
    own_right_ref,
    from_left_ref,
    from_right_ref,
    conv_ref,
    out_w_ref,
    lane_ref,
    forecast_ref,
    picked_ref,
    xf,
    first,
    second,
    final,
    seen,
):
    nvar, rows, cols = x_ref.shape
    block = 3 * nvar + PAD
    deep = 3 * block
    lane = lanes_of((nvar, cols))
    ones = jnp.ones((PAD, cols), F32)

    def tap_rows(row, west, east, at):
        left = jnp.where(lane == 0, pltpu.roll(west, (cols - at) % cols, 1), pltpu.roll(row, 1, 1))
        right = jnp.where(
            lane == cols - 1, pltpu.roll(east, (2 * cols - 1 - at) % cols, 1), pltpu.roll(row, cols - 1, 1)
        )
        return jnp.concatenate([row, left, right, ones], axis=0).astype(BF16)

    def advance(patches, centre):
        pre = jnp.dot(conv_ref[...], patches, preferred_element_type=F32)
        hidden = gelu2(pre).astype(BF16)
        change = jnp.dot(out_w_ref[...], hidden, preferred_element_type=F32)
        return (centre + change[:nvar]).astype(BF16).astype(F32)

    xf[...] = x_ref[...].reshape(nvar * rows, cols).astype(F32)
    from_left = from_left_ref[...].astype(F32)
    from_right = from_right_ref[...].astype(F32)
    own_left = own_left_ref[...].astype(F32)
    own_right = own_right_ref[...].astype(F32)
    far_west, west = from_left[:nvar], from_left[nvar:]
    east, far_east = from_right[:nvar], from_right[nvar:]
    inner_west, inner_east = own_left[:nvar], own_right[nvar:]

    for ref, start in ((north_ref, 0), (south_ref, rows + 2)):
        for i in range(2):
            row = ref[i * nvar : (i + 1) * nvar, :].astype(F32)
            first[(start + i) * block : (start + i + 1) * block, :] = tap_rows(row, west, east, start + i)

    def fill(r, carry):
        row = xf[pl.ds(r, nvar, stride=rows), :]
        at = pl.multiple_of((r + 2) * block, 16)
        first[pl.ds(at, block), :] = tap_rows(row, west, east, r + 2)
        return carry

    lax.fori_loop(0, rows, fill, 0, unroll=4)

    sides = []
    for mid, low, high in ((west, far_west, inner_west), (east, inner_east, far_east)):
        stack = []
        for a in range(3):
            for entry in (mid, low, high):
                stack.append(pltpu.roll(entry, (1 - a) % cols, 1) if a != 1 else entry)
            stack.append(ones)
        sides.append(jnp.concatenate(stack, axis=0).astype(BF16))
    patches = jnp.concatenate(sides, axis=1)
    beside = advance(patches, jnp.concatenate([west, east], axis=1))
    keep = jnp.where(lane == 1, north_in_ref[0], jnp.where(lane == rows + 2, north_in_ref[1], 1)) > 0
    mid_west = jnp.where(keep, beside[:, :cols], 0.0)
    mid_east = jnp.where(keep, beside[:, cols:], 0.0)

    def pair(source, at):
        at = pl.multiple_of(at * block, 16)
        patches = jnp.concatenate(
            [source[pl.ds(at, deep), :], source[pl.ds(at + block, deep), :]], axis=1
        )
        centre = jnp.concatenate(
            [source[pl.ds(at + block, nvar), :], source[pl.ds(at + 2 * block, nvar), :]], axis=1
        ).astype(F32)
        return advance(patches, centre)

    def first_step(i, carry):
        both = pair(first, 2 * i)
        for half in range(2):
            m = 2 * i + half
            good = (jnp.where(m == 0, north_in_ref[0], 1) * jnp.where(m == rows + 1, north_in_ref[1], 1)) > 0
            row = both[:, half * cols : (half + 1) * cols]
            row = jnp.where(good, row, 0.0)
            at = pl.multiple_of(m * block, 16)
            second[pl.ds(at, block), :] = tap_rows(row, mid_west, mid_east, m + 1)
        return carry

    lax.fori_loop(0, rows // 2 + 1, first_step, 0, unroll=3)

    def second_step(j, carry):
        both = pair(second, 2 * j)
        both = jnp.concatenate([both[:, :cols], both[:, cols:]], axis=0)
        at = pl.multiple_of(j * 2 * nvar, 16)
        final[pl.ds(at, 2 * nvar), :] = both
        forecast_ref[pl.ds(at, 2 * nvar), :] = both.astype(BF16)
        return carry

    lax.fori_loop(0, rows // 2, second_step, 0, unroll=4)

    def look(o, carry):
        seen[pl.ds(o, 1), :] = final[pl.ds(spot_ref[o], 1), :]
        return carry

    slots = seen.shape[0]
    lax.fori_loop(0, slots, look, 0, unroll=8)
    masked = jnp.where(lane_ref[...] == lanes_of((slots, cols)), seen[...], 0.0).astype(BF16)
    values = lax.dot_general(
        jnp.ones((8, cols), BF16), masked, (((1,), (1,)), ((), ())), preferred_element_type=F32
    )
    picked_ref[...] = values
    del inside_ref


def run_forecast(spot, inside, x, north, south, own_left, own_right, from_left, from_right, conv, out_w, lane):
    nvar, rows, cols = x.shape
    slots = spot.shape[0]
    block = 3 * nvar + PAD
    smem = pl.BlockSpec(memory_space=pltpu.SMEM)
    vmem = pl.BlockSpec(memory_space=pltpu.VMEM)
    return pl.pallas_call(
        forecast_kernel,
        out_shape=(
            jax.ShapeDtypeStruct((rows * nvar, cols), BF16),
            jax.ShapeDtypeStruct((8, slots), F32),
        ),
        in_specs=[smem, smem, smem] + [vmem] * 10,
        out_specs=(vmem, vmem),
        scratch_shapes=[
            pltpu.VMEM((nvar * rows, cols), F32),
            pltpu.VMEM(((rows + 4) * block, cols), BF16),
            pltpu.VMEM(((rows + 2) * block, cols), BF16),
            pltpu.VMEM((rows * nvar, cols), F32),
            pltpu.VMEM((slots, cols), F32),
        ],
        name="forecast",
    )(spot, inside, inside, x, north, south, own_left, own_right, from_left, from_right, conv, out_w, lane)


def pair_weights(gram, proj):
    count = len(proj)
    system = [[gram[k][m] + (float(count - 1) if k == m else 0.0) for m in range(count)] for k in range(count)]
    total = sum(entry * entry for line in system for entry in line)
    scale = jnp.sqrt(total)
    one = jnp.ones_like(scale)
    eye = [[one if k == m else 0.0 * one for m in range(count)] for k in range(count)]

    def times(left, right):
        return [
            [sum(left[k][j] * right[j][m] for j in range(count)) for m in range(count)] for k in range(count)
        ]

    current = [[entry / scale for entry in line] for line in system]
    inverse = eye
    for turn in range(NS_ITERS):
        both = times(inverse, current)
        factor = [[1.5 * eye[k][m] - 0.5 * both[k][m] for m in range(count)] for k in range(count)]
        current = times(current, factor)
        inverse = times(factor, inverse)
    root = jnp.sqrt(scale)
    root_inv = [[entry / root for entry in line] for line in inverse]
    half = [sum(root_inv[k][j] * proj[j] for j in range(count)) for k in range(count)]
    mean_w = [sum(root_inv[k][j] * half[j] for j in range(count)) for k in range(count)]
    span = math.sqrt(count - 1.0)
    full = [[mean_w[k] + span * root_inv[k][m] for m in range(count)] for k in range(count)]
    centre = [sum(full[k][m] for k in range(count)) / count for m in range(count)]
    return [[1.0 / count + full[k][m] - centre[m] for m in range(count)] for k in range(count)]


def analysis_kernel(me_ref, told_ref, mine_ref, other_ref, out_ref, blended):
    count, shards = told_ref.shape[0], told_ref.shape[1]
    nvar, rows, cols = out_ref.shape
    pairs = [(k, m) for k in range(count) for m in range(k, count)]
    sums = {key: 0.0 for key in pairs}
    for k in range(count):
        sums[k] = 0.0
    for s in range(shards):
        hx = [told_ref[k, s, 0:2, :] for k in range(count)]
        value = told_ref[0, s, 2:4, :]
        weight = told_ref[0, s, 4:6, :]
        mean = sum(hx) / count
        spread = [h - mean for h in hx]
        innov = value - mean
        for k in range(count):
            scaled = spread[k] * weight
            sums[k] = sums[k] + scaled * innov
            for m in range(k, count):
                sums[k, m] = sums[k, m] + scaled * spread[m]
    tile = (8, cols)
    whole = {key: jnp.broadcast_to(jnp.sum(term, keepdims=True), tile) for key, term in sums.items()}
    gram = [[whole[min(k, m), max(k, m)] for m in range(count)] for k in range(count)]
    weights = pair_weights(gram, [whole[k] for k in range(count)])
    me = me_ref[0]
    mine = jnp.where(me == 0, weights[0][0], weights[1][1])[0:1, :]
    other = jnp.where(me == 0, weights[1][0], weights[0][1])[0:1, :]
    blended[...] = mine * mine_ref[...].astype(F32) + other * other_ref[...].astype(F32)
    for v in range(nvar):
        for r in range(0, rows, 16):
            halves = [
                blended[pl.ds((r + 8 * i) * nvar + v, 8, stride=nvar), :] for i in range(2)
            ]
            out_ref[v, r : r + 16, :] = jnp.concatenate(halves, axis=0).astype(BF16)


def run_analysis(me, told, mine, other, shape):
    nvar, rows, cols = shape
    vmem = pl.BlockSpec(memory_space=pltpu.VMEM)
    return pl.pallas_call(
        analysis_kernel,
        out_shape=jax.ShapeDtypeStruct(shape, BF16),
        in_specs=[pl.BlockSpec(memory_space=pltpu.SMEM), vmem, vmem, vmem],
        out_specs=vmem,
        scratch_shapes=[pltpu.VMEM((nvar * rows, cols), F32)],
        name="analysis",
    )(me, told, mine, other)


def blend_weights(gram, proj):
    entries_number = gram.shape[0]
    eye = jnp.eye(entries_number, dtype=gram.dtype)
    system = (entries_number - 1) * eye + gram
    scale = jnp.sqrt(jnp.sum(system * system))
    current = system / scale
    inverse = eye
    for turn in range(NS_ITERS):
        factor = 1.5 * eye - 0.5 * jnp.dot(inverse, current, precision=lax.Precision.HIGHEST)
        current = jnp.dot(current, factor, precision=lax.Precision.HIGHEST)
        inverse = jnp.dot(factor, inverse, precision=lax.Precision.HIGHEST)
    root_inv = inverse / jnp.sqrt(scale)
    half = jnp.dot(root_inv, proj, precision=lax.Precision.HIGHEST)
    mean_w = jnp.dot(root_inv, half, precision=lax.Precision.HIGHEST)
    full = mean_w[:, None] + math.sqrt(entries_number - 1.0) * root_inv
    return 1.0 / entries_number + full - jnp.mean(full, axis=0, keepdims=True)


def many_members(told, forecast, shape):
    nvar, rows, cols = shape
    members = told[:, :, 0:2, :].reshape(told.shape[0], -1)
    value = told[0, :, 2:4, :].reshape(-1)
    weight = told[0, :, 4:6, :].reshape(-1)
    mean = jnp.mean(members, axis=0)
    spread = members - mean[None, :]
    innov = value - mean
    weighted = spread * weight[None, :]
    gram = jnp.dot(weighted, spread.T, precision=lax.Precision.HIGHEST)
    proj = jnp.dot(weighted, innov, precision=lax.Precision.HIGHEST)
    transform = blend_weights(gram, proj)
    column = lax.dynamic_slice_in_dim(transform, lax.axis_index("ens"), 1, 1)[:, 0]
    everyone = lax.all_gather(forecast[None], "ens", axis=0, tiled=True)
    blended = jnp.tensordot(column, everyone.astype(F32), axes=1, precision=lax.Precision.HIGHEST)
    return blended.astype(BF16).reshape(rows, nvar, cols).transpose(1, 0, 2)


def packed_weights(conv_weight, conv_bias, out_weight, nvar):
    hid = conv_bias.shape[0]
    taps = conv_weight.reshape(3, 3, nvar, hid)
    taps = jnp.stack([taps[:, 1], taps[:, 0], taps[:, 2]], axis=1).reshape(3, 3 * nvar, hid)
    high = conv_bias.astype(BF16)
    rest = conv_bias - high.astype(F32)
    middle = rest.astype(BF16)
    low = (rest - middle.astype(F32)).astype(BF16)
    bias = jnp.zeros((3, PAD, hid), BF16)
    bias = bias.at[1, 0].set(high).at[1, 1].set(middle).at[1, 2].set(low)
    conv = jnp.concatenate([taps, bias], axis=1).reshape(-1, hid).T
    half = (out_weight.astype(F32) * 0.5).astype(BF16).T
    return conv, half


def per_device(
    sample_quantities,
    conv_weight,
    conv_bias,
    out_weight,
    obs_index,
    obs_count,
    obs_value,
    obs_weight,
):
    x = sample_quantities[0]
    nvar, rows, cols = x.shape
    n_ens, n_lat, n_lon = (lax.axis_size(axis) for axis in ("ens", "lat", "lon"))
    down_lat = [(i, i + 1) for i in range(n_lat - 1)]
    up_lat = [(j, i) for i, j in down_lat]
    right_lon = [(i, (i + 1) % n_lon) for i in range(n_lon)]
    left_lon = [(j, i) for i, j in right_lon]

    first_rows, last_rows = edge_rows(x)
    north = lax.ppermute(last_rows, "lat", down_lat)
    south = lax.ppermute(first_rows, "lat", up_lat)
    own_left, own_right = edge_columns(x, north, south)
    from_left = lax.ppermute(own_right, "lon", right_lon)
    from_right = lax.ppermute(own_left, "lon", left_lon)

    conv, out_w = packed_weights(conv_weight, conv_bias, out_weight, nvar)
    slots = obs_index.reshape(-1)
    var, row, lane = slots // (rows * cols), slots // cols % rows, slots % cols
    spot = jnp.clip(row * nvar + var, 0, rows * nvar - 1)
    here = lax.axis_index("lat")
    inside = jnp.stack([here > 0, here < n_lat - 1]).astype(jnp.int32)
    forecast, picked = run_forecast(
        spot,
        inside,
        x,
        north,
        south,
        own_left,
        own_right,
        from_left,
        from_right,
        conv,
        out_w,
        lane[:, None],
    )

    count = slots.shape[0]
    live = (jnp.arange(count, dtype=jnp.int32) < obs_count.reshape(())).astype(F32)
    weight = obs_weight.reshape(-1) * live
    fold = (count // cols, cols)
    note = jnp.concatenate(
        [picked[0].reshape(fold), obs_value.reshape(fold), weight.reshape(fold), jnp.zeros(fold, F32)], axis=0
    )
    devices = n_ens * n_lat * n_lon
    notes = jnp.broadcast_to(note[None], (devices,) + note.shape)
    told = lax.all_to_all(notes, ("ens", "lat", "lon"), 0, 0, tiled=True)
    told = told.reshape(n_ens, n_lat * n_lon, *note.shape)
    if n_ens == 2:
        other = lax.ppermute(forecast, "ens", [(0, 1), (1, 0)])
        me = lax.axis_index("ens").reshape(1)
        return run_analysis(me, told, forecast, other, x.shape)[None]
    return many_members(told, forecast, x.shape)[None]


def solution(mesh):
    return jax.shard_map(
        per_device,
        mesh=mesh,
        in_specs=(
            P("ens", None, "lat", "lon"),
            P(),
            P(),
            P(),
            P("lat", "lon", None),
            P("lat", "lon"),
            P("lat", "lon", None),
            P("lat", "lon", None),
        ),
        out_specs=P("ens", None, "lat", "lon"),
        check_vma=False,
    )
```

```python
import functools
import math

import jax
import jax.numpy as jnp
from jax import lax
from jax.experimental import pallas as pl
from jax.experimental.pallas import tpu as pltpu
from jax.sharding import PartitionSpec as P

NS_ITERS = 20
GELU_A = math.sqrt(2.0 / math.pi)
GELU_B = GELU_A * 0.044715
F32 = jnp.float32
BF16 = jnp.bfloat16
PAD = 8
SMALL = 4 << 20


def lanes_of(shape):
    return lax.broadcasted_iota(jnp.int32, shape, len(shape) - 1)


def rows_kernel(top_ref, bottom_ref, up_ref, down_ref, stage):
    nvar, tile, cols = top_ref.shape
    for ref, out, first in ((top_ref, up_ref, 0), (bottom_ref, down_ref, tile - 2)):
        stage[...] = ref[...].reshape(nvar * tile, cols).astype(F32)
        both = [stage[pl.ds(first + i, nvar, stride=tile), :] for i in range(2)]
        out[...] = jnp.concatenate(both, axis=0).astype(BF16)


def edge_rows(x):
    nvar, rows, cols = x.shape
    tile = 16
    last = rows // tile - 1
    out = jax.ShapeDtypeStruct((2 * nvar, cols), BF16)
    return pl.pallas_call(
        rows_kernel,
        out_shape=(out, out),
        grid=(1,),
        in_specs=[
            pl.BlockSpec((nvar, tile, cols), lambda i: (0, 0, 0)),
            pl.BlockSpec((nvar, tile, cols), lambda i: (0, last, 0)),
        ],
        out_specs=[pl.BlockSpec((2 * nvar, cols), lambda i: (0, 0))] * 2,
        scratch_shapes=[pltpu.VMEM((nvar * tile, cols), F32)],
        compiler_params=pltpu.CompilerParams(vmem_limit_bytes=SMALL),
        name="edge_rows",
    )(x, x)


def spread_kernel(x_ref, taps_ref, own_ref, stage, xf):
    nvar, rows, cols = x_ref.shape
    block = 3 * nvar + PAD
    wanted = (0, 1, cols - 2, cols - 1)
    k = lax.broadcasted_iota(jnp.int32, (8, cols), 0)
    lane = lanes_of((8, cols))
    pick = jnp.zeros((8, cols), F32)
    for i, c in enumerate(wanted):
        pick = jnp.where((k == i) & (lane == c), 1.0, pick)
    pick = pick.astype(BF16)
    per = cols // rows
    flat = x_ref[...].reshape(nvar * rows, cols)
    xf[...] = flat.astype(F32)
    taken = lax.dot_general(pick, flat, (((1,), (1,)), ((), ())), preferred_element_type=F32)
    for v in range(nvar):
        part = taken[:, (v // per) * cols : (v // per + 1) * cols]
        shift = (2 - (v % per) * rows) % cols
        stage[8 * v : 8 * v + 8, :] = pltpu.roll(part, shift, 1)
    for i in range(len(wanted)):
        own_ref[i * nvar : (i + 1) * nvar, :] = stage[pl.ds(i, nvar, stride=8), :]
    ones = jnp.ones((PAD, cols), F32)

    def fill(r, carry):
        row = xf[pl.ds(r, nvar, stride=rows), :]
        tap = jnp.concatenate([row, pltpu.roll(row, 1, 1), pltpu.roll(row, cols - 1, 1), ones], axis=0)
        at = pl.multiple_of(r * block, 16)
        taps_ref[pl.ds(at, block), :] = tap.astype(BF16)
        return carry

    lax.fori_loop(0, rows, fill, 0, unroll=4)


def spread(x):
    nvar, rows, cols = x.shape
    block = 3 * nvar + PAD
    return pl.pallas_call(
        spread_kernel,
        out_shape=(
            jax.ShapeDtypeStruct((rows * block, cols), BF16),
            jax.ShapeDtypeStruct((4 * nvar, cols), F32),
        ),
        scratch_shapes=[pltpu.VMEM((8 * nvar, cols), F32), pltpu.VMEM((nvar * rows, cols), F32)],
        compiler_params=pltpu.CompilerParams(vmem_limit_bytes=SMALL),
        cost_estimate=pl.CostEstimate(flops=10**8, bytes_accessed=4 * 10**6, transcendentals=0),
        name="spread",
    )(x)


def edge_columns(own, north, south, rows):
    nvar, cols = own.shape[0] // 4, own.shape[1]
    wanted = (0, 1, cols - 2, cols - 1)

    def kernel(own_ref, north_ref, south_ref, left_ref, right_ref):
        lane = lanes_of((nvar, cols))
        halo = []
        for ref, first in ((north_ref, 0), (south_ref, rows + 2)):
            for i in range(2):
                halo.append((first + i, ref[i * nvar : (i + 1) * nvar, :].astype(F32)))
        outs = []
        for i, c in enumerate(wanted):
            column = own_ref[i * nvar : (i + 1) * nvar, :]
            column = jnp.where(lane < rows + 2, column, 0.0)
            for at, row in halo:
                column = jnp.where(lane == at, pltpu.roll(row, (at - c) % cols, 1), column)
            outs.append(column)
        left_ref[...] = jnp.concatenate(outs[:2], axis=0).astype(BF16)
        right_ref[...] = jnp.concatenate(outs[2:], axis=0).astype(BF16)

    out = jax.ShapeDtypeStruct((2 * nvar, cols), BF16)
    return pl.pallas_call(
        kernel,
        out_shape=(out, out),
        compiler_params=pltpu.CompilerParams(vmem_limit_bytes=SMALL),
        name="edge_columns",
    )(own, north, south)


def gelu2(pre):
    pre = pre.astype(BF16)
    inner = pre * (jnp.asarray(GELU_A, BF16) + jnp.asarray(GELU_B, BF16) * (pre * pre))
    return pre + pre * jnp.tanh(inner)


def forecast_kernel(
    spot_ref,
    north_in_ref,
    count_ref,
    taps_ref,
    north_ref,
    south_ref,
    own_left_ref,
    own_right_ref,
    from_left_ref,
    from_right_ref,
    conv_ref,
    out_w_ref,
    lane_ref,
    value_ref,
    weight_ref,
    forecast_ref,
    notes_ref,
    first,
    second,
    final,
    seen,
):
    nvar, cols = north_ref.shape[0] // 2, north_ref.shape[1]
    block = 3 * nvar + PAD
    rows = taps_ref.shape[0] // block
    deep = 3 * block
    lane = lanes_of((nvar, cols))
    ones = jnp.ones((PAD, cols), F32)

    def tap_rows(row, west, east, at):
        left = jnp.where(lane == 0, pltpu.roll(west, (cols - at) % cols, 1), pltpu.roll(row, 1, 1))
        right = jnp.where(
            lane == cols - 1, pltpu.roll(east, (2 * cols - 1 - at) % cols, 1), pltpu.roll(row, cols - 1, 1)
        )
        return jnp.concatenate([row, left, right, ones], axis=0).astype(BF16)

    def advance(patches, centre):
        pre = jnp.dot(conv_ref[...], patches, preferred_element_type=F32)
        hidden = gelu2(pre)
        change = jnp.dot(out_w_ref[...], hidden, preferred_element_type=F32)
        return (centre + change[:nvar]).astype(BF16).astype(F32)

    from_left = from_left_ref[...].astype(F32)
    from_right = from_right_ref[...].astype(F32)
    own_left = own_left_ref[...].astype(F32)
    own_right = own_right_ref[...].astype(F32)
    far_west, west = from_left[:nvar], from_left[nvar:]
    east, far_east = from_right[:nvar], from_right[nvar:]
    inner_west, inner_east = own_left[:nvar], own_right[nvar:]

    for ref, start in ((north_ref, 0), (south_ref, rows + 2)):
        for i in range(2):
            row = ref[i * nvar : (i + 1) * nvar, :].astype(F32)
            first[(start + i) * block : (start + i + 1) * block, :] = tap_rows(row, west, east, start + i)

    group = lax.broadcasted_iota(jnp.int32, (block, cols), 0)
    wide = lanes_of((block, cols))
    is_left = (group >= nvar) & (group < 2 * nvar) & (wide == 0)
    is_right = (group >= 2 * nvar) & (group < 3 * nvar) & (wide == cols - 1)
    fix = jnp.where(is_left | is_right, 1.0, 0.0).astype(BF16) > 0
    nothing = jnp.zeros((nvar, cols), F32)
    source = jnp.concatenate([nothing, west, pltpu.roll(east, cols - 1, 1), jnp.zeros((PAD, cols), F32)], axis=0)
    source = source.astype(BF16)

    def fill(r, carry):
        at = pl.multiple_of(r * block, 16)
        mine = pltpu.roll(source, cols - 2 - r, 1)
        to = pl.multiple_of((r + 2) * block, 16)
        first[pl.ds(to, block), :] = jnp.where(fix, mine, taps_ref[pl.ds(at, block), :])
        return carry

    lax.fori_loop(0, rows, fill, 0, unroll=4)

    sides = []
    for mid, low, high in ((west, far_west, inner_west), (east, inner_east, far_east)):
        stack = []
        for a in range(3):
            for entry in (mid, low, high):
                stack.append(pltpu.roll(entry, (1 - a) % cols, 1) if a != 1 else entry)
            stack.append(ones)
        sides.append(jnp.concatenate(stack, axis=0).astype(BF16))
    patches = jnp.concatenate(sides, axis=1)
    beside = advance(patches, jnp.concatenate([west, east], axis=1))
    keep = jnp.where(lane == 1, north_in_ref[0], jnp.where(lane == rows + 2, north_in_ref[1], 1)) > 0
    mid_west = jnp.where(keep, beside[:, :cols], 0.0)
    mid_east = jnp.where(keep, beside[:, cols:], 0.0)

    def pair(source, at):
        at = pl.multiple_of(at * block, 16)
        patches = jnp.concatenate(
            [source[pl.ds(at, deep), :], source[pl.ds(at + block, deep), :]], axis=1
        )
        centre = jnp.concatenate(
            [source[pl.ds(at + block, nvar), :], source[pl.ds(at + 2 * block, nvar), :]], axis=1
        ).astype(F32)
        return advance(patches, centre)

    def first_step(i, carry):
        both = pair(first, 2 * i)
        for half in range(2):
            m = 2 * i + half
            good = (jnp.where(m == 0, north_in_ref[0], 1) * jnp.where(m == rows + 1, north_in_ref[1], 1)) > 0
            row = both[:, half * cols : (half + 1) * cols]
            row = jnp.where(good, row, 0.0)
            at = pl.multiple_of(m * block, 16)
            second[pl.ds(at, block), :] = tap_rows(row, mid_west, mid_east, m + 1)
        return carry

    lax.fori_loop(0, rows // 2 + 1, first_step, 0, unroll=11)

    def second_step(j, carry):
        both = pair(second, 2 * j)
        both = jnp.concatenate([both[:, :cols], both[:, cols:]], axis=0)
        at = pl.multiple_of(j * 2 * nvar, 16)
        final[pl.ds(at, 2 * nvar), :] = both
        forecast_ref[pl.ds(at, 2 * nvar), :] = both.astype(BF16)
        return carry

    lax.fori_loop(0, rows // 2, second_step, 0, unroll=8)

    def look(o, carry):
        seen[pl.ds(o, 1), :] = final[pl.ds(spot_ref[o], 1), :]
        return carry

    slots = seen.shape[0]
    lax.fori_loop(0, slots, look, 0, unroll=16)
    masked = jnp.where(lane_ref[...] == lanes_of((slots, cols)), seen[...], 0.0).astype(BF16)
    values = lax.dot_general(
        jnp.ones((8, cols), BF16), masked, (((1,), (1,)), ((), ())), preferred_element_type=F32
    )
    fold = value_ref.shape[0]
    live = lanes_of((fold, cols)) + cols * lax.broadcasted_iota(jnp.int32, (fold, cols), 0) < count_ref[0]
    note = [values[0:1, i * cols : (i + 1) * cols] for i in range(fold)]
    note += [value_ref[...], jnp.where(live, weight_ref[...], 0.0)]
    note.append(jnp.zeros((notes_ref.shape[1] - 3 * fold, cols), F32))
    note = jnp.concatenate(note, axis=0)
    for d in range(notes_ref.shape[0]):
        notes_ref[d] = note


def run_forecast(spot, inside, count, taps, north, south, own_left, own_right, from_left, from_right, conv, out_w, lane, value, weight, devices):
    nvar, cols = north.shape[0] // 2, north.shape[1]
    slots = spot.shape[0]
    block = 3 * nvar + PAD
    rows = taps.shape[0] // block
    note_rows = -(-3 * value.shape[0] // 8) * 8
    smem = pl.BlockSpec(memory_space=pltpu.SMEM)
    vmem = pl.BlockSpec(memory_space=pltpu.VMEM)
    return pl.pallas_call(
        forecast_kernel,
        out_shape=(
            jax.ShapeDtypeStruct((rows * nvar, cols), BF16),
            jax.ShapeDtypeStruct((devices, note_rows, cols), F32),
        ),
        in_specs=[smem, smem, smem] + [vmem] * 12,
        out_specs=(vmem, vmem),
        scratch_shapes=[
            pltpu.VMEM(((rows + 4) * block, cols), BF16),
            pltpu.VMEM(((rows + 2) * block, cols), BF16),
            pltpu.VMEM((rows * nvar, cols), F32),
            pltpu.VMEM((slots, cols), F32),
        ],
        compiler_params=pltpu.CompilerParams(vmem_limit_bytes=16 << 20),
        name="forecast",
    )(spot, inside, count, taps, north, south, own_left, own_right, from_left, from_right, conv, out_w, lane, value, weight)


def pair_weights(gram, proj):
    count = len(proj)
    system = [[gram[k][m] + (float(count - 1) if k == m else 0.0) for m in range(count)] for k in range(count)]
    total = sum(entry * entry for line in system for entry in line)
    scale = jnp.sqrt(total)
    one = jnp.ones_like(scale)
    eye = [[one if k == m else 0.0 * one for m in range(count)] for k in range(count)]

    def times(left, right):
        return [
            [sum(left[k][j] * right[j][m] for j in range(count)) for m in range(count)] for k in range(count)
        ]

    current = [[entry / scale for entry in line] for line in system]
    inverse = eye
    for turn in range(NS_ITERS):
        both = times(inverse, current)
        factor = [[1.5 * eye[k][m] - 0.5 * both[k][m] for m in range(count)] for k in range(count)]
        current = times(current, factor)
        inverse = times(factor, inverse)
    root = jnp.sqrt(scale)
    root_inv = [[entry / root for entry in line] for line in inverse]
    half = [sum(root_inv[k][j] * proj[j] for j in range(count)) for k in range(count)]
    mean_w = [sum(root_inv[k][j] * half[j] for j in range(count)) for k in range(count)]
    span = math.sqrt(count - 1.0)
    full = [[mean_w[k] + span * root_inv[k][m] for m in range(count)] for k in range(count)]
    centre = [sum(full[k][m] for k in range(count)) / count for m in range(count)]
    return [[1.0 / count + full[k][m] - centre[m] for m in range(count)] for k in range(count)]


def analysis_kernel(me_ref, told_ref, mine_ref, other_ref, out_ref, blended):
    count, shards = told_ref.shape[0], told_ref.shape[1]
    nvar, rows, cols = out_ref.shape
    pairs = [(k, m) for k in range(count) for m in range(k, count)]
    sums = {key: 0.0 for key in pairs}
    for k in range(count):
        sums[k] = 0.0
    for s in range(shards):
        hx = [told_ref[k, s, 0:2, :] for k in range(count)]
        value = told_ref[0, s, 2:4, :]
        weight = told_ref[0, s, 4:6, :]
        mean = sum(hx) / count
        spread = [h - mean for h in hx]
        innov = value - mean
        for k in range(count):
            scaled = spread[k] * weight
            sums[k] = sums[k] + scaled * innov
            for m in range(k, count):
                sums[k, m] = sums[k, m] + scaled * spread[m]
    tile = (8, cols)
    whole = {key: jnp.broadcast_to(jnp.sum(term, keepdims=True), tile) for key, term in sums.items()}
    gram = [[whole[min(k, m), max(k, m)] for m in range(count)] for k in range(count)]
    weights = pair_weights(gram, [whole[k] for k in range(count)])
    me = me_ref[0]
    mine = jnp.where(me == 0, weights[0][0], weights[1][1])[0:1, :]
    other = jnp.where(me == 0, weights[1][0], weights[0][1])[0:1, :]
    blended[...] = mine * mine_ref[...].astype(F32) + other * other_ref[...].astype(F32)
    for v in range(nvar):
        for r in range(0, rows, 16):
            halves = [
                blended[pl.ds((r + 8 * i) * nvar + v, 8, stride=nvar), :] for i in range(2)
            ]
            out_ref[v, r : r + 16, :] = jnp.concatenate(halves, axis=0).astype(BF16)


def run_analysis(me, told, mine, other, shape):
    nvar, rows, cols = shape
    vmem = pl.BlockSpec(memory_space=pltpu.VMEM)
    return pl.pallas_call(
        analysis_kernel,
        out_shape=jax.ShapeDtypeStruct(shape, BF16),
        in_specs=[pl.BlockSpec(memory_space=pltpu.SMEM), vmem, vmem, vmem],
        out_specs=vmem,
        scratch_shapes=[pltpu.VMEM((nvar * rows, cols), F32)],
        compiler_params=pltpu.CompilerParams(vmem_limit_bytes=8 << 20),
        name="analysis",
    )(me, told, mine, other)


def blend_weights(gram, proj):
    entries_number = gram.shape[0]
    eye = jnp.eye(entries_number, dtype=gram.dtype)
    system = (entries_number - 1) * eye + gram
    scale = jnp.sqrt(jnp.sum(system * system))
    current = system / scale
    inverse = eye
    for turn in range(NS_ITERS):
        factor = 1.5 * eye - 0.5 * jnp.dot(inverse, current, precision=lax.Precision.HIGHEST)
        current = jnp.dot(current, factor, precision=lax.Precision.HIGHEST)
        inverse = jnp.dot(factor, inverse, precision=lax.Precision.HIGHEST)
    root_inv = inverse / jnp.sqrt(scale)
    half = jnp.dot(root_inv, proj, precision=lax.Precision.HIGHEST)
    mean_w = jnp.dot(root_inv, half, precision=lax.Precision.HIGHEST)
    full = mean_w[:, None] + math.sqrt(entries_number - 1.0) * root_inv
    return 1.0 / entries_number + full - jnp.mean(full, axis=0, keepdims=True)


def many_members(told, forecast, shape):
    nvar, rows, cols = shape
    members = told[:, :, 0:2, :].reshape(told.shape[0], -1)
    value = told[0, :, 2:4, :].reshape(-1)
    weight = told[0, :, 4:6, :].reshape(-1)
    mean = jnp.mean(members, axis=0)
    spread = members - mean[None, :]
    innov = value - mean
    weighted = spread * weight[None, :]
    gram = jnp.dot(weighted, spread.T, precision=lax.Precision.HIGHEST)
    proj = jnp.dot(weighted, innov, precision=lax.Precision.HIGHEST)
    transform = blend_weights(gram, proj)
    column = lax.dynamic_slice_in_dim(transform, lax.axis_index("ens"), 1, 1)[:, 0]
    everyone = lax.all_gather(forecast[None], "ens", axis=0, tiled=True)
    blended = jnp.tensordot(column, everyone.astype(F32), axes=1, precision=lax.Precision.HIGHEST)
    return blended.astype(BF16).reshape(rows, nvar, cols).transpose(1, 0, 2)


def packed_weights(conv_weight, conv_bias, out_weight, nvar):
    hid = conv_bias.shape[0]
    block = 3 * nvar + PAD

    def kernel(conv_ref, bias_ref, out_ref, packed_ref, half_ref):
        bias = bias_ref[...]
        high = bias.astype(BF16).astype(F32)
        middle = (bias - high).astype(BF16).astype(F32)
        low = (bias - high - middle).astype(BF16).astype(F32)
        rest = jnp.zeros((PAD - 3, hid), F32)
        pieces = []
        for a in range(3):
            for b in (1, 0, 2):
                at = (3 * a + b) * nvar
                pieces.append(conv_ref[at : at + nvar, :].astype(F32))
            if a == 1:
                pieces.append(jnp.concatenate([high, middle, low, rest], axis=0))
            else:
                pieces.append(jnp.zeros((PAD, hid), F32))
        packed_ref[...] = jnp.concatenate(pieces, axis=0).T.astype(BF16)
        half_ref[...] = (out_ref[...].astype(F32) * 0.5).astype(BF16)

    return pl.pallas_call(
        kernel,
        out_shape=(
            jax.ShapeDtypeStruct((hid, 3 * block), BF16),
            jax.ShapeDtypeStruct((nvar, hid), BF16),
        ),
        compiler_params=pltpu.CompilerParams(vmem_limit_bytes=SMALL),
        cost_estimate=pl.CostEstimate(flops=10**7, bytes_accessed=10**6, transcendentals=0),
        name="packed_weights",
    )(conv_weight, conv_bias[None], out_weight.T)


def per_device(
    sample_quantities,
    conv_weight,
    conv_bias,
    out_weight,
    obs_index,
    obs_count,
    obs_value,
    obs_weight,
):
    x = sample_quantities[0]
    nvar, rows, cols = x.shape
    n_ens, n_lat, n_lon = (lax.axis_size(axis) for axis in ("ens", "lat", "lon"))
    down_lat = [(i, i + 1) for i in range(n_lat - 1)]
    up_lat = [(j, i) for i, j in down_lat]
    right_lon = [(i, (i + 1) % n_lon) for i in range(n_lon)]
    left_lon = [(j, i) for i, j in right_lon]

    first_rows, last_rows = edge_rows(x)
    north = lax.ppermute(last_rows, "lat", down_lat)
    south = lax.ppermute(first_rows, "lat", up_lat)
    taps, own = spread(x)
    own_left, own_right = edge_columns(own, north, south, rows)
    from_left = lax.ppermute(own_right, "lon", right_lon)
    from_right = lax.ppermute(own_left, "lon", left_lon)

    conv, out_w = packed_weights(conv_weight, conv_bias, out_weight, nvar)
    slots = obs_index.reshape(-1)
    var, row, lane = slots // (rows * cols), slots // cols % rows, slots % cols
    spot = jnp.clip(row * nvar + var, 0, rows * nvar - 1)
    here = lax.axis_index("lat")
    inside = jnp.stack([here > 0, here < n_lat - 1]).astype(jnp.int32)
    fold = (slots.shape[0] // cols, cols)
    devices = n_ens * n_lat * n_lon
    forecast, notes = run_forecast(
        spot,
        inside,
        obs_count.reshape(1),
        taps,
        north,
        south,
        own_left,
        own_right,
        from_left,
        from_right,
        conv,
        out_w,
        lane[:, None],
        obs_value.reshape(fold),
        obs_weight.reshape(fold),
        devices,
    )
    told = lax.all_to_all(notes, ("ens", "lat", "lon"), 0, 0, tiled=True)
    told = told.reshape(n_ens, n_lat * n_lon, *notes.shape[1:])
    if n_ens == 2:
        other = lax.ppermute(forecast, "ens", [(0, 1), (1, 0)])
        me = lax.axis_index("ens").reshape(1)
        return run_analysis(me, told, forecast, other, x.shape)[None]
    return many_members(told, forecast, x.shape)[None]


def solution(mesh):
    return jax.shard_map(
        per_device,
        mesh=mesh,
        in_specs=(
            P("ens", None, "lat", "lon"),
            P(),
            P(),
            P(),
            P("lat", "lon", None),
            P("lat", "lon"),
            P("lat", "lon", None),
            P("lat", "lon", None),
        ),
        out_specs=P("ens", None, "lat", "lon"),
        check_vma=False,
    )
```

```python
import functools
import math

import jax
import jax.numpy as jnp
from jax import lax
from jax.experimental import pallas as pl
from jax.experimental.pallas import tpu as pltpu
from jax.sharding import PartitionSpec as P

NS_ITERS = 20
GELU_A = math.sqrt(2.0 / math.pi)
GELU_B = GELU_A * 0.044715
F32 = jnp.float32
BF16 = jnp.bfloat16
PAD = 8
SMALL = 4 << 20
GROUP = 12


def lanes_of(shape):
    return lax.broadcasted_iota(jnp.int32, shape, len(shape) - 1)


def most_of(total, limit):
    return max(d for d in range(1, limit + 1) if total % d == 0)


def rows_kernel(top_ref, bottom_ref, up_ref, down_ref, stage):
    nvar, tile, cols = top_ref.shape
    for ref, out, first in ((top_ref, up_ref, 0), (bottom_ref, down_ref, tile - 2)):
        stage[...] = ref[...].reshape(nvar * tile, cols).astype(F32)
        both = [stage[pl.ds(first + i, nvar, stride=tile), :] for i in range(2)]
        out[...] = jnp.concatenate(both, axis=0).astype(BF16)


def edge_rows(x):
    nvar, rows, cols = x.shape
    tile = 16
    last = rows // tile - 1
    out = jax.ShapeDtypeStruct((2 * nvar, cols), BF16)
    return pl.pallas_call(
        rows_kernel,
        out_shape=(out, out),
        grid=(1,),
        in_specs=[
            pl.BlockSpec((nvar, tile, cols), lambda i: (0, 0, 0)),
            pl.BlockSpec((nvar, tile, cols), lambda i: (0, last, 0)),
        ],
        out_specs=[pl.BlockSpec((2 * nvar, cols), lambda i: (0, 0))] * 2,
        scratch_shapes=[pltpu.VMEM((nvar * tile, cols), F32)],
        compiler_params=pltpu.CompilerParams(vmem_limit_bytes=SMALL),
        name="edge_rows",
    )(x, x)


def spread_kernel(x_ref, taps_ref, own_ref, stage, xf):
    nvar, rows, cols = x_ref.shape
    block = 3 * nvar + PAD
    wanted = (0, 1, cols - 2, cols - 1)
    k = lax.broadcasted_iota(jnp.int32, (8, cols), 0)
    lane = lanes_of((8, cols))
    pick = jnp.zeros((8, cols), F32)
    for i, c in enumerate(wanted):
        pick = jnp.where((k == i) & (lane == c), 1.0, pick)
    pick = pick.astype(BF16)
    per = cols // rows
    flat = x_ref[...].reshape(nvar * rows, cols)
    xf[...] = flat.astype(F32)
    taken = lax.dot_general(pick, flat, (((1,), (1,)), ((), ())), preferred_element_type=F32)
    for v in range(nvar):
        part = taken[:, (v // per) * cols : (v // per + 1) * cols]
        shift = (2 - (v % per) * rows) % cols
        stage[8 * v : 8 * v + 8, :] = pltpu.roll(part, shift, 1)
    for i in range(len(wanted)):
        own_ref[i * nvar : (i + 1) * nvar, :] = stage[pl.ds(i, nvar, stride=8), :]
    ones = jnp.ones((PAD, cols), F32)

    def fill(r, carry):
        row = xf[pl.ds(r, nvar, stride=rows), :]
        tap = jnp.concatenate([row, pltpu.roll(row, 1, 1), pltpu.roll(row, cols - 1, 1), ones], axis=0)
        at = pl.multiple_of(r * block, 16)
        taps_ref[pl.ds(at, block), :] = tap.astype(BF16)
        return carry

    lax.fori_loop(0, rows, fill, 0, unroll=4)


def spread(x):
    nvar, rows, cols = x.shape
    block = 3 * nvar + PAD
    return pl.pallas_call(
        spread_kernel,
        out_shape=(
            jax.ShapeDtypeStruct((rows * block, cols), BF16),
            jax.ShapeDtypeStruct((4 * nvar, cols), F32),
        ),
        scratch_shapes=[pltpu.VMEM((8 * nvar, cols), F32), pltpu.VMEM((nvar * rows, cols), F32)],
        compiler_params=pltpu.CompilerParams(vmem_limit_bytes=SMALL),
        cost_estimate=pl.CostEstimate(flops=10**8, bytes_accessed=4 * 10**6, transcendentals=0),
        name="spread",
    )(x)


def edge_columns(own, north, south, rows):
    nvar, cols = own.shape[0] // 4, own.shape[1]
    wanted = (0, 1, cols - 2, cols - 1)

    def kernel(own_ref, north_ref, south_ref, left_ref, right_ref):
        lane = lanes_of((nvar, cols))
        halo = []
        for ref, first in ((north_ref, 0), (south_ref, rows + 2)):
            for i in range(2):
                halo.append((first + i, ref[i * nvar : (i + 1) * nvar, :].astype(F32)))
        outs = []
        for i, c in enumerate(wanted):
            column = own_ref[i * nvar : (i + 1) * nvar, :]
            column = jnp.where(lane < rows + 2, column, 0.0)
            for at, row in halo:
                column = jnp.where(lane == at, pltpu.roll(row, (at - c) % cols, 1), column)
            outs.append(column)
        left_ref[...] = jnp.concatenate(outs[:2], axis=0).astype(BF16)
        right_ref[...] = jnp.concatenate(outs[2:], axis=0).astype(BF16)

    out = jax.ShapeDtypeStruct((2 * nvar, cols), BF16)
    return pl.pallas_call(
        kernel,
        out_shape=(out, out),
        compiler_params=pltpu.CompilerParams(vmem_limit_bytes=SMALL),
        name="edge_columns",
    )(own, north, south)


def gelu2(pre):
    pre = pre.astype(BF16)
    inner = pre * (jnp.asarray(GELU_A, BF16) + jnp.asarray(GELU_B, BF16) * (pre * pre))
    return pre + pre * jnp.tanh(inner)


def forecast_kernel(
    spot_ref,
    north_in_ref,
    count_ref,
    taps_ref,
    north_ref,
    south_ref,
    own_left_ref,
    own_right_ref,
    from_left_ref,
    from_right_ref,
    conv_ref,
    out_w_ref,
    lane_ref,
    value_ref,
    weight_ref,
    forecast_ref,
    notes_ref,
    first,
    second,
    final,
    hidden,
    seen,
):
    nvar, cols = north_ref.shape[0] // 2, north_ref.shape[1]
    block = 3 * nvar + PAD
    rows = taps_ref.shape[0] // block
    deep = 3 * block
    lane = lanes_of((nvar, cols))
    ones = jnp.ones((PAD, cols), F32)

    def tap_rows(row, west, east, at):
        left = jnp.where(lane == 0, pltpu.roll(west, (cols - at) % cols, 1), pltpu.roll(row, 1, 1))
        right = jnp.where(
            lane == cols - 1, pltpu.roll(east, (2 * cols - 1 - at) % cols, 1), pltpu.roll(row, cols - 1, 1)
        )
        return jnp.concatenate([row, left, right, ones], axis=0).astype(BF16)

    def hidden_of(patches):
        return gelu2(jnp.dot(conv_ref[...], patches, preferred_element_type=F32))

    def moved(centre, hidden):
        change = jnp.dot(out_w_ref[...], hidden, preferred_element_type=F32)
        return (centre + change).astype(BF16).astype(F32)

    from_left = from_left_ref[...].astype(F32)
    from_right = from_right_ref[...].astype(F32)
    own_left = own_left_ref[...].astype(F32)
    own_right = own_right_ref[...].astype(F32)
    far_west, west = from_left[:nvar], from_left[nvar:]
    east, far_east = from_right[:nvar], from_right[nvar:]
    inner_west, inner_east = own_left[:nvar], own_right[nvar:]

    for ref, start in ((north_ref, 0), (south_ref, rows + 2)):
        for i in range(2):
            row = ref[i * nvar : (i + 1) * nvar, :].astype(F32)
            first[(start + i) * block : (start + i + 1) * block, :] = tap_rows(row, west, east, start + i)

    group = lax.broadcasted_iota(jnp.int32, (block, cols), 0)
    wide = lanes_of((block, cols))
    is_left = (group >= nvar) & (group < 2 * nvar) & (wide == 0)
    is_right = (group >= 2 * nvar) & (group < 3 * nvar) & (wide == cols - 1)
    fix = jnp.where(is_left | is_right, 1.0, 0.0).astype(BF16) > 0
    nothing = jnp.zeros((nvar, cols), F32)
    source = jnp.concatenate([nothing, west, pltpu.roll(east, cols - 1, 1), jnp.zeros((PAD, cols), F32)], axis=0)
    source = source.astype(BF16)

    def fill(r, carry):
        at = pl.multiple_of(r * block, 16)
        mine = pltpu.roll(source, cols - 2 - r, 1)
        to = pl.multiple_of((r + 2) * block, 16)
        first[pl.ds(to, block), :] = jnp.where(fix, mine, taps_ref[pl.ds(at, block), :])
        return carry

    lax.fori_loop(0, rows, fill, 0, unroll=4)

    sides = []
    for mid, low, high in ((west, far_west, inner_west), (east, inner_east, far_east)):
        stack = []
        for a in range(3):
            for entry in (mid, low, high):
                stack.append(pltpu.roll(entry, (1 - a) % cols, 1) if a != 1 else entry)
            stack.append(ones)
        sides.append(jnp.concatenate(stack, axis=0).astype(BF16))
    patches = jnp.concatenate(sides, axis=1)
    beside = moved(jnp.concatenate([west, east], axis=1), hidden_of(patches))
    keep = jnp.where(lane == 1, north_in_ref[0], jnp.where(lane == rows + 2, north_in_ref[1], 1)) > 0
    mid_west = jnp.where(keep, beside[:, :cols], 0.0)
    mid_east = jnp.where(keep, beside[:, cols:], 0.0)

    def ahead(source, at, slot):
        at = pl.multiple_of(at * block, 16)
        patches = jnp.concatenate(
            [source[pl.ds(at, deep), :], source[pl.ds(at + block, deep), :]], axis=1
        )
        hidden[slot] = hidden_of(patches)

    def finish(source, at, slot):
        at = pl.multiple_of(at * block, 16)
        centre = jnp.concatenate(
            [source[pl.ds(at + block, nvar), :], source[pl.ds(at + 2 * block, nvar), :]], axis=1
        ).astype(F32)
        return moved(centre, hidden[slot])

    def first_step(g, carry):
        for q in range(group1):
            ahead(first, 2 * (g * group1 + q), q)
        for q in range(group1):
            i = g * group1 + q
            both = finish(first, 2 * i, q)
            for half in range(2):
                m = 2 * i + half
                good = (jnp.where(m == 0, north_in_ref[0], 1) * jnp.where(m == rows + 1, north_in_ref[1], 1)) > 0
                row = both[:, half * cols : (half + 1) * cols]
                row = jnp.where(good, row, 0.0)
                at = pl.multiple_of(m * block, 16)
                second[pl.ds(at, block), :] = tap_rows(row, mid_west, mid_east, m + 1)
        return carry

    group1 = most_of(rows // 2 + 1, hidden.shape[0])
    lax.fori_loop(0, (rows // 2 + 1) // group1, first_step, 0)

    def second_step(g, carry):
        for q in range(group2):
            ahead(second, 2 * (g * group2 + q), q)
        for q in range(group2):
            j = g * group2 + q
            both = finish(second, 2 * j, q)
            both = jnp.concatenate([both[:, :cols], both[:, cols:]], axis=0)
            at = pl.multiple_of(j * 2 * nvar, 16)
            final[pl.ds(at, 2 * nvar), :] = both
            forecast_ref[pl.ds(at, 2 * nvar), :] = both.astype(BF16)
        return carry

    group2 = most_of(rows // 2, hidden.shape[0])
    lax.fori_loop(0, (rows // 2) // group2, second_step, 0)

    def look(o, carry):
        seen[pl.ds(o, 1), :] = final[pl.ds(spot_ref[o], 1), :]
        return carry

    slots = seen.shape[0]
    lax.fori_loop(0, slots, look, 0, unroll=16)
    masked = jnp.where(lane_ref[...] == lanes_of((slots, cols)), seen[...], 0.0).astype(BF16)
    values = lax.dot_general(
        jnp.ones((8, cols), BF16), masked, (((1,), (1,)), ((), ())), preferred_element_type=F32
    )
    fold = value_ref.shape[0]
    live = lanes_of((fold, cols)) + cols * lax.broadcasted_iota(jnp.int32, (fold, cols), 0) < count_ref[0]
    note = [values[0:1, i * cols : (i + 1) * cols] for i in range(fold)]
    note += [value_ref[...], jnp.where(live, weight_ref[...], 0.0)]
    note.append(jnp.zeros((notes_ref.shape[1] - 3 * fold, cols), F32))
    note = jnp.concatenate(note, axis=0)
    for d in range(notes_ref.shape[0]):
        notes_ref[d] = note


def run_forecast(spot, inside, count, taps, north, south, own_left, own_right, from_left, from_right, conv, out_w, lane, value, weight, devices):
    nvar, cols = north.shape[0] // 2, north.shape[1]
    slots = spot.shape[0]
    block = 3 * nvar + PAD
    rows = taps.shape[0] // block
    note_rows = -(-3 * value.shape[0] // 8) * 8
    smem = pl.BlockSpec(memory_space=pltpu.SMEM)
    vmem = pl.BlockSpec(memory_space=pltpu.VMEM)
    return pl.pallas_call(
        forecast_kernel,
        out_shape=(
            jax.ShapeDtypeStruct((rows * nvar, cols), BF16),
            jax.ShapeDtypeStruct((devices, note_rows, cols), F32),
        ),
        in_specs=[smem, smem, smem] + [vmem] * 12,
        out_specs=(vmem, vmem),
        scratch_shapes=[
            pltpu.VMEM(((rows + 4) * block, cols), BF16),
            pltpu.VMEM(((rows + 2) * block, cols), BF16),
            pltpu.VMEM((rows * nvar, cols), F32),
            pltpu.VMEM((GROUP, conv.shape[0], 2 * cols), BF16),
            pltpu.VMEM((slots, cols), F32),
        ],
        compiler_params=pltpu.CompilerParams(vmem_limit_bytes=16 << 20),
        name="forecast",
    )(spot, inside, count, taps, north, south, own_left, own_right, from_left, from_right, conv, out_w, lane, value, weight)


def pair_weights(gram, proj):
    count = len(proj)
    system = [[gram[k][m] + (float(count - 1) if k == m else 0.0) for m in range(count)] for k in range(count)]
    total = sum(entry * entry for line in system for entry in line)
    scale = jnp.sqrt(total)
    one = jnp.ones_like(scale)
    eye = [[one if k == m else 0.0 * one for m in range(count)] for k in range(count)]

    def times(left, right):
        return [
            [sum(left[k][j] * right[j][m] for j in range(count)) for m in range(count)] for k in range(count)
        ]

    current = [[entry / scale for entry in line] for line in system]
    inverse = eye
    for turn in range(NS_ITERS):
        both = times(inverse, current)
        factor = [[1.5 * eye[k][m] - 0.5 * both[k][m] for m in range(count)] for k in range(count)]
        current = times(current, factor)
        inverse = times(factor, inverse)
    root = jnp.sqrt(scale)
    root_inv = [[entry / root for entry in line] for line in inverse]
    half = [sum(root_inv[k][j] * proj[j] for j in range(count)) for k in range(count)]
    mean_w = [sum(root_inv[k][j] * half[j] for j in range(count)) for k in range(count)]
    span = math.sqrt(count - 1.0)
    full = [[mean_w[k] + span * root_inv[k][m] for m in range(count)] for k in range(count)]
    centre = [sum(full[k][m] for k in range(count)) / count for m in range(count)]
    return [[1.0 / count + full[k][m] - centre[m] for m in range(count)] for k in range(count)]


def analysis_kernel(me_ref, told_ref, mine_ref, other_ref, out_ref, blended):
    count, shards = told_ref.shape[0], told_ref.shape[1]
    nvar, rows, cols = out_ref.shape
    pairs = [(k, m) for k in range(count) for m in range(k, count)]
    sums = {key: 0.0 for key in pairs}
    for k in range(count):
        sums[k] = 0.0
    for s in range(shards):
        hx = [told_ref[k, s, 0:2, :] for k in range(count)]
        value = told_ref[0, s, 2:4, :]
        weight = told_ref[0, s, 4:6, :]
        mean = sum(hx) / count
        spread = [h - mean for h in hx]
        innov = value - mean
        for k in range(count):
            scaled = spread[k] * weight
            sums[k] = sums[k] + scaled * innov
            for m in range(k, count):
                sums[k, m] = sums[k, m] + scaled * spread[m]
    tile = (8, cols)
    whole = {key: jnp.broadcast_to(jnp.sum(term, keepdims=True), tile) for key, term in sums.items()}
    gram = [[whole[min(k, m), max(k, m)] for m in range(count)] for k in range(count)]
    weights = pair_weights(gram, [whole[k] for k in range(count)])
    me = me_ref[0]
    mine = jnp.where(me == 0, weights[0][0], weights[1][1])[0:1, :]
    other = jnp.where(me == 0, weights[1][0], weights[0][1])[0:1, :]
    blended[...] = mine * mine_ref[...].astype(F32) + other * other_ref[...].astype(F32)
    for v in range(nvar):
        for r in range(0, rows, 16):
            halves = [
                blended[pl.ds((r + 8 * i) * nvar + v, 8, stride=nvar), :] for i in range(2)
            ]
            out_ref[v, r : r + 16, :] = jnp.concatenate(halves, axis=0).astype(BF16)


def run_analysis(me, told, mine, other, shape):
    nvar, rows, cols = shape
    vmem = pl.BlockSpec(memory_space=pltpu.VMEM)
    return pl.pallas_call(
        analysis_kernel,
        out_shape=jax.ShapeDtypeStruct(shape, BF16),
        in_specs=[pl.BlockSpec(memory_space=pltpu.SMEM), vmem, vmem, vmem],
        out_specs=vmem,
        scratch_shapes=[pltpu.VMEM((nvar * rows, cols), F32)],
        compiler_params=pltpu.CompilerParams(vmem_limit_bytes=8 << 20),
        name="analysis",
    )(me, told, mine, other)


def blend_weights(gram, proj):
    entries_number = gram.shape[0]
    eye = jnp.eye(entries_number, dtype=gram.dtype)
    system = (entries_number - 1) * eye + gram
    scale = jnp.sqrt(jnp.sum(system * system))
    current = system / scale
    inverse = eye
    for turn in range(NS_ITERS):
        factor = 1.5 * eye - 0.5 * jnp.dot(inverse, current, precision=lax.Precision.HIGHEST)
        current = jnp.dot(current, factor, precision=lax.Precision.HIGHEST)
        inverse = jnp.dot(factor, inverse, precision=lax.Precision.HIGHEST)
    root_inv = inverse / jnp.sqrt(scale)
    half = jnp.dot(root_inv, proj, precision=lax.Precision.HIGHEST)
    mean_w = jnp.dot(root_inv, half, precision=lax.Precision.HIGHEST)
    full = mean_w[:, None] + math.sqrt(entries_number - 1.0) * root_inv
    return 1.0 / entries_number + full - jnp.mean(full, axis=0, keepdims=True)


def many_members(told, forecast, shape):
    nvar, rows, cols = shape
    members = told[:, :, 0:2, :].reshape(told.shape[0], -1)
    value = told[0, :, 2:4, :].reshape(-1)
    weight = told[0, :, 4:6, :].reshape(-1)
    mean = jnp.mean(members, axis=0)
    spread = members - mean[None, :]
    innov = value - mean
    weighted = spread * weight[None, :]
    gram = jnp.dot(weighted, spread.T, precision=lax.Precision.HIGHEST)
    proj = jnp.dot(weighted, innov, precision=lax.Precision.HIGHEST)
    transform = blend_weights(gram, proj)
    column = lax.dynamic_slice_in_dim(transform, lax.axis_index("ens"), 1, 1)[:, 0]
    everyone = lax.all_gather(forecast[None], "ens", axis=0, tiled=True)
    blended = jnp.tensordot(column, everyone.astype(F32), axes=1, precision=lax.Precision.HIGHEST)
    return blended.astype(BF16).reshape(rows, nvar, cols).transpose(1, 0, 2)


def packed_weights(conv_weight, conv_bias, out_weight, nvar):
    hid = conv_bias.shape[0]
    block = 3 * nvar + PAD

    def kernel(conv_ref, bias_ref, out_ref, packed_ref, half_ref):
        bias = bias_ref[...]
        high = bias.astype(BF16).astype(F32)
        middle = (bias - high).astype(BF16).astype(F32)
        low = (bias - high - middle).astype(BF16).astype(F32)
        rest = jnp.zeros((PAD - 3, hid), F32)
        pieces = []
        for a in range(3):
            for b in (1, 0, 2):
                at = (3 * a + b) * nvar
                pieces.append(conv_ref[at : at + nvar, :].astype(F32))
            if a == 1:
                pieces.append(jnp.concatenate([high, middle, low, rest], axis=0))
            else:
                pieces.append(jnp.zeros((PAD, hid), F32))
        packed_ref[...] = jnp.concatenate(pieces, axis=0).T.astype(BF16)
        half_ref[...] = (out_ref[...].astype(F32) * 0.5).astype(BF16)

    return pl.pallas_call(
        kernel,
        out_shape=(
            jax.ShapeDtypeStruct((hid, 3 * block), BF16),
            jax.ShapeDtypeStruct((nvar, hid), BF16),
        ),
        compiler_params=pltpu.CompilerParams(vmem_limit_bytes=SMALL),
        cost_estimate=pl.CostEstimate(flops=10**7, bytes_accessed=10**6, transcendentals=0),
        name="packed_weights",
    )(conv_weight, conv_bias[None], out_weight.T)


def per_device(
    sample_quantities,
    conv_weight,
    conv_bias,
    out_weight,
    obs_index,
    obs_count,
    obs_value,
    obs_weight,
):
    x = sample_quantities[0]
    nvar, rows, cols = x.shape
    n_ens, n_lat, n_lon = (lax.axis_size(axis) for axis in ("ens", "lat", "lon"))
    down_lat = [(i, i + 1) for i in range(n_lat - 1)]
    up_lat = [(j, i) for i, j in down_lat]
    right_lon = [(i, (i + 1) % n_lon) for i in range(n_lon)]
    left_lon = [(j, i) for i, j in right_lon]

    first_rows, last_rows = edge_rows(x)
    north = lax.ppermute(last_rows, "lat", down_lat)
    south = lax.ppermute(first_rows, "lat", up_lat)
    taps, own = spread(x)
    own_left, own_right = edge_columns(own, north, south, rows)
    from_left = lax.ppermute(own_right, "lon", right_lon)
    from_right = lax.ppermute(own_left, "lon", left_lon)

    conv, out_w = packed_weights(conv_weight, conv_bias, out_weight, nvar)
    slots = obs_index.reshape(-1)
    var, row, lane = slots // (rows * cols), slots // cols % rows, slots % cols
    spot = jnp.clip(row * nvar + var, 0, rows * nvar - 1)
    here = lax.axis_index("lat")
    inside = jnp.stack([here > 0, here < n_lat - 1]).astype(jnp.int32)
    fold = (slots.shape[0] // cols, cols)
    devices = n_ens * n_lat * n_lon
    forecast, notes = run_forecast(
        spot,
        inside,
        obs_count.reshape(1),
        taps,
        north,
        south,
        own_left,
        own_right,
        from_left,
        from_right,
        conv,
        out_w,
        lane[:, None],
        obs_value.reshape(fold),
        obs_weight.reshape(fold),
        devices,
    )
    told = lax.all_to_all(notes, ("ens", "lat", "lon"), 0, 0, tiled=True)
    told = told.reshape(n_ens, n_lat * n_lon, *notes.shape[1:])
    if n_ens == 2:
        other = lax.ppermute(forecast, "ens", [(0, 1), (1, 0)])
        me = lax.axis_index("ens").reshape(1)
        return run_analysis(me, told, forecast, other, x.shape)[None]
    return many_members(told, forecast, x.shape)[None]


def solution(mesh):
    return jax.shard_map(
        per_device,
        mesh=mesh,
        in_specs=(
            P("ens", None, "lat", "lon"),
            P(),
            P(),
            P(),
            P("lat", "lon", None),
            P("lat", "lon"),
            P("lat", "lon", None),
            P("lat", "lon", None),
        ),
        out_specs=P("ens", None, "lat", "lon"),
        check_vma=False,
    )
```

```python
import functools
import math

import jax
import jax.numpy as jnp
from jax import lax
from jax.experimental import pallas as pl
from jax.experimental.pallas import tpu as pltpu
from jax.sharding import PartitionSpec as P

NS_ITERS = 20
GELU_A = math.sqrt(2.0 / math.pi)
GELU_B = GELU_A * 0.044715
F32 = jnp.float32
BF16 = jnp.bfloat16
PAD = 8
SMALL = 4 << 20
GROUP = 12


def lanes_of(shape):
    return lax.broadcasted_iota(jnp.int32, shape, len(shape) - 1)


def most_of(total, limit):
    return max(d for d in range(1, limit + 1) if total % d == 0)


def edge_rows(x):
    nvar, rows, cols = x.shape
    tile = 16

    def kernel(x_ref, up_ref, down_ref, part, stage, sems):
        copies = []
        for i, first in enumerate((0, rows - tile)):
            copies.append(pltpu.make_async_copy(x_ref.at[:, first : first + tile, :], part.at[i], sems.at[i]))
            copies[i].start()
        for i, (out, first) in enumerate(((up_ref, 0), (down_ref, tile - 2))):
            copies[i].wait()
            stage[...] = part[i].reshape(nvar * tile, cols).astype(F32)
            both = [stage[pl.ds(first + j, nvar, stride=tile), :] for j in range(2)]
            out[...] = jnp.concatenate(both, axis=0).astype(BF16)

    out = jax.ShapeDtypeStruct((2 * nvar, cols), BF16)
    return pl.pallas_call(
        kernel,
        out_shape=(out, out),
        in_specs=[pl.BlockSpec(memory_space=pltpu.HBM)],
        scratch_shapes=[
            pltpu.VMEM((2, nvar, tile, cols), BF16),
            pltpu.VMEM((nvar * tile, cols), F32),
            pltpu.SemaphoreType.DMA((2,)),
        ],
        compiler_params=pltpu.CompilerParams(vmem_limit_bytes=SMALL),
        name="edge_rows",
    )(x)


def spread_kernel(x_ref, taps_ref, own_ref, stage, xf):
    nvar, rows, cols = x_ref.shape
    block = 3 * nvar + PAD
    wanted = (0, 1, cols - 2, cols - 1)
    k = lax.broadcasted_iota(jnp.int32, (8, cols), 0)
    lane = lanes_of((8, cols))
    pick = jnp.zeros((8, cols), F32)
    for i, c in enumerate(wanted):
        pick = jnp.where((k == i) & (lane == c), 1.0, pick)
    pick = pick.astype(BF16)
    per = cols // rows
    flat = x_ref[...].reshape(nvar * rows, cols)
    for v in range(nvar):
        column = x_ref[v].astype(F32)
        for r in range(0, rows, 8):
            xf[pl.ds(r * nvar + v, 8, stride=nvar), :] = column[r : r + 8]
    taken = lax.dot_general(pick, flat, (((1,), (1,)), ((), ())), preferred_element_type=F32)
    for v in range(nvar):
        part = taken[:, (v // per) * cols : (v // per + 1) * cols]
        shift = (2 - (v % per) * rows) % cols
        stage[8 * v : 8 * v + 8, :] = pltpu.roll(part, shift, 1)
    for i in range(len(wanted)):
        own_ref[i * nvar : (i + 1) * nvar, :] = stage[pl.ds(i, nvar, stride=8), :]
    ones = jnp.ones((PAD, cols), F32)

    def fill(r, carry):
        row = xf[pl.ds(pl.multiple_of(r * nvar, 8), nvar), :]
        tap = jnp.concatenate([row, pltpu.roll(row, 1, 1), pltpu.roll(row, cols - 1, 1), ones], axis=0)
        at = pl.multiple_of(r * block, 16)
        taps_ref[pl.ds(at, block), :] = tap.astype(BF16)
        return carry

    lax.fori_loop(0, rows, fill, 0, unroll=4)


def spread(x):
    nvar, rows, cols = x.shape
    block = 3 * nvar + PAD
    return pl.pallas_call(
        spread_kernel,
        out_shape=(
            jax.ShapeDtypeStruct((rows * block, cols), BF16),
            jax.ShapeDtypeStruct((4 * nvar, cols), F32),
        ),
        scratch_shapes=[pltpu.VMEM((8 * nvar, cols), F32), pltpu.VMEM((nvar * rows, cols), F32)],
        compiler_params=pltpu.CompilerParams(vmem_limit_bytes=SMALL),
        cost_estimate=pl.CostEstimate(flops=10**8, bytes_accessed=4 * 10**6, transcendentals=0),
        name="spread",
    )(x)


def edge_columns(own, north, south, rows):
    nvar, cols = own.shape[0] // 4, own.shape[1]
    wanted = (0, 1, cols - 2, cols - 1)

    def kernel(own_ref, north_ref, south_ref, left_ref, right_ref):
        lane = lanes_of((nvar, cols))
        halo = []
        for ref, first in ((north_ref, 0), (south_ref, rows + 2)):
            for i in range(2):
                halo.append((first + i, ref[i * nvar : (i + 1) * nvar, :].astype(F32)))
        outs = []
        for i, c in enumerate(wanted):
            column = own_ref[i * nvar : (i + 1) * nvar, :]
            column = jnp.where(lane < rows + 2, column, 0.0)
            for at, row in halo:
                column = jnp.where(lane == at, pltpu.roll(row, (at - c) % cols, 1), column)
            outs.append(column)
        left_ref[...] = jnp.concatenate(outs[:2], axis=0).astype(BF16)
        right_ref[...] = jnp.concatenate(outs[2:], axis=0).astype(BF16)

    out = jax.ShapeDtypeStruct((2 * nvar, cols), BF16)
    return pl.pallas_call(
        kernel,
        out_shape=(out, out),
        compiler_params=pltpu.CompilerParams(vmem_limit_bytes=SMALL),
        name="edge_columns",
    )(own, north, south)


def gelu2(pre):
    pre = pre.astype(BF16)
    inner = pre * (jnp.asarray(GELU_A, BF16) + jnp.asarray(GELU_B, BF16) * (pre * pre))
    return pre + pre * jnp.tanh(inner)


def forecast_kernel(
    spot_ref,
    count_ref,
    taps_ref,
    north_ref,
    south_ref,
    own_left_ref,
    own_right_ref,
    from_left_ref,
    from_right_ref,
    conv_ref,
    out_w_ref,
    chosen_ref,
    value_ref,
    weight_ref,
    forecast_ref,
    notes_ref,
    first,
    second,
    final,
    hidden,
    seen,
):
    nvar, cols = north_ref.shape[0] // 2, north_ref.shape[1]
    block = 3 * nvar + PAD
    rows = taps_ref.shape[0] // block
    deep = 3 * block
    lane = lanes_of((nvar, cols))
    ones = jnp.ones((PAD, cols), F32)

    def tap_rows(row, west, east, at):
        left = jnp.where(lane == 0, pltpu.roll(west, (cols - at) % cols, 1), pltpu.roll(row, 1, 1))
        right = jnp.where(
            lane == cols - 1, pltpu.roll(east, (2 * cols - 1 - at) % cols, 1), pltpu.roll(row, cols - 1, 1)
        )
        return jnp.concatenate([row, left, right, ones], axis=0).astype(BF16)

    def hidden_of(patches):
        return gelu2(jnp.dot(conv_ref[...], patches, preferred_element_type=F32))

    def moved(centre, hidden):
        change = jnp.dot(out_w_ref[...], hidden, preferred_element_type=F32)
        return (centre + change).astype(BF16).astype(F32)

    from_left = from_left_ref[...].astype(F32)
    from_right = from_right_ref[...].astype(F32)
    own_left = own_left_ref[...].astype(F32)
    own_right = own_right_ref[...].astype(F32)
    far_west, west = from_left[:nvar], from_left[nvar:]
    east, far_east = from_right[:nvar], from_right[nvar:]
    inner_west, inner_east = own_left[:nvar], own_right[nvar:]

    for ref, start in ((north_ref, 0), (south_ref, rows + 2)):
        for i in range(2):
            row = ref[i * nvar : (i + 1) * nvar, :].astype(F32)
            first[(start + i) * block : (start + i + 1) * block, :] = tap_rows(row, west, east, start + i)

    group = lax.broadcasted_iota(jnp.int32, (block, cols), 0)
    wide = lanes_of((block, cols))
    is_left = (group >= nvar) & (group < 2 * nvar) & (wide == 0)
    is_right = (group >= 2 * nvar) & (group < 3 * nvar) & (wide == cols - 1)
    fix = jnp.where(is_left | is_right, 1.0, 0.0).astype(BF16) > 0
    nothing = jnp.zeros((nvar, cols), F32)
    source = jnp.concatenate([nothing, west, pltpu.roll(east, cols - 1, 1), jnp.zeros((PAD, cols), F32)], axis=0)
    source = source.astype(BF16)

    def fill(r, carry):
        at = pl.multiple_of(r * block, 16)
        mine = pltpu.roll(source, cols - 2 - r, 1)
        to = pl.multiple_of((r + 2) * block, 16)
        first[pl.ds(to, block), :] = jnp.where(fix, mine, taps_ref[pl.ds(at, block), :])
        return carry

    lax.fori_loop(0, rows, fill, 0, unroll=4)

    sides = []
    for mid, low, high in ((west, far_west, inner_west), (east, inner_east, far_east)):
        stack = []
        for a in range(3):
            for entry in (mid, low, high):
                stack.append(pltpu.roll(entry, (1 - a) % cols, 1) if a != 1 else entry)
            stack.append(ones)
        sides.append(jnp.concatenate(stack, axis=0).astype(BF16))
    patches = jnp.concatenate(sides, axis=1)
    beside = moved(jnp.concatenate([west, east], axis=1), hidden_of(patches))
    here = lax.axis_index("lat")
    north_in = (here > 0).astype(jnp.int32)
    south_in = (here < lax.axis_size("lat") - 1).astype(jnp.int32)
    keep = jnp.where(lane == 1, north_in, jnp.where(lane == rows + 2, south_in, 1)) > 0
    mid_west = jnp.where(keep, beside[:, :cols], 0.0)
    mid_east = jnp.where(keep, beside[:, cols:], 0.0)

    def ahead(source, at, slot):
        at = pl.multiple_of(at * block, 16)
        patches = jnp.concatenate(
            [source[pl.ds(at, deep), :], source[pl.ds(at + block, deep), :]], axis=1
        )
        hidden[slot] = hidden_of(patches)

    def finish(source, at, slot):
        at = pl.multiple_of(at * block, 16)
        centre = jnp.concatenate(
            [source[pl.ds(at + block, nvar), :], source[pl.ds(at + 2 * block, nvar), :]], axis=1
        ).astype(F32)
        return moved(centre, hidden[slot])

    def first_step(g, carry):
        for q in range(group1):
            ahead(first, 2 * (g * group1 + q), q)
        for q in range(group1):
            i = g * group1 + q
            both = finish(first, 2 * i, q)
            for half in range(2):
                m = 2 * i + half
                good = (jnp.where(m == 0, north_in, 1) * jnp.where(m == rows + 1, south_in, 1)) > 0
                row = both[:, half * cols : (half + 1) * cols]
                row = jnp.where(good, row, 0.0)
                at = pl.multiple_of(m * block, 16)
                second[pl.ds(at, block), :] = tap_rows(row, mid_west, mid_east, m + 1)
        return carry

    group1 = most_of(rows // 2 + 1, hidden.shape[0])
    lax.fori_loop(0, (rows // 2 + 1) // group1, first_step, 0)

    def second_step(g, carry):
        for q in range(group2):
            ahead(second, 2 * (g * group2 + q), q)
        for q in range(group2):
            j = g * group2 + q
            both = finish(second, 2 * j, q)
            both = jnp.concatenate([both[:, :cols], both[:, cols:]], axis=0)
            at = pl.multiple_of(j * 2 * nvar, 16)
            final[pl.ds(at, 2 * nvar), :] = both
            forecast_ref[pl.ds(at, 2 * nvar), :] = both.astype(BF16)
        return carry

    group2 = most_of(rows // 2, hidden.shape[0])
    lax.fori_loop(0, (rows // 2) // group2, second_step, 0)

    def look(o, carry):
        seen[pl.ds(o, 1), :] = final[pl.ds(spot_ref[o // cols, o % cols], 1), :]
        return carry

    slots = seen.shape[0]
    lax.fori_loop(0, slots, look, 0, unroll=16)
    masked = seen[...].astype(BF16) * chosen_ref[...]
    values = lax.dot_general(
        jnp.ones((8, cols), BF16), masked, (((1,), (1,)), ((), ())), preferred_element_type=F32
    )
    fold = value_ref.shape[0]
    live = lanes_of((fold, cols)) + cols * lax.broadcasted_iota(jnp.int32, (fold, cols), 0) < count_ref[0, 0]
    member = lax.axis_index("ens")
    weight = jnp.where(live, weight_ref[...], 0.0)
    extra = jnp.where(member == 0, value_ref[...], jnp.where(member == 1, weight, 0.0))
    note = [values[0:1, i * cols : (i + 1) * cols] for i in range(fold)] + [extra]
    note = jnp.concatenate(note, axis=0).astype(BF16)
    for d in range(notes_ref.shape[0]):
        notes_ref[d] = note


def run_forecast(spot, count, taps, north, south, own_left, own_right, from_left, from_right, conv, out_w, chosen, value, weight, devices):
    nvar, cols = north.shape[0] // 2, north.shape[1]
    slots = spot.shape[0] * spot.shape[1]
    block = 3 * nvar + PAD
    rows = taps.shape[0] // block
    smem = pl.BlockSpec(memory_space=pltpu.SMEM)
    vmem = pl.BlockSpec(memory_space=pltpu.VMEM)
    return pl.pallas_call(
        forecast_kernel,
        out_shape=(
            jax.ShapeDtypeStruct((rows * nvar, cols), BF16),
            jax.ShapeDtypeStruct((devices, 2 * value.shape[0], cols), BF16),
        ),
        in_specs=[smem, smem] + [vmem] * 12,
        out_specs=(vmem, vmem),
        scratch_shapes=[
            pltpu.VMEM(((rows + 4) * block, cols), BF16),
            pltpu.VMEM(((rows + 2) * block, cols), BF16),
            pltpu.VMEM((rows * nvar, cols), F32),
            pltpu.VMEM((GROUP, conv.shape[0], 2 * cols), BF16),
            pltpu.VMEM((slots, cols), F32),
        ],
        compiler_params=pltpu.CompilerParams(vmem_limit_bytes=16 << 20),
        name="forecast",
    )(spot, count, taps, north, south, own_left, own_right, from_left, from_right, conv, out_w, chosen, value, weight)


def pair_weights(gram, proj):
    count = len(proj)
    system = [[gram[k][m] + (float(count - 1) if k == m else 0.0) for m in range(count)] for k in range(count)]
    total = sum(entry * entry for line in system for entry in line)
    scale = jnp.sqrt(total)
    one = jnp.ones_like(scale)
    eye = [[one if k == m else 0.0 * one for m in range(count)] for k in range(count)]

    def times(left, right):
        return [
            [sum(left[k][j] * right[j][m] for j in range(count)) for m in range(count)] for k in range(count)
        ]

    current = [[entry / scale for entry in line] for line in system]
    inverse = eye
    for turn in range(NS_ITERS):
        both = times(inverse, current)
        factor = [[1.5 * eye[k][m] - 0.5 * both[k][m] for m in range(count)] for k in range(count)]
        current = times(current, factor)
        inverse = times(factor, inverse)
    root = jnp.sqrt(scale)
    root_inv = [[entry / root for entry in line] for line in inverse]
    half = [sum(root_inv[k][j] * proj[j] for j in range(count)) for k in range(count)]
    mean_w = [sum(root_inv[k][j] * half[j] for j in range(count)) for k in range(count)]
    span = math.sqrt(count - 1.0)
    full = [[mean_w[k] + span * root_inv[k][m] for m in range(count)] for k in range(count)]
    centre = [sum(full[k][m] for k in range(count)) / count for m in range(count)]
    return [[1.0 / count + full[k][m] - centre[m] for m in range(count)] for k in range(count)]


def analysis_kernel(told_ref, mine_ref, other_ref, out_ref, blended, packed, sems):
    count = lax.axis_size("ens")
    nvar, rows, cols = packed.shape[1], out_ref.shape[1], packed.shape[3]
    depth = told_ref.shape[1]
    told = told_ref[...].astype(F32).reshape(count, -1, cols)
    fold = depth // 2
    size = told.shape[1]
    hx = [told[k] for k in range(count)]
    value = pltpu.roll(told[0], size - fold, 0)
    weight = pltpu.roll(told[1], size - fold, 0)
    used = lax.broadcasted_iota(jnp.int32, (size, cols), 0) % depth < fold
    weight = jnp.where(used, weight, 0.0)
    mean = sum(hx) / count
    spread_of = [h - mean for h in hx]
    innov = value - mean
    tile = (8, cols)

    def total(term):
        return jnp.broadcast_to(jnp.sum(term, keepdims=True), tile)

    scaled = [part * weight for part in spread_of]
    gram = [[None] * count for k in range(count)]
    for k in range(count):
        for m in range(k, count):
            gram[k][m] = gram[m][k] = total(scaled[k] * spread_of[m])
    weights = pair_weights(gram, [total(scaled[k] * innov) for k in range(count)])
    me = lax.axis_index("ens")
    mine = jnp.where(me == 0, weights[0][0], weights[1][1])[0:1, :]
    other = jnp.where(me == 0, weights[1][0], weights[0][1])[0:1, :]
    high = packed.shape[2]

    def copy_of(c):
        return pltpu.make_async_copy(packed.at[c], out_ref.at[:, pl.ds(c * high, high), :], sems.at[c])

    for c in range(rows // high):
        at = c * high * nvar
        part = slice(at, at + high * nvar)
        blended[c] = mine * mine_ref[part, :].astype(F32) + other * other_ref[part, :].astype(F32)
        for v in range(nvar):
            for r in range(0, high, 16):
                halves = [blended[c, pl.ds((r + 8 * i) * nvar + v, 8, stride=nvar), :] for i in range(2)]
                packed[c, v, r : r + 16, :] = jnp.concatenate(halves, axis=0).astype(BF16)
        copy_of(c).start()
    for c in range(rows // high):
        copy_of(c).wait()


def run_analysis(told, mine, other, shape):
    nvar, rows, cols = shape
    high = 16
    vmem = pl.BlockSpec(memory_space=pltpu.VMEM)
    return pl.pallas_call(
        analysis_kernel,
        out_shape=jax.ShapeDtypeStruct(shape, BF16),
        in_specs=[vmem, vmem, vmem],
        out_specs=pl.BlockSpec(memory_space=pltpu.HBM),
        scratch_shapes=[
            pltpu.VMEM((rows // high, high * nvar, cols), F32),
            pltpu.VMEM((rows // high, nvar, high, cols), BF16),
            pltpu.SemaphoreType.DMA((rows // high,)),
        ],
        compiler_params=pltpu.CompilerParams(vmem_limit_bytes=8 << 20),
        name="analysis",
    )(told, mine, other)


def blend_weights(gram, proj):
    entries_number = gram.shape[0]
    eye = jnp.eye(entries_number, dtype=gram.dtype)
    system = (entries_number - 1) * eye + gram
    scale = jnp.sqrt(jnp.sum(system * system))
    current = system / scale
    inverse = eye
    for turn in range(NS_ITERS):
        factor = 1.5 * eye - 0.5 * jnp.dot(inverse, current, precision=lax.Precision.HIGHEST)
        current = jnp.dot(current, factor, precision=lax.Precision.HIGHEST)
        inverse = jnp.dot(factor, inverse, precision=lax.Precision.HIGHEST)
    root_inv = inverse / jnp.sqrt(scale)
    half = jnp.dot(root_inv, proj, precision=lax.Precision.HIGHEST)
    mean_w = jnp.dot(root_inv, half, precision=lax.Precision.HIGHEST)
    full = mean_w[:, None] + math.sqrt(entries_number - 1.0) * root_inv
    return 1.0 / entries_number + full - jnp.mean(full, axis=0, keepdims=True)


def many_members(told, forecast, shape):
    nvar, rows, cols = shape
    fold = told.shape[1] // 2
    told = told.astype(F32).reshape(lax.axis_size("ens"), -1, *told.shape[1:])
    members = told[:, :, :fold, :].reshape(told.shape[0], -1)
    value = told[0, :, fold:, :].reshape(-1)
    weight = told[1, :, fold:, :].reshape(-1)
    mean = jnp.mean(members, axis=0)
    spread = members - mean[None, :]
    innov = value - mean
    weighted = spread * weight[None, :]
    gram = jnp.dot(weighted, spread.T, precision=lax.Precision.HIGHEST)
    proj = jnp.dot(weighted, innov, precision=lax.Precision.HIGHEST)
    transform = blend_weights(gram, proj)
    column = lax.dynamic_slice_in_dim(transform, lax.axis_index("ens"), 1, 1)[:, 0]
    everyone = lax.all_gather(forecast[None], "ens", axis=0, tiled=True)
    blended = jnp.tensordot(column, everyone.astype(F32), axes=1, precision=lax.Precision.HIGHEST)
    return blended.astype(BF16).reshape(rows, nvar, cols).transpose(1, 0, 2)


def prepare(conv_weight, conv_bias, out_weight, index, shape):
    nvar, rows, cols = shape
    fold = index.shape[0]
    hid = conv_bias.shape[0]
    block = 3 * nvar + PAD

    def kernel(conv_ref, bias_ref, out_ref, index_ref, packed_ref, half_ref, spot_ref, chosen_ref):
        bias = bias_ref[...]
        high = bias.astype(BF16).astype(F32)
        middle = (bias - high).astype(BF16).astype(F32)
        low = (bias - high - middle).astype(BF16).astype(F32)
        rest = jnp.zeros((PAD - 3, hid), F32)
        pieces = []
        for a in range(3):
            for b in (1, 0, 2):
                at = (3 * a + b) * nvar
                pieces.append(conv_ref[at : at + nvar, :].astype(F32))
            if a == 1:
                pieces.append(jnp.concatenate([high, middle, low, rest], axis=0))
            else:
                pieces.append(jnp.zeros((PAD, hid), F32))
        packed_ref[...] = jnp.concatenate(pieces, axis=0).T.astype(BF16)
        half_ref[...] = (out_ref[...].astype(F32) * 0.5).astype(BF16)
        index = index_ref[...]
        row = index // cols % rows
        var = index // (rows * cols)
        spot_ref[...] = jnp.clip(row * nvar + var, 0, rows * nvar - 1)
        lane = (index % cols).astype(F32)
        for i in range(fold):
            across = jnp.broadcast_to(lane[i : i + 1, :], (cols, cols)).T
            hot = across == lanes_of((cols, cols)).astype(F32)
            chosen_ref[i * cols : (i + 1) * cols, :] = jnp.where(hot, 1.0, 0.0).astype(BF16)

    return pl.pallas_call(
        kernel,
        out_shape=(
            jax.ShapeDtypeStruct((hid, 3 * block), BF16),
            jax.ShapeDtypeStruct((nvar, hid), BF16),
            jax.ShapeDtypeStruct((fold, cols), jnp.int32),
            jax.ShapeDtypeStruct((fold * cols, cols), BF16),
        ),
        compiler_params=pltpu.CompilerParams(vmem_limit_bytes=SMALL),
        cost_estimate=pl.CostEstimate(flops=10**7, bytes_accessed=10**6, transcendentals=0),
        name="prepare",
    )(conv_weight, conv_bias[None], out_weight.T, index)


def per_device(
    sample_quantities,
    conv_weight,
    conv_bias,
    out_weight,
    obs_index,
    obs_count,
    obs_value,
    obs_weight,
):
    x = sample_quantities[0]
    nvar, rows, cols = x.shape
    n_ens, n_lat, n_lon = (lax.axis_size(axis) for axis in ("ens", "lat", "lon"))
    down_lat = [(i, i + 1) for i in range(n_lat - 1)]
    up_lat = [(j, i) for i, j in down_lat]
    right_lon = [(i, (i + 1) % n_lon) for i in range(n_lon)]
    left_lon = [(j, i) for i, j in right_lon]

    first_rows, last_rows = edge_rows(x)
    north = lax.ppermute(last_rows, "lat", down_lat)
    south = lax.ppermute(first_rows, "lat", up_lat)
    taps, own = spread(x)
    own_left, own_right = edge_columns(own, north, south, rows)
    from_left = lax.ppermute(own_right, "lon", right_lon)
    from_right = lax.ppermute(own_left, "lon", left_lon)

    fold = (obs_index.size // cols, cols)
    index, own_left, own_right = lax.optimization_barrier((obs_index, own_left, own_right))
    conv, out_w, spot, chosen = prepare(conv_weight, conv_bias, out_weight, index.reshape(fold), x.shape)
    forecast, notes = run_forecast(
        spot,
        obs_count,
        taps,
        north,
        south,
        own_left,
        own_right,
        from_left,
        from_right,
        conv,
        out_w,
        chosen,
        obs_value.reshape(fold),
        obs_weight.reshape(fold),
        n_ens * n_lat * n_lon,
    )
    told = lax.all_to_all(notes, ("ens", "lat", "lon"), 0, 0, tiled=True)
    if n_ens == 2:
        other = lax.ppermute(forecast, "ens", [(0, 1), (1, 0)])
        return run_analysis(told, forecast, other, x.shape)[None]
    return many_members(told, forecast, x.shape)[None]


def solution(mesh):
    return jax.shard_map(
        per_device,
        mesh=mesh,
        in_specs=(
            P("ens", None, "lat", "lon"),
            P(),
            P(),
            P(),
            P("lat", "lon", None),
            P("lat", "lon"),
            P("lat", "lon", None),
            P("lat", "lon", None),
        ),
        out_specs=P("ens", None, "lat", "lon"),
        check_vma=False,
    )
```

```python
import functools
import math

import jax
import jax.numpy as jnp
from jax import lax
from jax.experimental import pallas as pl
from jax.experimental.pallas import tpu as pltpu
from jax.sharding import PartitionSpec as P

NS_ITERS = 20
GELU_A = math.sqrt(2.0 / math.pi)
GELU_B = GELU_A * 0.044715
F32 = jnp.float32
BF16 = jnp.bfloat16
PAD = 8
SMALL = 4 << 20
GROUP = 12


def lanes_of(shape):
    return lax.broadcasted_iota(jnp.int32, shape, len(shape) - 1)


def most_of(total, limit):
    return max(d for d in range(1, limit + 1) if total % d == 0)


def edge_rows(x):
    nvar, rows, cols = x.shape
    tile = 16

    def kernel(x_ref, up_ref, down_ref, part, stage, sems):
        copies = []
        for i, first in enumerate((0, rows - tile)):
            copies.append(pltpu.make_async_copy(x_ref.at[:, first : first + tile, :], part.at[i], sems.at[i]))
            copies[i].start()
        for i, (out, first) in enumerate(((up_ref, 0), (down_ref, tile - 2))):
            copies[i].wait()
            stage[...] = part[i].reshape(nvar * tile, cols).astype(F32)
            both = [stage[pl.ds(first + j, nvar, stride=tile), :] for j in range(2)]
            out[...] = jnp.concatenate(both, axis=0).astype(BF16)

    out = jax.ShapeDtypeStruct((2 * nvar, cols), BF16)
    return pl.pallas_call(
        kernel,
        out_shape=(out, out),
        in_specs=[pl.BlockSpec(memory_space=pltpu.HBM)],
        scratch_shapes=[
            pltpu.VMEM((2, nvar, tile, cols), BF16),
            pltpu.VMEM((nvar * tile, cols), F32),
            pltpu.SemaphoreType.DMA((2,)),
        ],
        compiler_params=pltpu.CompilerParams(vmem_limit_bytes=SMALL),
        name="edge_rows",
    )(pltpu.with_memory_space_constraint(x, pltpu.HBM))


def spread_kernel(x_hbm, taps_ref, own_ref, x_ref, stage, xf, sems):
    nvar, rows, cols = x_ref.shape
    block = 3 * nvar + PAD
    wanted = (0, 1, cols - 2, cols - 1)
    k = lax.broadcasted_iota(jnp.int32, (8, cols), 0)
    lane = lanes_of((8, cols))
    pick = jnp.zeros((8, cols), F32)
    for i, c in enumerate(wanted):
        pick = jnp.where((k == i) & (lane == c), 1.0, pick)
    pick = pick.astype(BF16)
    per = cols // rows
    parts = sems.shape[0]
    each = nvar // parts
    copies = []
    for i in range(parts):
        part = slice(i * each, (i + 1) * each)
        copies.append(pltpu.make_async_copy(x_hbm.at[part], x_ref.at[part], sems.at[i]))
        copies[i].start()
    for v in range(nvar):
        if v % each == 0:
            copies[v // each].wait()
        column = x_ref[v].astype(F32)
        for r in range(0, rows, 8):
            xf[pl.ds(r * nvar + v, 8, stride=nvar), :] = column[r : r + 8]
    flat = x_ref[...].reshape(nvar * rows, cols)
    taken = lax.dot_general(pick, flat, (((1,), (1,)), ((), ())), preferred_element_type=F32)
    for v in range(nvar):
        part = taken[:, (v // per) * cols : (v // per + 1) * cols]
        shift = (2 - (v % per) * rows) % cols
        stage[8 * v : 8 * v + 8, :] = pltpu.roll(part, shift, 1)
    for i in range(len(wanted)):
        own_ref[i * nvar : (i + 1) * nvar, :] = stage[pl.ds(i, nvar, stride=8), :]
    ones = jnp.ones((PAD, cols), F32)

    def fill(r, carry):
        row = xf[pl.ds(pl.multiple_of(r * nvar, 8), nvar), :]
        tap = jnp.concatenate([row, pltpu.roll(row, 1, 1), pltpu.roll(row, cols - 1, 1), ones], axis=0)
        at = pl.multiple_of(r * block, 16)
        taps_ref[pl.ds(at, block), :] = tap.astype(BF16)
        return carry

    lax.fori_loop(0, rows, fill, 0, unroll=4)


def spread(x):
    nvar, rows, cols = x.shape
    block = 3 * nvar + PAD
    return pl.pallas_call(
        spread_kernel,
        out_shape=(
            jax.ShapeDtypeStruct((rows * block, cols), BF16),
            jax.ShapeDtypeStruct((4 * nvar, cols), F32),
        ),
        in_specs=[pl.BlockSpec(memory_space=pltpu.HBM)],
        scratch_shapes=[
            pltpu.VMEM((nvar, rows, cols), BF16),
            pltpu.VMEM((8 * nvar, cols), F32),
            pltpu.VMEM((nvar * rows, cols), F32),
            pltpu.SemaphoreType.DMA((most_of(nvar, 4),)),
        ],
        compiler_params=pltpu.CompilerParams(vmem_limit_bytes=SMALL),
        cost_estimate=pl.CostEstimate(flops=10**8, bytes_accessed=4 * 10**6, transcendentals=0),
        name="spread",
    )(pltpu.with_memory_space_constraint(x, pltpu.HBM))


def edge_columns(own, north, south, rows):
    nvar, cols = own.shape[0] // 4, own.shape[1]
    wanted = (0, 1, cols - 2, cols - 1)

    def kernel(own_ref, north_ref, south_ref, left_ref, right_ref):
        lane = lanes_of((nvar, cols))
        halo = []
        for ref, first in ((north_ref, 0), (south_ref, rows + 2)):
            for i in range(2):
                halo.append((first + i, ref[i * nvar : (i + 1) * nvar, :].astype(F32)))
        outs = []
        for i, c in enumerate(wanted):
            column = own_ref[i * nvar : (i + 1) * nvar, :]
            column = jnp.where(lane < rows + 2, column, 0.0)
            for at, row in halo:
                column = jnp.where(lane == at, pltpu.roll(row, (at - c) % cols, 1), column)
            outs.append(column)
        left_ref[...] = jnp.concatenate(outs[:2], axis=0).astype(BF16)
        right_ref[...] = jnp.concatenate(outs[2:], axis=0).astype(BF16)

    out = jax.ShapeDtypeStruct((2 * nvar, cols), BF16)
    return pl.pallas_call(
        kernel,
        out_shape=(out, out),
        compiler_params=pltpu.CompilerParams(vmem_limit_bytes=SMALL),
        name="edge_columns",
    )(own, north, south)


def gelu2(pre):
    pre = pre.astype(BF16)
    inner = pre * (jnp.asarray(GELU_A, BF16) + jnp.asarray(GELU_B, BF16) * (pre * pre))
    return pre + pre * jnp.tanh(inner)


def forecast_kernel(
    spot_ref,
    taps_ref,
    north_ref,
    south_ref,
    own_left_ref,
    own_right_ref,
    from_left_ref,
    from_right_ref,
    conv_ref,
    out_w_ref,
    chosen_ref,
    extra_ref,
    forecast_ref,
    notes_ref,
    first,
    second,
    final,
    hidden,
    seen,
):
    nvar, cols = north_ref.shape[0] // 2, north_ref.shape[1]
    block = 3 * nvar + PAD
    rows = taps_ref.shape[0] // block
    deep = 3 * block
    lane = lanes_of((nvar, cols))
    ones = jnp.ones((PAD, cols), F32)

    def tap_rows(row, west, east, at):
        left = jnp.where(lane == 0, pltpu.roll(west, (cols - at) % cols, 1), pltpu.roll(row, 1, 1))
        right = jnp.where(
            lane == cols - 1, pltpu.roll(east, (2 * cols - 1 - at) % cols, 1), pltpu.roll(row, cols - 1, 1)
        )
        return jnp.concatenate([row, left, right, ones], axis=0).astype(BF16)

    def hidden_of(patches):
        return gelu2(jnp.dot(conv_ref[...], patches, preferred_element_type=F32))

    def moved(centre, hidden):
        change = jnp.dot(out_w_ref[...], hidden, preferred_element_type=F32)
        return (centre + change).astype(BF16).astype(F32)

    from_left = from_left_ref[...].astype(F32)
    from_right = from_right_ref[...].astype(F32)
    own_left = own_left_ref[...].astype(F32)
    own_right = own_right_ref[...].astype(F32)
    far_west, west = from_left[:nvar], from_left[nvar:]
    east, far_east = from_right[:nvar], from_right[nvar:]
    inner_west, inner_east = own_left[:nvar], own_right[nvar:]

    for ref, start in ((north_ref, 0), (south_ref, rows + 2)):
        for i in range(2):
            row = ref[i * nvar : (i + 1) * nvar, :].astype(F32)
            first[(start + i) * block : (start + i + 1) * block, :] = tap_rows(row, west, east, start + i)

    group = lax.broadcasted_iota(jnp.int32, (block, cols), 0)
    wide = lanes_of((block, cols))
    is_left = (group >= nvar) & (group < 2 * nvar) & (wide == 0)
    is_right = (group >= 2 * nvar) & (group < 3 * nvar) & (wide == cols - 1)
    fix = jnp.where(is_left | is_right, 1.0, 0.0).astype(BF16) > 0
    nothing = jnp.zeros((nvar, cols), F32)
    source = jnp.concatenate([nothing, west, pltpu.roll(east, cols - 1, 1), jnp.zeros((PAD, cols), F32)], axis=0)
    source = source.astype(BF16)

    def fill(r, carry):
        at = pl.multiple_of(r * block, 16)
        mine = pltpu.roll(source, cols - 2 - r, 1)
        to = pl.multiple_of((r + 2) * block, 16)
        first[pl.ds(to, block), :] = jnp.where(fix, mine, taps_ref[pl.ds(at, block), :])
        return carry

    lax.fori_loop(0, rows, fill, 0, unroll=4)

    sides = []
    for mid, low, high in ((west, far_west, inner_west), (east, inner_east, far_east)):
        stack = []
        for a in range(3):
            for entry in (mid, low, high):
                stack.append(pltpu.roll(entry, (1 - a) % cols, 1) if a != 1 else entry)
            stack.append(ones)
        sides.append(jnp.concatenate(stack, axis=0).astype(BF16))
    patches = jnp.concatenate(sides, axis=1)
    beside = moved(jnp.concatenate([west, east], axis=1), hidden_of(patches))
    here = lax.axis_index("lat")
    north_in = (here > 0).astype(jnp.int32)
    south_in = (here < lax.axis_size("lat") - 1).astype(jnp.int32)
    keep = jnp.where(lane == 1, north_in, jnp.where(lane == rows + 2, south_in, 1)) > 0
    mid_west = jnp.where(keep, beside[:, :cols], 0.0)
    mid_east = jnp.where(keep, beside[:, cols:], 0.0)

    def ahead(source, at, slot):
        at = pl.multiple_of(at * block, 16)
        patches = jnp.concatenate(
            [source[pl.ds(at, deep), :], source[pl.ds(at + block, deep), :]], axis=1
        )
        hidden[slot] = hidden_of(patches)

    def finish(source, at, slot):
        at = pl.multiple_of(at * block, 16)
        centre = jnp.concatenate(
            [source[pl.ds(at + block, nvar), :], source[pl.ds(at + 2 * block, nvar), :]], axis=1
        ).astype(F32)
        return moved(centre, hidden[slot])

    def first_step(g, carry):
        for q in range(group1):
            ahead(first, 2 * (g * group1 + q), q)
        for q in range(group1):
            i = g * group1 + q
            both = finish(first, 2 * i, q)
            for half in range(2):
                m = 2 * i + half
                good = (jnp.where(m == 0, north_in, 1) * jnp.where(m == rows + 1, south_in, 1)) > 0
                row = both[:, half * cols : (half + 1) * cols]
                row = jnp.where(good, row, 0.0)
                at = pl.multiple_of(m * block, 16)
                second[pl.ds(at, block), :] = tap_rows(row, mid_west, mid_east, m + 1)
        return carry

    group1 = most_of(rows // 2 + 1, hidden.shape[0])
    lax.fori_loop(0, (rows // 2 + 1) // group1, first_step, 0)

    def second_step(g, carry):
        for q in range(group2):
            ahead(second, 2 * (g * group2 + q), q)
        for q in range(group2):
            j = g * group2 + q
            both = finish(second, 2 * j, q)
            both = jnp.concatenate([both[:, :cols], both[:, cols:]], axis=0)
            at = pl.multiple_of(j * 2 * nvar, 16)
            final[pl.ds(at, 2 * nvar), :] = both
            forecast_ref[pl.ds(at, 2 * nvar), :] = both.astype(BF16)
        return carry

    group2 = most_of(rows // 2, hidden.shape[0])
    lax.fori_loop(0, (rows // 2) // group2, second_step, 0)

    for half in range(spot_ref.shape[0]):

        def look(o, carry, half=half):
            seen[pl.ds(half * cols + o, 1), :] = final[pl.ds(spot_ref[half, o], 1), :]
            return carry

        lax.fori_loop(0, cols, look, 0, unroll=32)
    masked = seen[...].astype(BF16) * chosen_ref[...]
    values = lax.dot_general(
        jnp.ones((8, cols), BF16), masked, (((1,), (1,)), ((), ())), preferred_element_type=F32
    )
    fold = extra_ref.shape[0]
    note = [values[0:1, i * cols : (i + 1) * cols] for i in range(fold)] + [extra_ref[...]]
    note = jnp.concatenate(note, axis=0).astype(BF16)
    for d in range(notes_ref.shape[0]):
        notes_ref[d] = note


def run_forecast(spot, taps, north, south, own_left, own_right, from_left, from_right, conv, out_w, chosen, extra, devices):
    nvar, cols = north.shape[0] // 2, north.shape[1]
    slots = spot.shape[0] * spot.shape[1]
    block = 3 * nvar + PAD
    rows = taps.shape[0] // block
    smem = pl.BlockSpec(memory_space=pltpu.SMEM)
    vmem = pl.BlockSpec(memory_space=pltpu.VMEM)
    return pl.pallas_call(
        forecast_kernel,
        out_shape=(
            jax.ShapeDtypeStruct((rows * nvar, cols), BF16),
            jax.ShapeDtypeStruct((devices, 2 * extra.shape[0], cols), BF16),
        ),
        in_specs=[smem] + [vmem] * 11,
        out_specs=(vmem, vmem),
        scratch_shapes=[
            pltpu.VMEM(((rows + 4) * block, cols), BF16),
            pltpu.VMEM(((rows + 2) * block, cols), BF16),
            pltpu.VMEM((rows * nvar, cols), F32),
            pltpu.VMEM((GROUP, conv.shape[0], 2 * cols), BF16),
            pltpu.VMEM((slots, cols), F32),
        ],
        compiler_params=pltpu.CompilerParams(vmem_limit_bytes=16 << 20),
        name="forecast",
    )(spot, taps, north, south, own_left, own_right, from_left, from_right, conv, out_w, chosen, extra)


def pair_weights(gram, proj):
    count = len(proj)
    system = [[gram[k][m] + (float(count - 1) if k == m else 0.0) for m in range(count)] for k in range(count)]
    total = sum(entry * entry for line in system for entry in line)
    scale = jnp.sqrt(total)
    one = jnp.ones_like(scale)
    eye = [[one if k == m else 0.0 * one for m in range(count)] for k in range(count)]

    def times(left, right):
        return [
            [sum(left[k][j] * right[j][m] for j in range(count)) for m in range(count)] for k in range(count)
        ]

    current = [[entry / scale for entry in line] for line in system]
    inverse = eye
    for turn in range(NS_ITERS):
        both = times(inverse, current)
        factor = [[1.5 * eye[k][m] - 0.5 * both[k][m] for m in range(count)] for k in range(count)]
        current = times(current, factor)
        inverse = times(factor, inverse)
    root = jnp.sqrt(scale)
    root_inv = [[entry / root for entry in line] for line in inverse]
    half = [sum(root_inv[k][j] * proj[j] for j in range(count)) for k in range(count)]
    mean_w = [sum(root_inv[k][j] * half[j] for j in range(count)) for k in range(count)]
    span = math.sqrt(count - 1.0)
    full = [[mean_w[k] + span * root_inv[k][m] for m in range(count)] for k in range(count)]
    centre = [sum(full[k][m] for k in range(count)) / count for m in range(count)]
    return [[1.0 / count + full[k][m] - centre[m] for m in range(count)] for k in range(count)]


def analysis_kernel(told_ref, mine_ref, other_ref, out_ref, blended, packed, sems):
    count = lax.axis_size("ens")
    nvar, rows, cols = packed.shape[1], out_ref.shape[1], packed.shape[3]
    depth = told_ref.shape[1]
    told = told_ref[...].astype(F32).reshape(count, -1, cols)
    fold = depth // 2
    size = told.shape[1]
    hx = [told[k] for k in range(count)]
    value = pltpu.roll(told[0], size - fold, 0)
    weight = pltpu.roll(told[1], size - fold, 0)
    used = lax.broadcasted_iota(jnp.int32, (size, cols), 0) % depth < fold
    weight = jnp.where(used, weight, 0.0)
    mean = sum(hx) / count
    spread_of = [h - mean for h in hx]
    innov = value - mean
    tile = (8, cols)

    def total(term):
        return jnp.broadcast_to(jnp.sum(term, keepdims=True), tile)

    scaled = [part * weight for part in spread_of]
    gram = [[None] * count for k in range(count)]
    for k in range(count):
        for m in range(k, count):
            gram[k][m] = gram[m][k] = total(scaled[k] * spread_of[m])
    weights = pair_weights(gram, [total(scaled[k] * innov) for k in range(count)])
    me = lax.axis_index("ens")
    mine = jnp.where(me == 0, weights[0][0], weights[1][1])[0:1, :]
    other = jnp.where(me == 0, weights[1][0], weights[0][1])[0:1, :]
    high = packed.shape[2]

    def copy_of(c):
        return pltpu.make_async_copy(packed.at[c], out_ref.at[:, pl.ds(c * high, high), :], sems.at[c])

    for c in range(rows // high):
        at = c * high * nvar
        part = slice(at, at + high * nvar)
        blended[c] = mine * mine_ref[part, :].astype(F32) + other * other_ref[part, :].astype(F32)
        for v in range(nvar):
            for r in range(0, high, 16):
                halves = [blended[c, pl.ds((r + 8 * i) * nvar + v, 8, stride=nvar), :] for i in range(2)]
                packed[c, v, r : r + 16, :] = jnp.concatenate(halves, axis=0).astype(BF16)
        copy_of(c).start()
    for c in range(rows // high):
        copy_of(c).wait()


def run_analysis(told, mine, other, shape):
    nvar, rows, cols = shape
    high = 16
    vmem = pl.BlockSpec(memory_space=pltpu.VMEM)
    return pl.pallas_call(
        analysis_kernel,
        out_shape=jax.ShapeDtypeStruct(shape, BF16),
        in_specs=[vmem, vmem, vmem],
        out_specs=pl.BlockSpec(memory_space=pltpu.HBM),
        scratch_shapes=[
            pltpu.VMEM((rows // high, high * nvar, cols), F32),
            pltpu.VMEM((rows // high, nvar, high, cols), BF16),
            pltpu.SemaphoreType.DMA((rows // high,)),
        ],
        compiler_params=pltpu.CompilerParams(vmem_limit_bytes=8 << 20),
        name="analysis",
    )(told, mine, other)


def blend_weights(gram, proj):
    entries_number = gram.shape[0]
    eye = jnp.eye(entries_number, dtype=gram.dtype)
    system = (entries_number - 1) * eye + gram
    scale = jnp.sqrt(jnp.sum(system * system))
    current = system / scale
    inverse = eye
    for turn in range(NS_ITERS):
        factor = 1.5 * eye - 0.5 * jnp.dot(inverse, current, precision=lax.Precision.HIGHEST)
        current = jnp.dot(current, factor, precision=lax.Precision.HIGHEST)
        inverse = jnp.dot(factor, inverse, precision=lax.Precision.HIGHEST)
    root_inv = inverse / jnp.sqrt(scale)
    half = jnp.dot(root_inv, proj, precision=lax.Precision.HIGHEST)
    mean_w = jnp.dot(root_inv, half, precision=lax.Precision.HIGHEST)
    full = mean_w[:, None] + math.sqrt(entries_number - 1.0) * root_inv
    return 1.0 / entries_number + full - jnp.mean(full, axis=0, keepdims=True)


def many_members(told, forecast, shape):
    nvar, rows, cols = shape
    fold = told.shape[1] // 2
    told = told.astype(F32).reshape(lax.axis_size("ens"), -1, *told.shape[1:])
    members = told[:, :, :fold, :].reshape(told.shape[0], -1)
    value = told[0, :, fold:, :].reshape(-1)
    weight = told[1, :, fold:, :].reshape(-1)
    mean = jnp.mean(members, axis=0)
    spread = members - mean[None, :]
    innov = value - mean
    weighted = spread * weight[None, :]
    gram = jnp.dot(weighted, spread.T, precision=lax.Precision.HIGHEST)
    proj = jnp.dot(weighted, innov, precision=lax.Precision.HIGHEST)
    transform = blend_weights(gram, proj)
    column = lax.dynamic_slice_in_dim(transform, lax.axis_index("ens"), 1, 1)[:, 0]
    everyone = lax.all_gather(forecast[None], "ens", axis=0, tiled=True)
    blended = jnp.tensordot(column, everyone.astype(F32), axes=1, precision=lax.Precision.HIGHEST)
    return blended.astype(BF16).reshape(rows, nvar, cols).transpose(1, 0, 2)


def prepare(conv_weight, conv_bias, out_weight, index, count, value, weight, shape):
    nvar, rows, cols = shape
    fold = index.shape[0]
    hid = conv_bias.shape[0]
    block = 3 * nvar + PAD

    def kernel(
        count_ref, conv_ref, bias_ref, out_ref, index_ref, value_ref, weight_ref, packed_ref, half_ref, spot_ref, chosen_ref, extra_ref
    ):
        bias = bias_ref[...]
        high = bias.astype(BF16).astype(F32)
        middle = (bias - high).astype(BF16).astype(F32)
        low = (bias - high - middle).astype(BF16).astype(F32)
        rest = jnp.zeros((PAD - 3, hid), F32)
        pieces = []
        for a in range(3):
            for b in (1, 0, 2):
                at = (3 * a + b) * nvar
                pieces.append(conv_ref[at : at + nvar, :].astype(F32))
            if a == 1:
                pieces.append(jnp.concatenate([high, middle, low, rest], axis=0))
            else:
                pieces.append(jnp.zeros((PAD, hid), F32))
        packed_ref[...] = jnp.concatenate(pieces, axis=0).T.astype(BF16)
        half_ref[...] = (out_ref[...].astype(F32) * 0.5).astype(BF16)
        index = index_ref[...]
        row = index // cols % rows
        var = index // (rows * cols)
        spot_ref[...] = jnp.clip(row * nvar + var, 0, rows * nvar - 1)
        lane = (index % cols).astype(F32)
        for i in range(fold):
            across = jnp.broadcast_to(lane[i : i + 1, :], (cols, cols)).T
            hot = across == lanes_of((cols, cols)).astype(F32)
            chosen_ref[i * cols : (i + 1) * cols, :] = jnp.where(hot, 1.0, 0.0).astype(BF16)
        slot = lanes_of((fold, cols)) + cols * lax.broadcasted_iota(jnp.int32, (fold, cols), 0)
        live = jnp.where(slot < count_ref[0, 0], weight_ref[...], 0.0)
        member = lax.axis_index("ens")
        extra_ref[...] = jnp.where(member == 0, value_ref[...], jnp.where(member == 1, live, 0.0))

    return pl.pallas_call(
        kernel,
        out_shape=(
            jax.ShapeDtypeStruct((hid, 3 * block), BF16),
            jax.ShapeDtypeStruct((nvar, hid), BF16),
            jax.ShapeDtypeStruct((fold, cols), jnp.int32),
            jax.ShapeDtypeStruct((fold * cols, cols), BF16),
            jax.ShapeDtypeStruct((fold, cols), F32),
        ),
        in_specs=[pl.BlockSpec(memory_space=pltpu.SMEM)] + [pl.BlockSpec(memory_space=pltpu.VMEM)] * 6,
        compiler_params=pltpu.CompilerParams(vmem_limit_bytes=SMALL),
        cost_estimate=pl.CostEstimate(flops=10**7, bytes_accessed=10**6, transcendentals=0),
        name="prepare",
    )(
        count,
        *(
            pltpu.with_memory_space_constraint(entry, pltpu.HBM)
            for entry in (conv_weight, conv_bias[None], out_weight.T, index, value, weight)
        ),
    )


def per_device(
    sample_quantities,
    conv_weight,
    conv_bias,
    out_weight,
    obs_index,
    obs_count,
    obs_value,
    obs_weight,
):
    x = sample_quantities[0]
    nvar, rows, cols = x.shape
    n_ens, n_lat, n_lon = (lax.axis_size(axis) for axis in ("ens", "lat", "lon"))
    down_lat = [(i, i + 1) for i in range(n_lat - 1)]
    up_lat = [(j, i) for i, j in down_lat]
    right_lon = [(i, (i + 1) % n_lon) for i in range(n_lon)]
    left_lon = [(j, i) for i, j in right_lon]

    first_rows, last_rows = edge_rows(x)
    north = lax.ppermute(last_rows, "lat", down_lat)
    south = lax.ppermute(first_rows, "lat", up_lat)
    taps, own = spread(x)
    own_left, own_right = edge_columns(own, north, south, rows)
    from_left = lax.ppermute(own_right, "lon", right_lon)
    from_right = lax.ppermute(own_left, "lon", left_lon)

    fold = (obs_index.size // cols, cols)
    index, own_left, own_right = lax.optimization_barrier((obs_index, own_left, own_right))
    conv, out_w, spot, chosen, extra = prepare(
        conv_weight,
        conv_bias,
        out_weight,
        index.reshape(fold),
        obs_count,
        obs_value.reshape(fold),
        obs_weight.reshape(fold),
        x.shape,
    )
    forecast, notes = run_forecast(
        spot,
        taps,
        north,
        south,
        own_left,
        own_right,
        from_left,
        from_right,
        conv,
        out_w,
        chosen,
        extra,
        n_ens * n_lat * n_lon,
    )
    told = lax.all_to_all(notes, ("ens", "lat", "lon"), 0, 0, tiled=True)
    if n_ens == 2:
        other = lax.ppermute(forecast, "ens", [(0, 1), (1, 0)])
        return run_analysis(told, forecast, other, x.shape)[None]
    return many_members(told, forecast, x.shape)[None]


def solution(mesh):
    return jax.shard_map(
        per_device,
        mesh=mesh,
        in_specs=(
            P("ens", None, "lat", "lon"),
            P(),
            P(),
            P(),
            P("lat", "lon", None),
            P("lat", "lon"),
            P("lat", "lon", None),
            P("lat", "lon", None),
        ),
        out_specs=P("ens", None, "lat", "lon"),
        check_vma=False,
    )
```

```python
import functools
import math

import jax
import jax.numpy as jnp
from jax import lax
from jax.experimental import pallas as pl
from jax.experimental.pallas import tpu as pltpu
from jax.sharding import PartitionSpec as P

NS_ITERS = 20
GELU_A = math.sqrt(2.0 / math.pi)
GELU_B = GELU_A * 0.044715
F32 = jnp.float32
BF16 = jnp.bfloat16
PAD = 8
SMALL = 4 << 20
GROUP = 34


def lanes_of(shape):
    return lax.broadcasted_iota(jnp.int32, shape, len(shape) - 1)


def most_of(total, limit):
    return max(d for d in range(1, limit + 1) if total % d == 0)


def edge_rows(x):
    nvar, rows, cols = x.shape
    tile = 16

    def kernel(x_ref, up_ref, down_ref, part, stage, sems):
        copies = []
        for i, first in enumerate((0, rows - tile)):
            copies.append(pltpu.make_async_copy(x_ref.at[:, first : first + tile, :], part.at[i], sems.at[i]))
            copies[i].start()
        for i, (out, first) in enumerate(((up_ref, 0), (down_ref, tile - 2))):
            copies[i].wait()
            stage[...] = part[i].reshape(nvar * tile, cols).astype(F32)
            both = [stage[pl.ds(first + j, nvar, stride=tile), :] for j in range(2)]
            out[...] = jnp.concatenate(both, axis=0).astype(BF16)

    out = jax.ShapeDtypeStruct((2 * nvar, cols), BF16)
    return pl.pallas_call(
        kernel,
        out_shape=(out, out),
        in_specs=[pl.BlockSpec(memory_space=pltpu.HBM)],
        scratch_shapes=[
            pltpu.VMEM((2, nvar, tile, cols), BF16),
            pltpu.VMEM((nvar * tile, cols), F32),
            pltpu.SemaphoreType.DMA((2,)),
        ],
        compiler_params=pltpu.CompilerParams(vmem_limit_bytes=SMALL),
        name="edge_rows",
    )(pltpu.with_memory_space_constraint(x, pltpu.HBM))


def packed_rows(conv, bias, nvar):
    hid = bias.shape[1]
    high = bias.astype(BF16).astype(F32)
    middle = (bias - high).astype(BF16).astype(F32)
    low = (bias - high - middle).astype(BF16).astype(F32)
    rest = jnp.zeros((PAD - 3, hid), F32)
    pieces = []
    for a in range(3):
        for b in (1, 0, 2):
            at = (3 * a + b) * nvar
            pieces.append(conv[at : at + nvar, :].astype(F32))
        if a == 1:
            pieces.append(jnp.concatenate([high, middle, low, rest], axis=0))
        else:
            pieces.append(jnp.zeros((PAD, hid), F32))
    return jnp.concatenate(pieces, axis=0).T


def spread_kernel(
    x_hbm,
    conv_hbm,
    bias_hbm,
    out_hbm,
    index_hbm,
    count_ref,
    value_hbm,
    weight_hbm,
    taps_ref,
    own_ref,
    packed_ref,
    half_ref,
    extra_ref,
    chosen_ref,
    *rest,
):
    fold = extra_ref.shape[0]
    spot_refs = rest[:fold]
    x_ref, conv_ref, bias_ref, out_ref, index_ref, value_ref, weight_ref, stage, xf, sems = rest[fold:]
    nvar, rows, cols = x_ref.shape
    block = 3 * nvar + PAD
    small = [
        (conv_hbm, conv_ref),
        (bias_hbm, bias_ref),
        (out_hbm, out_ref),
        (index_hbm, index_ref),
        (value_hbm, value_ref),
        (weight_hbm, weight_ref),
    ]
    parts = sems.shape[0] - len(small)
    each = nvar // parts
    copies = []
    for i in range(parts):
        part = slice(i * each, (i + 1) * each)
        copies.append(pltpu.make_async_copy(x_hbm.at[part], x_ref.at[part], sems.at[i]))
    for i, (source, target) in enumerate(small):
        copies.append(pltpu.make_async_copy(source, target, sems.at[parts + i]))
    for copy in copies:
        copy.start()

    wanted = (0, 1, cols - 2, cols - 1)
    k = lax.broadcasted_iota(jnp.int32, (8, cols), 0)
    lane = lanes_of((8, cols))
    pick = jnp.zeros((8, cols), F32)
    for i, c in enumerate(wanted):
        pick = jnp.where((k == i) & (lane == c), 1.0, pick)
    pick = pick.astype(BF16)
    per = cols // rows
    for v in range(nvar):
        if v % each == 0:
            copies[v // each].wait()
        column = x_ref[v].astype(F32)
        for r in range(0, rows, 8):
            xf[pl.ds(r * nvar + v, 8, stride=nvar), :] = column[r : r + 8]
    flat = x_ref[...].reshape(nvar * rows, cols)
    taken = lax.dot_general(pick, flat, (((1,), (1,)), ((), ())), preferred_element_type=F32)
    for v in range(nvar):
        part = taken[:, (v // per) * cols : (v // per + 1) * cols]
        shift = (2 - (v % per) * rows) % cols
        stage[8 * v : 8 * v + 8, :] = pltpu.roll(part, shift, 1)
    for i in range(len(wanted)):
        own_ref[i * nvar : (i + 1) * nvar, :] = stage[pl.ds(i, nvar, stride=8), :]
    ones = jnp.ones((PAD, cols), F32)

    def fill(r, carry):
        row = xf[pl.ds(pl.multiple_of(r * nvar, 8), nvar), :]
        tap = jnp.concatenate([row, pltpu.roll(row, 1, 1), pltpu.roll(row, cols - 1, 1), ones], axis=0)
        at = pl.multiple_of(r * block, 16)
        taps_ref[pl.ds(at, block), :] = tap.astype(BF16)
        return carry

    lax.fori_loop(0, rows, fill, 0, unroll=8)

    for copy in copies[parts:]:
        copy.wait()
    packed_ref[...] = packed_rows(conv_ref[...], bias_ref[...], nvar).astype(BF16)
    half_ref[...] = (out_ref[...].astype(F32) * 0.5).astype(BF16)
    index = index_ref[...]
    row = index // cols % rows
    var = index // (rows * cols)
    spot = jnp.clip(row * nvar + var, 0, rows * nvar - 1)
    place = (index % cols).astype(F32)
    for i in range(fold):
        spot_refs[i][...] = spot[i : i + 1, :]
        across = jnp.broadcast_to(place[i : i + 1, :], (cols, cols)).T
        hot = across == lanes_of((cols, cols)).astype(F32)
        chosen_ref[i * cols : (i + 1) * cols, :] = jnp.where(hot, 1.0, 0.0).astype(BF16)
    slot = lanes_of((fold, cols)) + cols * lax.broadcasted_iota(jnp.int32, (fold, cols), 0)
    live = jnp.where(slot < count_ref[0, 0], weight_ref[...], 0.0)
    member = lax.axis_index("ens")
    extra_ref[...] = jnp.where(member == 0, value_ref[...], jnp.where(member == 1, live, 0.0))


def spread(x, conv_weight, conv_bias, out_weight, index, count, value, weight):
    nvar, rows, cols = x.shape
    fold, hid = index.shape[0], conv_bias.shape[0]
    block = 3 * nvar + PAD
    args = (x, conv_weight, conv_bias[None], out_weight.T, index, count, value, weight)
    shape = jax.ShapeDtypeStruct
    scratch = [pltpu.VMEM(arg.shape, arg.dtype) for arg in args]
    del scratch[5]
    in_specs = [pl.BlockSpec(memory_space=pltpu.HBM)] * len(args)
    in_specs[5] = pl.BlockSpec(memory_space=pltpu.SMEM)
    placed = [pltpu.with_memory_space_constraint(arg, pltpu.HBM) for arg in args]
    placed[5] = count
    return pl.pallas_call(
        spread_kernel,
        out_shape=(
            shape((rows * block, cols), BF16),
            shape((4 * nvar, cols), F32),
            shape((hid, 3 * block), BF16),
            shape((nvar, hid), BF16),
            shape((fold, cols), F32),
            shape((fold * cols, cols), BF16),
        )
        + (shape((1, cols), jnp.int32),) * fold,
        in_specs=in_specs,
        scratch_shapes=scratch
        + [
            pltpu.VMEM((8 * nvar, cols), F32),
            pltpu.VMEM((nvar * rows, cols), F32),
            pltpu.SemaphoreType.DMA((most_of(nvar, 4) + len(args) - 2,)),
        ],
        compiler_params=pltpu.CompilerParams(vmem_limit_bytes=SMALL),
        cost_estimate=pl.CostEstimate(flops=10**8, bytes_accessed=4 * 10**6, transcendentals=0),
        name="spread",
    )(*placed)


def edge_columns(own, north, south, rows):
    nvar, cols = own.shape[0] // 4, own.shape[1]
    wanted = (0, 1, cols - 2, cols - 1)

    def kernel(own_ref, north_ref, south_ref, left_ref, right_ref):
        lane = lanes_of((nvar, cols))
        halo = []
        for ref, first in ((north_ref, 0), (south_ref, rows + 2)):
            for i in range(2):
                halo.append((first + i, ref[i * nvar : (i + 1) * nvar, :].astype(F32)))
        outs = []
        for i, c in enumerate(wanted):
            column = own_ref[i * nvar : (i + 1) * nvar, :]
            column = jnp.where(lane < rows + 2, column, 0.0)
            for at, row in halo:
                column = jnp.where(lane == at, pltpu.roll(row, (at - c) % cols, 1), column)
            outs.append(column)
        left_ref[...] = jnp.concatenate(outs[:2], axis=0).astype(BF16)
        right_ref[...] = jnp.concatenate(outs[2:], axis=0).astype(BF16)

    out = jax.ShapeDtypeStruct((2 * nvar, cols), BF16)
    return pl.pallas_call(
        kernel,
        out_shape=(out, out),
        compiler_params=pltpu.CompilerParams(vmem_limit_bytes=SMALL),
        name="edge_columns",
    )(own, north, south)


def gelu2(pre):
    pre = pre.astype(BF16)
    inner = pre * (jnp.asarray(GELU_A, BF16) + jnp.asarray(GELU_B, BF16) * (pre * pre))
    return pre + pre * jnp.tanh(inner)


def forecast_kernel(
    fold,
    *refs,
):
    spot_refs = refs[:fold]
    (
    taps_ref,
    north_ref,
    south_ref,
    own_left_ref,
    own_right_ref,
    from_left_ref,
    from_right_ref,
    conv_ref,
    out_w_ref,
    chosen_ref,
    extra_ref,
    forecast_ref,
    notes_ref,
    first,
    second,
    final,
    hidden,
    seen,
    conv,
    out_w,
    ) = refs[fold:]
    nvar, cols = north_ref.shape[0] // 2, north_ref.shape[1]
    block = 3 * nvar + PAD
    rows = taps_ref.shape[0] // block
    deep = 3 * block
    lane = lanes_of((nvar, cols))
    ones = jnp.ones((PAD, cols), F32)

    def tap_rows(row, west, east, at):
        left = jnp.where(lane == 0, pltpu.roll(west, (cols - at) % cols, 1), pltpu.roll(row, 1, 1))
        right = jnp.where(
            lane == cols - 1, pltpu.roll(east, (2 * cols - 1 - at) % cols, 1), pltpu.roll(row, cols - 1, 1)
        )
        return jnp.concatenate([row, left, right, ones], axis=0).astype(BF16)

    def hidden_of(patches):
        return gelu2(jnp.dot(conv[...], patches, preferred_element_type=F32))

    def moved(centre, hidden):
        change = jnp.dot(out_w[...], hidden, preferred_element_type=F32)
        return (centre + change).astype(BF16).astype(F32)

    conv[...] = conv_ref[...]
    out_w[...] = out_w_ref[...]
    from_left = from_left_ref[...].astype(F32)
    from_right = from_right_ref[...].astype(F32)
    own_left = own_left_ref[...].astype(F32)
    own_right = own_right_ref[...].astype(F32)
    far_west, west = from_left[:nvar], from_left[nvar:]
    east, far_east = from_right[:nvar], from_right[nvar:]
    inner_west, inner_east = own_left[:nvar], own_right[nvar:]

    for ref, start in ((north_ref, 0), (south_ref, rows + 2)):
        for i in range(2):
            row = ref[i * nvar : (i + 1) * nvar, :].astype(F32)
            first[(start + i) * block : (start + i + 1) * block, :] = tap_rows(row, west, east, start + i)

    group = lax.broadcasted_iota(jnp.int32, (block, cols), 0)
    wide = lanes_of((block, cols))
    is_left = (group >= nvar) & (group < 2 * nvar) & (wide == 0)
    is_right = (group >= 2 * nvar) & (group < 3 * nvar) & (wide == cols - 1)
    fix = jnp.where(is_left | is_right, 1.0, 0.0).astype(BF16) > 0
    nothing = jnp.zeros((nvar, cols), F32)
    source = jnp.concatenate([nothing, west, pltpu.roll(east, cols - 1, 1), jnp.zeros((PAD, cols), F32)], axis=0)
    source = source.astype(BF16)

    def fill(r, carry):
        at = pl.multiple_of(r * block, 16)
        mine = pltpu.roll(source, cols - 2 - r, 1)
        to = pl.multiple_of((r + 2) * block, 16)
        first[pl.ds(to, block), :] = jnp.where(fix, mine, taps_ref[pl.ds(at, block), :])
        return carry

    lax.fori_loop(0, rows, fill, 0, unroll=4)

    sides = []
    for mid, low, high in ((west, far_west, inner_west), (east, inner_east, far_east)):
        stack = []
        for a in range(3):
            for entry in (mid, low, high):
                stack.append(pltpu.roll(entry, (1 - a) % cols, 1) if a != 1 else entry)
            stack.append(ones)
        sides.append(jnp.concatenate(stack, axis=0).astype(BF16))
    patches = jnp.concatenate(sides, axis=1)
    beside = moved(jnp.concatenate([west, east], axis=1), hidden_of(patches))
    here = lax.axis_index("lat")
    north_in = (here > 0).astype(jnp.int32)
    south_in = (here < lax.axis_size("lat") - 1).astype(jnp.int32)
    keep = jnp.where(lane == 1, north_in, jnp.where(lane == rows + 2, south_in, 1)) > 0
    mid_west = jnp.where(keep, beside[:, :cols], 0.0)
    mid_east = jnp.where(keep, beside[:, cols:], 0.0)

    def ahead(source, at, slot):
        at = pl.multiple_of(at * block, 16)
        patches = jnp.concatenate(
            [source[pl.ds(at, deep), :], source[pl.ds(at + block, deep), :]], axis=1
        )
        hidden[slot] = hidden_of(patches)

    def finish(source, at, slot):
        at = pl.multiple_of(at * block, 16)
        centre = jnp.concatenate(
            [source[pl.ds(at + block, nvar), :], source[pl.ds(at + 2 * block, nvar), :]], axis=1
        ).astype(F32)
        return moved(centre, hidden[slot])

    def first_step(g, carry):
        for q in range(group1):
            ahead(first, 2 * (g * group1 + q), q)
        for q in range(group1):
            i = g * group1 + q
            both = finish(first, 2 * i, q)
            for half in range(2):
                m = 2 * i + half
                good = (jnp.where(m == 0, north_in, 1) * jnp.where(m == rows + 1, south_in, 1)) > 0
                row = both[:, half * cols : (half + 1) * cols]
                row = jnp.where(good, row, 0.0)
                at = pl.multiple_of(m * block, 16)
                second[pl.ds(at, block), :] = tap_rows(row, mid_west, mid_east, m + 1)
        return carry

    group1 = most_of(rows // 2 + 1, hidden.shape[0])
    lax.fori_loop(0, (rows // 2 + 1) // group1, first_step, 0)

    def second_step(g, carry):
        for q in range(group2):
            ahead(second, 2 * (g * group2 + q), q)
        for q in range(group2):
            j = g * group2 + q
            both = finish(second, 2 * j, q)
            both = jnp.concatenate([both[:, :cols], both[:, cols:]], axis=0)
            at = pl.multiple_of(j * 2 * nvar, 16)
            final[pl.ds(at, 2 * nvar), :] = both
            forecast_ref[pl.ds(at, 2 * nvar), :] = both.astype(BF16)
        return carry

    group2 = most_of(rows // 2, hidden.shape[0])
    lax.fori_loop(0, (rows // 2) // group2, second_step, 0)

    for half in range(fold):

        def look(o, carry, half=half):
            seen[pl.ds(half * cols + o, 1), :] = final[pl.ds(spot_refs[half][0, o], 1), :]
            return carry

        lax.fori_loop(0, cols, look, 0, unroll=32)
    masked = seen[...].astype(BF16) * chosen_ref[...]
    values = lax.dot_general(
        jnp.ones((8, cols), BF16), masked, (((1,), (1,)), ((), ())), preferred_element_type=F32
    )
    note = [values[0:1, i * cols : (i + 1) * cols] for i in range(fold)] + [extra_ref[...]]
    note = jnp.concatenate(note, axis=0).astype(BF16)
    for d in range(notes_ref.shape[0]):
        notes_ref[d] = note


def run_forecast(spot, taps, north, south, own_left, own_right, from_left, from_right, conv, out_w, chosen, extra, devices):
    nvar, cols = north.shape[0] // 2, north.shape[1]
    slots = len(spot) * cols
    block = 3 * nvar + PAD
    rows = taps.shape[0] // block
    smem = pl.BlockSpec(memory_space=pltpu.SMEM)
    vmem = pl.BlockSpec(memory_space=pltpu.VMEM)
    return pl.pallas_call(
        functools.partial(forecast_kernel, len(spot)),
        out_shape=(
            jax.ShapeDtypeStruct((rows * nvar, cols), BF16),
            jax.ShapeDtypeStruct((devices, 2 * extra.shape[0], cols), BF16),
        ),
        in_specs=[smem] * len(spot) + [vmem] * 11,
        out_specs=(vmem, vmem),
        scratch_shapes=[
            pltpu.VMEM(((rows + 4) * block, cols), BF16),
            pltpu.VMEM(((rows + 2) * block, cols), BF16),
            pltpu.VMEM((rows * nvar, cols), F32),
            pltpu.VMEM((GROUP, conv.shape[0], 2 * cols), BF16),
            pltpu.VMEM((slots, cols), F32),
            pltpu.VMEM(conv.shape, BF16),
            pltpu.VMEM(out_w.shape, BF16),
        ],
        compiler_params=pltpu.CompilerParams(vmem_limit_bytes=24 << 20),
        name="forecast",
    )(*spot, taps, north, south, own_left, own_right, from_left, from_right, conv, out_w, chosen, extra)


def pair_weights(gram, proj):
    count = len(proj)
    system = [[gram[k][m] + (float(count - 1) if k == m else 0.0) for m in range(count)] for k in range(count)]
    total = sum(entry * entry for line in system for entry in line)
    scale = jnp.sqrt(total)
    one = jnp.ones_like(scale)
    eye = [[one if k == m else 0.0 * one for m in range(count)] for k in range(count)]

    def times(left, right):
        return [
            [sum(left[k][j] * right[j][m] for j in range(count)) for m in range(count)] for k in range(count)
        ]

    current = [[entry / scale for entry in line] for line in system]
    inverse = eye
    for turn in range(NS_ITERS):
        both = times(inverse, current)
        factor = [[1.5 * eye[k][m] - 0.5 * both[k][m] for m in range(count)] for k in range(count)]
        current = times(current, factor)
        inverse = times(factor, inverse)
    root = jnp.sqrt(scale)
    root_inv = [[entry / root for entry in line] for line in inverse]
    half = [sum(root_inv[k][j] * proj[j] for j in range(count)) for k in range(count)]
    mean_w = [sum(root_inv[k][j] * half[j] for j in range(count)) for k in range(count)]
    span = math.sqrt(count - 1.0)
    full = [[mean_w[k] + span * root_inv[k][m] for m in range(count)] for k in range(count)]
    centre = [sum(full[k][m] for k in range(count)) / count for m in range(count)]
    return [[1.0 / count + full[k][m] - centre[m] for m in range(count)] for k in range(count)]


def analysis_kernel(told_ref, mine_ref, other_ref, out_ref, blended, packed, sems):
    count = lax.axis_size("ens")
    nvar, rows, cols = packed.shape[1], out_ref.shape[1], packed.shape[3]
    depth = told_ref.shape[1]
    told = told_ref[...].astype(F32).reshape(count, -1, cols)
    fold = depth // 2
    size = told.shape[1]
    hx = [told[k] for k in range(count)]
    value = pltpu.roll(told[0], size - fold, 0)
    weight = pltpu.roll(told[1], size - fold, 0)
    used = lax.broadcasted_iota(jnp.int32, (size, cols), 0) % depth < fold
    weight = jnp.where(used, weight, 0.0)
    mean = sum(hx) / count
    spread_of = [h - mean for h in hx]
    innov = value - mean
    tile = (8, cols)

    def total(term):
        return jnp.broadcast_to(jnp.sum(term, keepdims=True), tile)

    scaled = [part * weight for part in spread_of]
    gram = [[None] * count for k in range(count)]
    for k in range(count):
        for m in range(k, count):
            gram[k][m] = gram[m][k] = total(scaled[k] * spread_of[m])
    weights = pair_weights(gram, [total(scaled[k] * innov) for k in range(count)])
    me = lax.axis_index("ens")
    mine = jnp.where(me == 0, weights[0][0], weights[1][1])[0:1, :]
    other = jnp.where(me == 0, weights[1][0], weights[0][1])[0:1, :]
    high = packed.shape[2]

    def copy_of(c):
        return pltpu.make_async_copy(packed.at[c], out_ref.at[:, pl.ds(c * high, high), :], sems.at[c])

    for c in range(rows // high):
        at = c * high * nvar
        part = slice(at, at + high * nvar)
        blended[c] = mine * mine_ref[part, :].astype(F32) + other * other_ref[part, :].astype(F32)
        for v in range(nvar):
            for r in range(0, high, 16):
                halves = [blended[c, pl.ds((r + 8 * i) * nvar + v, 8, stride=nvar), :] for i in range(2)]
                packed[c, v, r : r + 16, :] = jnp.concatenate(halves, axis=0).astype(BF16)
        copy_of(c).start()
    for c in range(rows // high):
        copy_of(c).wait()


def run_analysis(told, mine, other, shape):
    nvar, rows, cols = shape
    high = 16
    vmem = pl.BlockSpec(memory_space=pltpu.VMEM)
    return pl.pallas_call(
        analysis_kernel,
        out_shape=jax.ShapeDtypeStruct(shape, BF16),
        in_specs=[vmem, vmem, vmem],
        out_specs=pl.BlockSpec(memory_space=pltpu.HBM),
        scratch_shapes=[
            pltpu.VMEM((rows // high, high * nvar, cols), F32),
            pltpu.VMEM((rows // high, nvar, high, cols), BF16),
            pltpu.SemaphoreType.DMA((rows // high,)),
        ],
        compiler_params=pltpu.CompilerParams(vmem_limit_bytes=8 << 20),
        name="analysis",
    )(told, mine, other)


def blend_weights(gram, proj):
    entries_number = gram.shape[0]
    eye = jnp.eye(entries_number, dtype=gram.dtype)
    system = (entries_number - 1) * eye + gram
    scale = jnp.sqrt(jnp.sum(system * system))
    current = system / scale
    inverse = eye
    for turn in range(NS_ITERS):
        factor = 1.5 * eye - 0.5 * jnp.dot(inverse, current, precision=lax.Precision.HIGHEST)
        current = jnp.dot(current, factor, precision=lax.Precision.HIGHEST)
        inverse = jnp.dot(factor, inverse, precision=lax.Precision.HIGHEST)
    root_inv = inverse / jnp.sqrt(scale)
    half = jnp.dot(root_inv, proj, precision=lax.Precision.HIGHEST)
    mean_w = jnp.dot(root_inv, half, precision=lax.Precision.HIGHEST)
    full = mean_w[:, None] + math.sqrt(entries_number - 1.0) * root_inv
    return 1.0 / entries_number + full - jnp.mean(full, axis=0, keepdims=True)


def many_members(told, forecast, shape):
    nvar, rows, cols = shape
    fold = told.shape[1] // 2
    told = told.astype(F32).reshape(lax.axis_size("ens"), -1, *told.shape[1:])
    members = told[:, :, :fold, :].reshape(told.shape[0], -1)
    value = told[0, :, fold:, :].reshape(-1)
    weight = told[1, :, fold:, :].reshape(-1)
    mean = jnp.mean(members, axis=0)
    spread = members - mean[None, :]
    innov = value - mean
    weighted = spread * weight[None, :]
    gram = jnp.dot(weighted, spread.T, precision=lax.Precision.HIGHEST)
    proj = jnp.dot(weighted, innov, precision=lax.Precision.HIGHEST)
    transform = blend_weights(gram, proj)
    column = lax.dynamic_slice_in_dim(transform, lax.axis_index("ens"), 1, 1)[:, 0]
    everyone = lax.all_gather(forecast[None], "ens", axis=0, tiled=True)
    blended = jnp.tensordot(column, everyone.astype(F32), axes=1, precision=lax.Precision.HIGHEST)
    return blended.astype(BF16).reshape(rows, nvar, cols).transpose(1, 0, 2)


def per_device(
    sample_quantities,
    conv_weight,
    conv_bias,
    out_weight,
    obs_index,
    obs_count,
    obs_value,
    obs_weight,
):
    x = sample_quantities[0]
    nvar, rows, cols = x.shape
    n_ens, n_lat, n_lon = (lax.axis_size(axis) for axis in ("ens", "lat", "lon"))
    down_lat = [(i, i + 1) for i in range(n_lat - 1)]
    up_lat = [(j, i) for i, j in down_lat]
    right_lon = [(i, (i + 1) % n_lon) for i in range(n_lon)]
    left_lon = [(j, i) for i, j in right_lon]

    first_rows, last_rows = edge_rows(x)
    north = lax.ppermute(last_rows, "lat", down_lat)
    south = lax.ppermute(first_rows, "lat", up_lat)
    fold = (obs_index.size // cols, cols)
    taps, own, conv, out_w, extra, chosen, *spot = spread(
        x,
        conv_weight,
        conv_bias,
        out_weight,
        obs_index.reshape(fold),
        obs_count,
        obs_value.reshape(fold),
        obs_weight.reshape(fold),
    )
    own_left, own_right = edge_columns(own, north, south, rows)
    from_left = lax.ppermute(own_right, "lon", right_lon)
    from_right = lax.ppermute(own_left, "lon", left_lon)

    forecast, notes = run_forecast(
        spot,
        taps,
        north,
        south,
        own_left,
        own_right,
        from_left,
        from_right,
        conv,
        out_w,
        chosen,
        extra,
        n_ens * n_lat * n_lon,
    )
    told = lax.all_to_all(notes, ("ens", "lat", "lon"), 0, 0, tiled=True)
    if n_ens == 2:
        other = lax.ppermute(forecast, "ens", [(0, 1), (1, 0)])
        return run_analysis(told, forecast, other, x.shape)[None]
    return many_members(told, forecast, x.shape)[None]


def solution(mesh):
    return jax.shard_map(
        per_device,
        mesh=mesh,
        in_specs=(
            P("ens", None, "lat", "lon"),
            P(),
            P(),
            P(),
            P("lat", "lon", None),
            P("lat", "lon"),
            P("lat", "lon", None),
            P("lat", "lon", None),
        ),
        out_specs=P("ens", None, "lat", "lon"),
        check_vma=False,
    )
```

```python
import functools
import math

import jax
import jax.numpy as jnp
from jax import lax
from jax.experimental import pallas as pl
from jax.experimental.pallas import tpu as pltpu
from jax.sharding import PartitionSpec as P

NS_ITERS = 20
GELU_A = math.sqrt(2.0 / math.pi)
GELU_B = GELU_A * 0.044715
F32 = jnp.float32
BF16 = jnp.bfloat16
PAD = 8
SMALL = 4 << 20
GROUP = 34


def lanes_of(shape):
    return lax.broadcasted_iota(jnp.int32, shape, len(shape) - 1)


def most_of(total, limit):
    return max(d for d in range(1, limit + 1) if total % d == 0)


def edge_rows(x):
    nvar, rows, cols = x.shape
    tile = 16

    def kernel(x_ref, up_ref, down_ref, part, stage, sems):
        copies = []
        for i, first in enumerate((0, rows - tile)):
            copies.append(pltpu.make_async_copy(x_ref.at[:, first : first + tile, :], part.at[i], sems.at[i]))
            copies[i].start()
        for i, (out, first) in enumerate(((up_ref, 0), (down_ref, tile - 2))):
            copies[i].wait()
            stage[...] = part[i].reshape(nvar * tile, cols).astype(F32)
            both = [stage[pl.ds(first + j, nvar, stride=tile), :] for j in range(2)]
            out[...] = jnp.concatenate(both, axis=0).astype(BF16)

    out = jax.ShapeDtypeStruct((2 * nvar, cols), BF16)
    return pl.pallas_call(
        kernel,
        out_shape=(out, out),
        in_specs=[pl.BlockSpec(memory_space=pltpu.HBM)],
        scratch_shapes=[
            pltpu.VMEM((2, nvar, tile, cols), BF16),
            pltpu.VMEM((nvar * tile, cols), F32),
            pltpu.SemaphoreType.DMA((2,)),
        ],
        compiler_params=pltpu.CompilerParams(vmem_limit_bytes=SMALL),
        name="edge_rows",
    )(pltpu.with_memory_space_constraint(x, pltpu.HBM))


def packed_rows(conv, bias, nvar):
    hid = bias.shape[1]
    high = bias.astype(BF16).astype(F32)
    middle = (bias - high).astype(BF16).astype(F32)
    low = (bias - high - middle).astype(BF16).astype(F32)
    rest = jnp.zeros((PAD - 3, hid), F32)
    pieces = []
    for a in range(3):
        for b in (1, 0, 2):
            at = (3 * a + b) * nvar
            pieces.append(conv[at : at + nvar, :].astype(F32))
        if a == 1:
            pieces.append(jnp.concatenate([high, middle, low, rest], axis=0))
        else:
            pieces.append(jnp.zeros((PAD, hid), F32))
    return jnp.concatenate(pieces, axis=0).T


def spread_kernel(
    x_hbm,
    conv_hbm,
    bias_hbm,
    out_hbm,
    index_hbm,
    count_ref,
    value_hbm,
    weight_hbm,
    taps_ref,
    own_ref,
    packed_ref,
    half_ref,
    extra_ref,
    chosen_ref,
    *rest,
):
    fold = extra_ref.shape[0]
    spot_refs = rest[:fold]
    x_ref, conv_ref, bias_ref, out_ref, index_ref, value_ref, weight_ref, stage, xf, sems = rest[fold:]
    nvar, rows, cols = x_ref.shape
    block = 3 * nvar + PAD
    small = [
        (conv_hbm, conv_ref),
        (bias_hbm, bias_ref),
        (out_hbm, out_ref),
        (index_hbm, index_ref),
        (value_hbm, value_ref),
        (weight_hbm, weight_ref),
    ]
    parts = sems.shape[0] - len(small)
    each = nvar // parts
    copies = []
    for i in range(parts):
        part = slice(i * each, (i + 1) * each)
        copies.append(pltpu.make_async_copy(x_hbm.at[part], x_ref.at[part], sems.at[i]))
    for i, (source, target) in enumerate(small):
        copies.append(pltpu.make_async_copy(source, target, sems.at[parts + i]))
    for copy in copies:
        copy.start()

    wanted = (0, 1, cols - 2, cols - 1)
    k = lax.broadcasted_iota(jnp.int32, (8, cols), 0)
    lane = lanes_of((8, cols))
    pick = jnp.zeros((8, cols), F32)
    for i, c in enumerate(wanted):
        pick = jnp.where((k == i) & (lane == c), 1.0, pick)
    pick = pick.astype(BF16)
    per = cols // rows
    for v in range(nvar):
        if v % each == 0:
            copies[v // each].wait()
        column = x_ref[v].astype(F32)
        for r in range(0, rows, 8):
            xf[pl.ds(r * nvar + v, 8, stride=nvar), :] = column[r : r + 8]
    flat = x_ref[...].reshape(nvar * rows, cols)
    taken = lax.dot_general(pick, flat, (((1,), (1,)), ((), ())), preferred_element_type=F32)
    for v in range(nvar):
        part = taken[:, (v // per) * cols : (v // per + 1) * cols]
        shift = (2 - (v % per) * rows) % cols
        stage[8 * v : 8 * v + 8, :] = pltpu.roll(part, shift, 1)
    for i in range(len(wanted)):
        own_ref[i * nvar : (i + 1) * nvar, :] = stage[pl.ds(i, nvar, stride=8), :]
    ones = jnp.ones((PAD, cols), F32)

    def fill(r, carry):
        row = xf[pl.ds(pl.multiple_of(r * nvar, 8), nvar), :]
        tap = jnp.concatenate([row, pltpu.roll(row, 1, 1), pltpu.roll(row, cols - 1, 1), ones], axis=0)
        at = pl.multiple_of(r * block, 16)
        taps_ref[pl.ds(at, block), :] = tap.astype(BF16)
        return carry

    lax.fori_loop(0, rows, fill, 0, unroll=8)

    for copy in copies[parts:]:
        copy.wait()
    packed_ref[...] = packed_rows(conv_ref[...], bias_ref[...], nvar).astype(BF16)
    half_ref[...] = (out_ref[...].astype(F32) * 0.5).astype(BF16)
    index = index_ref[...]
    row = index // cols % rows
    var = index // (rows * cols)
    spot = jnp.clip(row * nvar + var, 0, rows * nvar - 1)
    place = (index % cols).astype(F32)
    for i in range(fold):
        spot_refs[i][...] = spot[i : i + 1, :]
        across = jnp.broadcast_to(place[i : i + 1, :], (cols, cols)).T
        hot = across == lanes_of((cols, cols)).astype(F32)
        chosen_ref[i * cols : (i + 1) * cols, :] = jnp.where(hot, 1.0, 0.0).astype(BF16)
    slot = lanes_of((fold, cols)) + cols * lax.broadcasted_iota(jnp.int32, (fold, cols), 0)
    live = jnp.where(slot < count_ref[0, 0], weight_ref[...], 0.0)
    member = lax.axis_index("ens")
    extra_ref[...] = jnp.where(member == 0, value_ref[...], jnp.where(member == 1, live, 0.0))


def spread(x, conv_weight, conv_bias, out_weight, index, count, value, weight):
    nvar, rows, cols = x.shape
    fold, hid = index.shape[0], conv_bias.shape[0]
    block = 3 * nvar + PAD
    args = (x, conv_weight, conv_bias[None], out_weight.T, index, count, value, weight)
    shape = jax.ShapeDtypeStruct
    scratch = [pltpu.VMEM(arg.shape, arg.dtype) for arg in args]
    del scratch[5]
    in_specs = [pl.BlockSpec(memory_space=pltpu.HBM)] * len(args)
    in_specs[5] = pl.BlockSpec(memory_space=pltpu.SMEM)
    placed = [pltpu.with_memory_space_constraint(arg, pltpu.HBM) for arg in args]
    placed[5] = count
    return pl.pallas_call(
        spread_kernel,
        out_shape=(
            shape((rows * block, cols), BF16),
            shape((4 * nvar, cols), F32),
            shape((hid, 3 * block), BF16),
            shape((nvar, hid), BF16),
            shape((fold, cols), F32),
            shape((fold * cols, cols), BF16),
        )
        + (shape((1, cols), jnp.int32),) * fold,
        in_specs=in_specs,
        scratch_shapes=scratch
        + [
            pltpu.VMEM((8 * nvar, cols), F32),
            pltpu.VMEM((nvar * rows, cols), F32),
            pltpu.SemaphoreType.DMA((most_of(nvar, 4) + len(args) - 2,)),
        ],
        compiler_params=pltpu.CompilerParams(vmem_limit_bytes=SMALL),
        cost_estimate=pl.CostEstimate(flops=10**8, bytes_accessed=4 * 10**6, transcendentals=0),
        name="spread",
    )(*placed)


def edge_columns(own, north, south, rows):
    nvar, cols = own.shape[0] // 4, own.shape[1]
    wanted = (0, 1, cols - 2, cols - 1)

    def kernel(own_ref, north_ref, south_ref, left_ref, right_ref):
        lane = lanes_of((nvar, cols))
        halo = []
        for ref, first in ((north_ref, 0), (south_ref, rows + 2)):
            for i in range(2):
                halo.append((first + i, ref[i * nvar : (i + 1) * nvar, :].astype(F32)))
        outs = []
        for i, c in enumerate(wanted):
            column = own_ref[i * nvar : (i + 1) * nvar, :]
            column = jnp.where(lane < rows + 2, column, 0.0)
            for at, row in halo:
                column = jnp.where(lane == at, pltpu.roll(row, (at - c) % cols, 1), column)
            outs.append(column)
        left_ref[...] = jnp.concatenate(outs[:2], axis=0).astype(BF16)
        right_ref[...] = jnp.concatenate(outs[2:], axis=0).astype(BF16)

    out = jax.ShapeDtypeStruct((2 * nvar, cols), BF16)
    return pl.pallas_call(
        kernel,
        out_shape=(out, out),
        compiler_params=pltpu.CompilerParams(vmem_limit_bytes=SMALL),
        name="edge_columns",
    )(own, north, south)


def gelu2(pre):
    pre = pre.astype(BF16)
    inner = pre * (jnp.asarray(GELU_A, BF16) + jnp.asarray(GELU_B, BF16) * (pre * pre))
    return pre + pre * jnp.tanh(inner)


def forecast_kernel(
    fold,
    *refs,
):
    spot_refs = refs[:fold]
    (
    taps_ref,
    north_ref,
    south_ref,
    own_left_ref,
    own_right_ref,
    from_left_ref,
    from_right_ref,
    conv_ref,
    out_w_ref,
    chosen_ref,
    extra_ref,
    forecast_ref,
    notes_ref,
    first,
    second,
    final,
    hidden,
    seen,
    conv,
    out_w,
    ) = refs[fold:]
    nvar, cols = north_ref.shape[0] // 2, north_ref.shape[1]
    block = 3 * nvar + PAD
    rows = taps_ref.shape[0] // block
    deep = 3 * block
    lane = lanes_of((nvar, cols))
    ones = jnp.ones((PAD, cols), F32)

    def tap_rows(row, west, east, at):
        left = jnp.where(lane == 0, pltpu.roll(west, (cols - at) % cols, 1), pltpu.roll(row, 1, 1))
        right = jnp.where(
            lane == cols - 1, pltpu.roll(east, (2 * cols - 1 - at) % cols, 1), pltpu.roll(row, cols - 1, 1)
        )
        return jnp.concatenate([row, left, right, ones], axis=0).astype(BF16)

    def hidden_of(patches):
        return gelu2(jnp.dot(conv[...], patches, preferred_element_type=F32))

    def moved(centre, hidden):
        change = jnp.dot(out_w[...], hidden, preferred_element_type=F32)
        return (centre + change).astype(BF16).astype(F32)

    conv[...] = conv_ref[...]
    out_w[...] = out_w_ref[...]
    from_left = from_left_ref[...].astype(F32)
    from_right = from_right_ref[...].astype(F32)
    own_left = own_left_ref[...].astype(F32)
    own_right = own_right_ref[...].astype(F32)
    far_west, west = from_left[:nvar], from_left[nvar:]
    east, far_east = from_right[:nvar], from_right[nvar:]
    inner_west, inner_east = own_left[:nvar], own_right[nvar:]

    for ref, start in ((north_ref, 0), (south_ref, rows + 2)):
        for i in range(2):
            row = ref[i * nvar : (i + 1) * nvar, :].astype(F32)
            first[(start + i) * block : (start + i + 1) * block, :] = tap_rows(row, west, east, start + i)

    group = lax.broadcasted_iota(jnp.int32, (block, cols), 0)
    wide = lanes_of((block, cols))
    is_left = (group >= nvar) & (group < 2 * nvar) & (wide == 0)
    is_right = (group >= 2 * nvar) & (group < 3 * nvar) & (wide == cols - 1)
    fix = jnp.where(is_left | is_right, 1.0, 0.0).astype(BF16) > 0
    nothing = jnp.zeros((nvar, cols), F32)
    source = jnp.concatenate([nothing, west, pltpu.roll(east, cols - 1, 1), jnp.zeros((PAD, cols), F32)], axis=0)
    source = source.astype(BF16)

    def fill(r, carry):
        at = pl.multiple_of(r * block, 16)
        mine = pltpu.roll(source, cols - 2 - r, 1)
        to = pl.multiple_of((r + 2) * block, 16)
        first[pl.ds(to, block), :] = jnp.where(fix, mine, taps_ref[pl.ds(at, block), :])
        return carry

    lax.fori_loop(0, rows, fill, 0, unroll=4)

    sides = []
    for mid, low, high in ((west, far_west, inner_west), (east, inner_east, far_east)):
        stack = []
        for a in range(3):
            for entry in (mid, low, high):
                stack.append(pltpu.roll(entry, (1 - a) % cols, 1) if a != 1 else entry)
            stack.append(ones)
        sides.append(jnp.concatenate(stack, axis=0).astype(BF16))
    patches = jnp.concatenate(sides, axis=1)
    beside = moved(jnp.concatenate([west, east], axis=1), hidden_of(patches))
    here = lax.axis_index("lat")
    north_in = (here > 0).astype(jnp.int32)
    south_in = (here < lax.axis_size("lat") - 1).astype(jnp.int32)
    keep = jnp.where(lane == 1, north_in, jnp.where(lane == rows + 2, south_in, 1)) > 0
    mid_west = jnp.where(keep, beside[:, :cols], 0.0)
    mid_east = jnp.where(keep, beside[:, cols:], 0.0)

    def ahead(source, at, slot):
        at = pl.multiple_of(at * block, 16)
        patches = jnp.concatenate(
            [source[pl.ds(at, deep), :], source[pl.ds(at + block, deep), :]], axis=1
        )
        hidden[slot] = hidden_of(patches)

    def finish(source, at, slot):
        at = pl.multiple_of(at * block, 16)
        centre = jnp.concatenate(
            [source[pl.ds(at + block, nvar), :], source[pl.ds(at + 2 * block, nvar), :]], axis=1
        ).astype(F32)
        return moved(centre, hidden[slot])

    def first_step(g, carry):
        for q in range(group1):
            ahead(first, 2 * (g * group1 + q), q)
        for q in range(group1):
            i = g * group1 + q
            both = finish(first, 2 * i, q)
            for half in range(2):
                m = 2 * i + half
                good = (jnp.where(m == 0, north_in, 1) * jnp.where(m == rows + 1, south_in, 1)) > 0
                row = both[:, half * cols : (half + 1) * cols]
                row = jnp.where(good, row, 0.0)
                at = pl.multiple_of(m * block, 16)
                second[pl.ds(at, block), :] = tap_rows(row, mid_west, mid_east, m + 1)
        return carry

    group1 = most_of(rows // 2 + 1, hidden.shape[0])
    lax.fori_loop(0, (rows // 2 + 1) // group1, first_step, 0)

    def second_step(g, carry):
        for q in range(group2):
            ahead(second, 2 * (g * group2 + q), q)
        for q in range(group2):
            j = g * group2 + q
            both = finish(second, 2 * j, q)
            both = jnp.concatenate([both[:, :cols], both[:, cols:]], axis=0)
            at = pl.multiple_of(j * 2 * nvar, 16)
            final[pl.ds(at, 2 * nvar), :] = both
            forecast_ref[pl.ds(at, 2 * nvar), :] = both.astype(BF16)
        return carry

    group2 = most_of(rows // 2, hidden.shape[0])
    lax.fori_loop(0, (rows // 2) // group2, second_step, 0)

    for half in range(fold):

        def look(o, carry, half=half):
            seen[pl.ds(half * cols + o, 1), :] = final[pl.ds(spot_refs[half][0, o], 1), :]
            return carry

        lax.fori_loop(0, cols, look, 0, unroll=32)
    masked = seen[...].astype(BF16) * chosen_ref[...]
    values = lax.dot_general(
        jnp.ones((8, cols), BF16), masked, (((1,), (1,)), ((), ())), preferred_element_type=F32
    )
    note = [values[0:1, i * cols : (i + 1) * cols] for i in range(fold)] + [extra_ref[...]]
    note = jnp.concatenate(note, axis=0).astype(BF16)
    for d in range(notes_ref.shape[0]):
        notes_ref[d] = note


def run_forecast(spot, taps, north, south, own_left, own_right, from_left, from_right, conv, out_w, chosen, extra, devices):
    nvar, cols = north.shape[0] // 2, north.shape[1]
    slots = len(spot) * cols
    block = 3 * nvar + PAD
    rows = taps.shape[0] // block
    smem = pl.BlockSpec(memory_space=pltpu.SMEM)
    vmem = pl.BlockSpec(memory_space=pltpu.VMEM)
    return pl.pallas_call(
        functools.partial(forecast_kernel, len(spot)),
        out_shape=(
            jax.ShapeDtypeStruct((rows * nvar, cols), BF16),
            jax.ShapeDtypeStruct((devices, 2 * extra.shape[0], cols), BF16),
        ),
        in_specs=[smem] * len(spot) + [vmem] * 11,
        out_specs=(vmem, vmem),
        scratch_shapes=[
            pltpu.VMEM(((rows + 4) * block, cols), BF16),
            pltpu.VMEM(((rows + 2) * block, cols), BF16),
            pltpu.VMEM((rows * nvar, cols), F32),
            pltpu.VMEM((GROUP, conv.shape[0], 2 * cols), BF16),
            pltpu.VMEM((slots, cols), F32),
            pltpu.VMEM(conv.shape, BF16),
            pltpu.VMEM(out_w.shape, BF16),
        ],
        compiler_params=pltpu.CompilerParams(vmem_limit_bytes=24 << 20),
        name="forecast",
    )(*spot, taps, north, south, own_left, own_right, from_left, from_right, conv, out_w, chosen, extra)


def pair_weights(gram, proj):
    count = len(proj)
    system = [[gram[k][m] + (float(count - 1) if k == m else 0.0) for m in range(count)] for k in range(count)]
    total = sum(entry * entry for line in system for entry in line)
    scale = jnp.sqrt(total)
    one = jnp.ones_like(scale)
    eye = [[one if k == m else 0.0 * one for m in range(count)] for k in range(count)]

    def times(left, right):
        return [
            [sum(left[k][j] * right[j][m] for j in range(count)) for m in range(count)] for k in range(count)
        ]

    current = [[entry / scale for entry in line] for line in system]
    inverse = eye
    for _ in range(NS_ITERS):
        both = times(inverse, current)
        factor = [[1.5 * eye[k][m] - 0.5 * both[k][m] for m in range(count)] for k in range(count)]
        current = times(current, factor)
        inverse = times(factor, inverse)
    root = jnp.sqrt(scale)
    root_inv = [[entry / root for entry in line] for line in inverse]
    half = [sum(root_inv[k][j] * proj[j] for j in range(count)) for k in range(count)]
    mean_w = [sum(root_inv[k][j] * half[j] for j in range(count)) for k in range(count)]
    span = math.sqrt(count - 1.0)
    full = [[mean_w[k] + span * root_inv[k][m] for m in range(count)] for k in range(count)]
    centre = [sum(full[k][m] for k in range(count)) / count for m in range(count)]
    return [[1.0 / count + full[k][m] - centre[m] for m in range(count)] for k in range(count)]


def analysis_kernel(told_ref, mine_ref, other_ref, out_ref, blended, packed, sems):
    count = lax.axis_size("ens")
    nvar, rows, cols = packed.shape[1], out_ref.shape[1], packed.shape[3]
    depth = told_ref.shape[1]
    told = told_ref[...].astype(F32).reshape(count, -1, cols)
    fold = depth // 2
    size = told.shape[1]
    hx = [told[k] for k in range(count)]
    value = pltpu.roll(told[0], size - fold, 0)
    weight = pltpu.roll(told[1], size - fold, 0)
    used = lax.broadcasted_iota(jnp.int32, (size, cols), 0) % depth < fold
    weight = jnp.where(used, weight, 0.0)
    mean = sum(hx) / count
    spread_of = [h - mean for h in hx]
    innov = value - mean
    tile = (8, cols)

    def total(term):
        return jnp.broadcast_to(jnp.sum(term, keepdims=True), tile)

    scaled = [part * weight for part in spread_of]
    gram = [[None] * count for _ in range(count)]
    for k in range(count):
        for m in range(k, count):
            gram[k][m] = gram[m][k] = total(scaled[k] * spread_of[m])
    weights = pair_weights(gram, [total(scaled[k] * innov) for k in range(count)])
    me = lax.axis_index("ens")
    mine = jnp.where(me == 0, weights[0][0], weights[1][1])[0:1, :]
    other = jnp.where(me == 0, weights[1][0], weights[0][1])[0:1, :]
    high = packed.shape[2]

    def copy_of(c):
        return pltpu.make_async_copy(packed.at[c], out_ref.at[:, pl.ds(c * high, high), :], sems.at[c])

    for c in range(rows // high):
        at = c * high * nvar
        part = slice(at, at + high * nvar)
        blended[c] = mine * mine_ref[part, :].astype(F32) + other * other_ref[part, :].astype(F32)
        for v in range(nvar):
            for r in range(0, high, 16):
                halves = [blended[c, pl.ds((r + 8 * i) * nvar + v, 8, stride=nvar), :] for i in range(2)]
                packed[c, v, r : r + 16, :] = jnp.concatenate(halves, axis=0).astype(BF16)
        copy_of(c).start()
    for c in range(rows // high):
        copy_of(c).wait()


def run_analysis(told, mine, other, shape):
    nvar, rows, cols = shape
    high = 16
    vmem = pl.BlockSpec(memory_space=pltpu.VMEM)
    return pl.pallas_call(
        analysis_kernel,
        out_shape=jax.ShapeDtypeStruct(shape, BF16),
        in_specs=[vmem, vmem, vmem],
        out_specs=pl.BlockSpec(memory_space=pltpu.HBM),
        scratch_shapes=[
            pltpu.VMEM((rows // high, high * nvar, cols), F32),
            pltpu.VMEM((rows // high, nvar, high, cols), BF16),
            pltpu.SemaphoreType.DMA((rows // high,)),
        ],
        compiler_params=pltpu.CompilerParams(vmem_limit_bytes=8 << 20),
        name="analysis",
    )(told, mine, other)


def blend_weights(gram, proj):
    entries_number = gram.shape[0]
    eye = jnp.eye(entries_number, dtype=gram.dtype)
    system = (entries_number - 1) * eye + gram
    scale = jnp.sqrt(jnp.sum(system * system))
    current = system / scale
    inverse = eye
    for _ in range(NS_ITERS):
        factor = 1.5 * eye - 0.5 * jnp.dot(inverse, current, precision=lax.Precision.HIGHEST)
        current = jnp.dot(current, factor, precision=lax.Precision.HIGHEST)
        inverse = jnp.dot(factor, inverse, precision=lax.Precision.HIGHEST)
    root_inv = inverse / jnp.sqrt(scale)
    half = jnp.dot(root_inv, proj, precision=lax.Precision.HIGHEST)
    mean_w = jnp.dot(root_inv, half, precision=lax.Precision.HIGHEST)
    full = mean_w[:, None] + math.sqrt(entries_number - 1.0) * root_inv
    return 1.0 / entries_number + full - jnp.mean(full, axis=0, keepdims=True)


def many_members(told, forecast, shape):
    nvar, rows, cols = shape
    fold = told.shape[1] // 2
    told = told.astype(F32).reshape(lax.axis_size("ens"), -1, *told.shape[1:])
    members = told[:, :, :fold, :].reshape(told.shape[0], -1)
    value = told[0, :, fold:, :].reshape(-1)
    weight = told[1, :, fold:, :].reshape(-1)
    mean = jnp.mean(members, axis=0)
    spread = members - mean[None, :]
    innov = value - mean
    weighted = spread * weight[None, :]
    gram = jnp.dot(weighted, spread.T, precision=lax.Precision.HIGHEST)
    proj = jnp.dot(weighted, innov, precision=lax.Precision.HIGHEST)
    transform = blend_weights(gram, proj)
    column = lax.dynamic_slice_in_dim(transform, lax.axis_index("ens"), 1, 1)[:, 0]
    everyone = lax.all_gather(forecast[None], "ens", axis=0, tiled=True)
    blended = jnp.tensordot(column, everyone.astype(F32), axes=1, precision=lax.Precision.HIGHEST)
    return blended.astype(BF16).reshape(rows, nvar, cols).transpose(1, 0, 2)


def per_device(
    sample_quantities,
    conv_weight,
    conv_bias,
    out_weight,
    obs_index,
    obs_count,
    obs_value,
    obs_weight,
):
    x = sample_quantities[0]
    _, rows, cols = x.shape
    n_ens, n_lat, n_lon = (lax.axis_size(axis) for axis in ("ens", "lat", "lon"))
    down_lat = [(i, i + 1) for i in range(n_lat - 1)]
    up_lat = [(j, i) for i, j in down_lat]
    right_lon = [(i, (i + 1) % n_lon) for i in range(n_lon)]
    left_lon = [(j, i) for i, j in right_lon]

    first_rows, last_rows = edge_rows(x)
    north = lax.ppermute(last_rows, "lat", down_lat)
    south = lax.ppermute(first_rows, "lat", up_lat)
    fold = (obs_index.size // cols, cols)
    taps, own, conv, out_w, extra, chosen, *spot = spread(
        x,
        conv_weight,
        conv_bias,
        out_weight,
        obs_index.reshape(fold),
        obs_count,
        obs_value.reshape(fold),
        obs_weight.reshape(fold),
    )
    own_left, own_right = edge_columns(own, north, south, rows)
    from_left = lax.ppermute(own_right, "lon", right_lon)
    from_right = lax.ppermute(own_left, "lon", left_lon)

    forecast, notes = run_forecast(
        spot,
        taps,
        north,
        south,
        own_left,
        own_right,
        from_left,
        from_right,
        conv,
        out_w,
        chosen,
        extra,
        n_ens * n_lat * n_lon,
    )
    told = lax.all_to_all(notes, ("ens", "lat", "lon"), 0, 0, tiled=True)
    if n_ens == 2:
        other = lax.ppermute(forecast, "ens", [(0, 1), (1, 0)])
        return run_analysis(told, forecast, other, x.shape)[None]
    return many_members(told, forecast, x.shape)[None]


def solution(mesh):
    return jax.shard_map(
        per_device,
        mesh=mesh,
        in_specs=(
            P("ens", None, "lat", "lon"),
            P(),
            P(),
            P(),
            P("lat", "lon", None),
            P("lat", "lon"),
            P("lat", "lon", None),
            P("lat", "lon", None),
        ),
        out_specs=P("ens", None, "lat", "lon"),
        check_vma=False,
    )
```

```python
import functools
import math

import jax
import jax.numpy as jnp
from jax import lax
from jax.experimental import pallas as pl
from jax.experimental.pallas import tpu as pltpu
from jax.sharding import PartitionSpec as P

NS_ITERS = 20
GELU_A = math.sqrt(2.0 / math.pi)
GELU_B = GELU_A * 0.044715
F32 = jnp.float32
BF16 = jnp.bfloat16
PAD = 8
SMALL = 4 << 20
GROUP = 34


def lanes_of(shape):
    return lax.broadcasted_iota(jnp.int32, shape, len(shape) - 1)


def most_of(total, limit):
    return max(d for d in range(1, limit + 1) if total % d == 0)


def edge_rows(x):
    nvar, rows, cols = x.shape
    tile = 16

    def kernel(x_ref, up_ref, down_ref, part, stage, sems):
        copies = []
        for i, first in enumerate((0, rows - tile)):
            copies.append(pltpu.make_async_copy(x_ref.at[:, first : first + tile, :], part.at[i], sems.at[i]))
            copies[i].start()
        for i, (out, first) in enumerate(((up_ref, 0), (down_ref, tile - 2))):
            copies[i].wait()
            stage[...] = part[i].reshape(nvar * tile, cols).astype(F32)
            both = [stage[pl.ds(first + j, nvar, stride=tile), :] for j in range(2)]
            out[...] = jnp.concatenate(both, axis=0).astype(BF16)

    out = jax.ShapeDtypeStruct((2 * nvar, cols), BF16)
    return pl.pallas_call(
        kernel,
        out_shape=(out, out),
        in_specs=[pl.BlockSpec(memory_space=pltpu.HBM)],
        scratch_shapes=[
            pltpu.VMEM((2, nvar, tile, cols), BF16),
            pltpu.VMEM((nvar * tile, cols), F32),
            pltpu.SemaphoreType.DMA((2,)),
        ],
        compiler_params=pltpu.CompilerParams(vmem_limit_bytes=SMALL),
        name="edge_rows",
    )(pltpu.with_memory_space_constraint(x, pltpu.HBM))


def packed_rows(conv, bias, nvar):
    hid = bias.shape[1]
    high = bias.astype(BF16).astype(F32)
    middle = (bias - high).astype(BF16).astype(F32)
    low = (bias - high - middle).astype(BF16).astype(F32)
    rest = jnp.zeros((PAD - 3, hid), F32)
    pieces = []
    for a in range(3):
        for b in (1, 0, 2):
            at = (3 * a + b) * nvar
            pieces.append(conv[at : at + nvar, :].astype(F32))
        if a == 1:
            pieces.append(jnp.concatenate([high, middle, low, rest], axis=0))
        else:
            pieces.append(jnp.zeros((PAD, hid), F32))
    return jnp.concatenate(pieces, axis=0).T


def spread_kernel(
    x_hbm,
    conv_hbm,
    bias_hbm,
    out_hbm,
    index_hbm,
    count_ref,
    value_hbm,
    weight_hbm,
    taps_ref,
    own_ref,
    packed_ref,
    half_ref,
    extra_ref,
    chosen_ref,
    *rest,
):
    fold = extra_ref.shape[0]
    spot_refs = rest[:fold]
    x_ref, conv_ref, bias_ref, out_ref, index_ref, value_ref, weight_ref, stage, xf, sems = rest[fold:]
    nvar, rows, cols = x_ref.shape
    block = 3 * nvar + PAD
    small = [
        (conv_hbm, conv_ref),
        (bias_hbm, bias_ref),
        (out_hbm, out_ref),
        (index_hbm, index_ref),
        (value_hbm, value_ref),
        (weight_hbm, weight_ref),
    ]
    parts = sems.shape[0] - len(small)
    each = nvar // parts
    copies = []
    for i in range(parts):
        part = slice(i * each, (i + 1) * each)
        copies.append(pltpu.make_async_copy(x_hbm.at[part], x_ref.at[part], sems.at[i]))
    for i, (source, target) in enumerate(small):
        copies.append(pltpu.make_async_copy(source, target, sems.at[parts + i]))
    for copy in copies:
        copy.start()

    wanted = (0, 1, cols - 2, cols - 1)
    k = lax.broadcasted_iota(jnp.int32, (8, cols), 0)
    lane = lanes_of((8, cols))
    pick = jnp.zeros((8, cols), F32)
    for i, c in enumerate(wanted):
        pick = jnp.where((k == i) & (lane == c), 1.0, pick)
    pick = pick.astype(BF16)
    per = cols // rows
    for v in range(nvar):
        if v % each == 0:
            copies[v // each].wait()
        column = x_ref[v].astype(F32)
        for r in range(0, rows, 8):
            xf[pl.ds(r * nvar + v, 8, stride=nvar), :] = column[r : r + 8]
    flat = x_ref[...].reshape(nvar * rows, cols)
    taken = lax.dot_general(pick, flat, (((1,), (1,)), ((), ())), preferred_element_type=F32)
    for v in range(nvar):
        part = taken[:, (v // per) * cols : (v // per + 1) * cols]
        shift = (2 - (v % per) * rows) % cols
        stage[8 * v : 8 * v + 8, :] = pltpu.roll(part, shift, 1)
    for i in range(len(wanted)):
        own_ref[i * nvar : (i + 1) * nvar, :] = stage[pl.ds(i, nvar, stride=8), :]
    ones = jnp.ones((PAD, cols), F32)

    def fill(r, carry):
        row = xf[pl.ds(pl.multiple_of(r * nvar, 8), nvar), :]
        tap = jnp.concatenate([row, pltpu.roll(row, 1, 1), pltpu.roll(row, cols - 1, 1), ones], axis=0)
        at = pl.multiple_of(r * block, 16)
        taps_ref[pl.ds(at, block), :] = tap.astype(BF16)
        return carry

    lax.fori_loop(0, rows, fill, 0, unroll=8)

    for copy in copies[parts:]:
        copy.wait()
    packed_ref[...] = packed_rows(conv_ref[...], bias_ref[...], nvar).astype(BF16)
    half_ref[...] = (out_ref[...].astype(F32) * 0.5).astype(BF16)
    index = index_ref[...]
    row = index // cols % rows
    var = index // (rows * cols)
    spot = jnp.clip(row * nvar + var, 0, rows * nvar - 1)
    place = (index % cols).astype(F32)
    for i in range(fold):
        spot_refs[i][...] = spot[i : i + 1, :]
        across = jnp.broadcast_to(place[i : i + 1, :], (cols, cols)).T
        hot = across == lanes_of((cols, cols)).astype(F32)
        chosen_ref[i * cols : (i + 1) * cols, :] = jnp.where(hot, 1.0, 0.0).astype(BF16)
    slot = lanes_of((fold, cols)) + cols * lax.broadcasted_iota(jnp.int32, (fold, cols), 0)
    live = jnp.where(slot < count_ref[0, 0], weight_ref[...], 0.0)
    member = lax.axis_index("ens")
    extra_ref[...] = jnp.where(member == 0, value_ref[...], jnp.where(member == 1, live, 0.0))


def spread(x, conv_weight, conv_bias, out_weight, index, count, value, weight):
    nvar, rows, cols = x.shape
    fold, hid = index.shape[0], conv_bias.shape[0]
    block = 3 * nvar + PAD
    args = (x, conv_weight, conv_bias[None], out_weight.T, index, count, value, weight)
    shape = jax.ShapeDtypeStruct
    scratch = [pltpu.VMEM(arg.shape, arg.dtype) for arg in args]
    del scratch[5]
    in_specs = [pl.BlockSpec(memory_space=pltpu.HBM)] * len(args)
    in_specs[5] = pl.BlockSpec(memory_space=pltpu.SMEM)
    placed = [pltpu.with_memory_space_constraint(arg, pltpu.HBM) for arg in args]
    placed[5] = count
    return pl.pallas_call(
        spread_kernel,
        out_shape=(
            shape((rows * block, cols), BF16),
            shape((4 * nvar, cols), F32),
            shape((hid, 3 * block), BF16),
            shape((nvar, hid), BF16),
            shape((fold, cols), F32),
            shape((fold * cols, cols), BF16),
        )
        + (shape((1, cols), jnp.int32),) * fold,
        in_specs=in_specs,
        scratch_shapes=scratch
        + [
            pltpu.VMEM((8 * nvar, cols), F32),
            pltpu.VMEM((nvar * rows, cols), F32),
            pltpu.SemaphoreType.DMA((most_of(nvar, 4) + len(args) - 2,)),
        ],
        compiler_params=pltpu.CompilerParams(vmem_limit_bytes=SMALL),
        cost_estimate=pl.CostEstimate(flops=10**8, bytes_accessed=4 * 10**6, transcendentals=0),
        name="spread",
    )(*placed)


def edge_columns(own, north, south, rows):
    nvar, cols = own.shape[0] // 4, own.shape[1]
    wanted = (0, 1, cols - 2, cols - 1)

    def kernel(own_ref, north_ref, south_ref, left_ref, right_ref, between_ref, within_ref):
        lane = lanes_of((nvar, cols))
        halo = []
        for ref, first in ((north_ref, 0), (south_ref, rows + 2)):
            for i in range(2):
                halo.append((first + i, ref[i * nvar : (i + 1) * nvar, :].astype(F32)))
        outs = []
        for i, c in enumerate(wanted):
            column = own_ref[i * nvar : (i + 1) * nvar, :]
            column = jnp.where(lane < rows + 2, column, 0.0)
            for at, row in halo:
                column = jnp.where(lane == at, pltpu.roll(row, (at - c) % cols, 1), column)
            outs.append(column)
        left, right = jnp.concatenate(outs[:2], axis=0), jnp.concatenate(outs[2:], axis=0)
        even = lax.axis_index("lon") % 2 == 0
        left_ref[...] = left.astype(BF16)
        right_ref[...] = right.astype(BF16)
        between_ref[...] = jnp.where(even, left, right).astype(BF16)
        within_ref[...] = jnp.where(even, right, left).astype(BF16)

    out = jax.ShapeDtypeStruct((2 * nvar, cols), BF16)
    return pl.pallas_call(
        kernel,
        out_shape=(out,) * 4,
        compiler_params=pltpu.CompilerParams(vmem_limit_bytes=SMALL),
        name="edge_columns",
    )(own, north, south)


def gelu2(pre):
    pre = pre.astype(BF16)
    inner = pre * (jnp.asarray(GELU_A, BF16) + jnp.asarray(GELU_B, BF16) * (pre * pre))
    return pre + pre * jnp.tanh(inner)


def forecast_kernel(
    fold,
    *refs,
):
    spot_refs = refs[:fold]
    (
    taps_ref,
    north_ref,
    south_ref,
    own_left_ref,
    own_right_ref,
    between_ref,
    within_ref,
    conv_ref,
    out_w_ref,
    chosen_ref,
    extra_ref,
    forecast_ref,
    notes_ref,
    first,
    second,
    final,
    hidden,
    seen,
    conv,
    out_w,
    ) = refs[fold:]
    nvar, cols = north_ref.shape[0] // 2, north_ref.shape[1]
    block = 3 * nvar + PAD
    rows = taps_ref.shape[0] // block
    deep = 3 * block
    lane = lanes_of((nvar, cols))
    ones = jnp.ones((PAD, cols), F32)

    def tap_rows(row, west, east, at):
        left = jnp.where(lane == 0, pltpu.roll(west, (cols - at) % cols, 1), pltpu.roll(row, 1, 1))
        right = jnp.where(
            lane == cols - 1, pltpu.roll(east, (2 * cols - 1 - at) % cols, 1), pltpu.roll(row, cols - 1, 1)
        )
        return jnp.concatenate([row, left, right, ones], axis=0).astype(BF16)

    def hidden_of(patches):
        return gelu2(jnp.dot(conv[...], patches, preferred_element_type=F32))

    def moved(centre, hidden):
        change = jnp.dot(out_w[...], hidden, preferred_element_type=F32)
        return (centre + change).astype(BF16).astype(F32)

    conv[...] = conv_ref[...]
    out_w[...] = out_w_ref[...]
    even = lax.axis_index("lon") % 2 == 0
    between = between_ref[...].astype(F32)
    within = within_ref[...].astype(F32)
    from_left = jnp.where(even, between, within)
    from_right = jnp.where(even, within, between)
    own_left = own_left_ref[...].astype(F32)
    own_right = own_right_ref[...].astype(F32)
    far_west, west = from_left[:nvar], from_left[nvar:]
    east, far_east = from_right[:nvar], from_right[nvar:]
    inner_west, inner_east = own_left[:nvar], own_right[nvar:]

    for ref, start in ((north_ref, 0), (south_ref, rows + 2)):
        for i in range(2):
            row = ref[i * nvar : (i + 1) * nvar, :].astype(F32)
            first[(start + i) * block : (start + i + 1) * block, :] = tap_rows(row, west, east, start + i)

    group = lax.broadcasted_iota(jnp.int32, (block, cols), 0)
    wide = lanes_of((block, cols))
    is_left = (group >= nvar) & (group < 2 * nvar) & (wide == 0)
    is_right = (group >= 2 * nvar) & (group < 3 * nvar) & (wide == cols - 1)
    fix = jnp.where(is_left | is_right, 1.0, 0.0).astype(BF16) > 0
    nothing = jnp.zeros((nvar, cols), F32)
    source = jnp.concatenate([nothing, west, pltpu.roll(east, cols - 1, 1), jnp.zeros((PAD, cols), F32)], axis=0)
    source = source.astype(BF16)

    def fill(r, carry):
        at = pl.multiple_of(r * block, 16)
        mine = pltpu.roll(source, cols - 2 - r, 1)
        to = pl.multiple_of((r + 2) * block, 16)
        first[pl.ds(to, block), :] = jnp.where(fix, mine, taps_ref[pl.ds(at, block), :])
        return carry

    lax.fori_loop(0, rows, fill, 0, unroll=4)

    sides = []
    for mid, low, high in ((west, far_west, inner_west), (east, inner_east, far_east)):
        stack = []
        for a in range(3):
            for entry in (mid, low, high):
                stack.append(pltpu.roll(entry, (1 - a) % cols, 1) if a != 1 else entry)
            stack.append(ones)
        sides.append(jnp.concatenate(stack, axis=0).astype(BF16))
    patches = jnp.concatenate(sides, axis=1)
    beside = moved(jnp.concatenate([west, east], axis=1), hidden_of(patches))
    here = lax.axis_index("lat")
    north_in = (here > 0).astype(jnp.int32)
    south_in = (here < lax.axis_size("lat") - 1).astype(jnp.int32)
    keep = jnp.where(lane == 1, north_in, jnp.where(lane == rows + 2, south_in, 1)) > 0
    mid_west = jnp.where(keep, beside[:, :cols], 0.0)
    mid_east = jnp.where(keep, beside[:, cols:], 0.0)

    def ahead(source, at, slot):
        at = pl.multiple_of(at * block, 16)
        patches = jnp.concatenate(
            [source[pl.ds(at, deep), :], source[pl.ds(at + block, deep), :]], axis=1
        )
        hidden[slot] = hidden_of(patches)

    def finish(source, at, slot):
        at = pl.multiple_of(at * block, 16)
        centre = jnp.concatenate(
            [source[pl.ds(at + block, nvar), :], source[pl.ds(at + 2 * block, nvar), :]], axis=1
        ).astype(F32)
        return moved(centre, hidden[slot])

    def first_step(g, carry):
        for q in range(group1):
            ahead(first, 2 * (g * group1 + q), q)
        for q in range(group1):
            i = g * group1 + q
            both = finish(first, 2 * i, q)
            for half in range(2):
                m = 2 * i + half
                good = (jnp.where(m == 0, north_in, 1) * jnp.where(m == rows + 1, south_in, 1)) > 0
                row = both[:, half * cols : (half + 1) * cols]
                row = jnp.where(good, row, 0.0)
                at = pl.multiple_of(m * block, 16)
                second[pl.ds(at, block), :] = tap_rows(row, mid_west, mid_east, m + 1)
        return carry

    group1 = most_of(rows // 2 + 1, hidden.shape[0])
    lax.fori_loop(0, (rows // 2 + 1) // group1, first_step, 0)

    def second_step(g, carry):
        for q in range(group2):
            ahead(second, 2 * (g * group2 + q), q)
        for q in range(group2):
            j = g * group2 + q
            both = finish(second, 2 * j, q)
            both = jnp.concatenate([both[:, :cols], both[:, cols:]], axis=0)
            at = pl.multiple_of(j * 2 * nvar, 16)
            final[pl.ds(at, 2 * nvar), :] = both
            forecast_ref[pl.ds(at, 2 * nvar), :] = both.astype(BF16)
        return carry

    group2 = most_of(rows // 2, hidden.shape[0])
    lax.fori_loop(0, (rows // 2) // group2, second_step, 0)

    for half in range(fold):

        def look(o, carry, half=half):
            seen[pl.ds(half * cols + o, 1), :] = final[pl.ds(spot_refs[half][0, o], 1), :]
            return carry

        lax.fori_loop(0, cols, look, 0, unroll=32)
    masked = seen[...].astype(BF16) * chosen_ref[...]
    values = lax.dot_general(
        jnp.ones((8, cols), BF16), masked, (((1,), (1,)), ((), ())), preferred_element_type=F32
    )
    note = [values[0:1, i * cols : (i + 1) * cols] for i in range(fold)] + [extra_ref[...]]
    note = jnp.concatenate(note, axis=0).astype(BF16)
    for d in range(notes_ref.shape[0]):
        notes_ref[d] = note


def run_forecast(spot, taps, north, south, own_left, own_right, between, within, conv, out_w, chosen, extra, devices):
    nvar, cols = north.shape[0] // 2, north.shape[1]
    slots = len(spot) * cols
    block = 3 * nvar + PAD
    rows = taps.shape[0] // block
    smem = pl.BlockSpec(memory_space=pltpu.SMEM)
    vmem = pl.BlockSpec(memory_space=pltpu.VMEM)
    return pl.pallas_call(
        functools.partial(forecast_kernel, len(spot)),
        out_shape=(
            jax.ShapeDtypeStruct((rows * nvar, cols), BF16),
            jax.ShapeDtypeStruct((devices, 2 * extra.shape[0], cols), BF16),
        ),
        in_specs=[smem] * len(spot) + [vmem] * 11,
        out_specs=(vmem, vmem),
        scratch_shapes=[
            pltpu.VMEM(((rows + 4) * block, cols), BF16),
            pltpu.VMEM(((rows + 2) * block, cols), BF16),
            pltpu.VMEM((rows * nvar, cols), F32),
            pltpu.VMEM((GROUP, conv.shape[0], 2 * cols), BF16),
            pltpu.VMEM((slots, cols), F32),
            pltpu.VMEM(conv.shape, BF16),
            pltpu.VMEM(out_w.shape, BF16),
        ],
        compiler_params=pltpu.CompilerParams(vmem_limit_bytes=24 << 20),
        name="forecast",
    )(*spot, taps, north, south, own_left, own_right, between, within, conv, out_w, chosen, extra)


def pair_weights(gram, proj):
    count = len(proj)
    system = [[gram[k][m] + (float(count - 1) if k == m else 0.0) for m in range(count)] for k in range(count)]
    total = sum(entry * entry for line in system for entry in line)
    scale = jnp.sqrt(total)
    one = jnp.ones_like(scale)
    eye = [[one if k == m else 0.0 * one for m in range(count)] for k in range(count)]

    def times(left, right):
        return [
            [sum(left[k][j] * right[j][m] for j in range(count)) for m in range(count)] for k in range(count)
        ]

    current = [[entry / scale for entry in line] for line in system]
    inverse = eye
    for _ in range(NS_ITERS):
        both = times(inverse, current)
        factor = [[1.5 * eye[k][m] - 0.5 * both[k][m] for m in range(count)] for k in range(count)]
        current = times(current, factor)
        inverse = times(factor, inverse)
    root = jnp.sqrt(scale)
    root_inv = [[entry / root for entry in line] for line in inverse]
    half = [sum(root_inv[k][j] * proj[j] for j in range(count)) for k in range(count)]
    mean_w = [sum(root_inv[k][j] * half[j] for j in range(count)) for k in range(count)]
    span = math.sqrt(count - 1.0)
    full = [[mean_w[k] + span * root_inv[k][m] for m in range(count)] for k in range(count)]
    centre = [sum(full[k][m] for k in range(count)) / count for m in range(count)]
    return [[1.0 / count + full[k][m] - centre[m] for m in range(count)] for k in range(count)]


def analysis_kernel(told_ref, mine_ref, other_ref, out_ref, blended, packed, sems):
    count = lax.axis_size("ens")
    nvar, rows, cols = packed.shape[1], out_ref.shape[1], packed.shape[3]
    depth = told_ref.shape[1]
    told = told_ref[...].astype(F32).reshape(count, -1, cols)
    fold = depth // 2
    size = told.shape[1]
    hx = [told[k] for k in range(count)]
    value = pltpu.roll(told[0], size - fold, 0)
    weight = pltpu.roll(told[1], size - fold, 0)
    used = lax.broadcasted_iota(jnp.int32, (size, cols), 0) % depth < fold
    weight = jnp.where(used, weight, 0.0)
    mean = sum(hx) / count
    spread_of = [h - mean for h in hx]
    innov = value - mean
    tile = (8, cols)

    def total(term):
        return jnp.broadcast_to(jnp.sum(term, keepdims=True), tile)

    scaled = [part * weight for part in spread_of]
    gram = [[None] * count for _ in range(count)]
    for k in range(count):
        for m in range(k, count):
            gram[k][m] = gram[m][k] = total(scaled[k] * spread_of[m])
    weights = pair_weights(gram, [total(scaled[k] * innov) for k in range(count)])
    me = lax.axis_index("ens")
    mine = jnp.where(me == 0, weights[0][0], weights[1][1])[0:1, :]
    other = jnp.where(me == 0, weights[1][0], weights[0][1])[0:1, :]
    high = packed.shape[2]

    def copy_of(c):
        return pltpu.make_async_copy(packed.at[c], out_ref.at[:, pl.ds(c * high, high), :], sems.at[c])

    for c in range(rows // high):
        at = c * high * nvar
        part = slice(at, at + high * nvar)
        blended[c] = mine * mine_ref[part, :].astype(F32) + other * other_ref[part, :].astype(F32)
        for v in range(nvar):
            for r in range(0, high, 16):
                halves = [blended[c, pl.ds((r + 8 * i) * nvar + v, 8, stride=nvar), :] for i in range(2)]
                packed[c, v, r : r + 16, :] = jnp.concatenate(halves, axis=0).astype(BF16)
        copy_of(c).start()
    for c in range(rows // high):
        copy_of(c).wait()


def run_analysis(told, mine, other, shape):
    nvar, rows, cols = shape
    high = 16
    vmem = pl.BlockSpec(memory_space=pltpu.VMEM)
    return pl.pallas_call(
        analysis_kernel,
        out_shape=jax.ShapeDtypeStruct(shape, BF16),
        in_specs=[vmem, vmem, vmem],
        out_specs=pl.BlockSpec(memory_space=pltpu.HBM),
        scratch_shapes=[
            pltpu.VMEM((rows // high, high * nvar, cols), F32),
            pltpu.VMEM((rows // high, nvar, high, cols), BF16),
            pltpu.SemaphoreType.DMA((rows // high,)),
        ],
        compiler_params=pltpu.CompilerParams(vmem_limit_bytes=8 << 20),
        name="analysis",
    )(told, mine, other)


def blend_weights(gram, proj):
    entries_number = gram.shape[0]
    eye = jnp.eye(entries_number, dtype=gram.dtype)
    system = (entries_number - 1) * eye + gram
    scale = jnp.sqrt(jnp.sum(system * system))
    current = system / scale
    inverse = eye
    for _ in range(NS_ITERS):
        factor = 1.5 * eye - 0.5 * jnp.dot(inverse, current, precision=lax.Precision.HIGHEST)
        current = jnp.dot(current, factor, precision=lax.Precision.HIGHEST)
        inverse = jnp.dot(factor, inverse, precision=lax.Precision.HIGHEST)
    root_inv = inverse / jnp.sqrt(scale)
    half = jnp.dot(root_inv, proj, precision=lax.Precision.HIGHEST)
    mean_w = jnp.dot(root_inv, half, precision=lax.Precision.HIGHEST)
    full = mean_w[:, None] + math.sqrt(entries_number - 1.0) * root_inv
    return 1.0 / entries_number + full - jnp.mean(full, axis=0, keepdims=True)


def many_members(told, forecast, shape):
    nvar, rows, cols = shape
    fold = told.shape[1] // 2
    told = told.astype(F32).reshape(lax.axis_size("ens"), -1, *told.shape[1:])
    members = told[:, :, :fold, :].reshape(told.shape[0], -1)
    value = told[0, :, fold:, :].reshape(-1)
    weight = told[1, :, fold:, :].reshape(-1)
    mean = jnp.mean(members, axis=0)
    spread = members - mean[None, :]
    innov = value - mean
    weighted = spread * weight[None, :]
    gram = jnp.dot(weighted, spread.T, precision=lax.Precision.HIGHEST)
    proj = jnp.dot(weighted, innov, precision=lax.Precision.HIGHEST)
    transform = blend_weights(gram, proj)
    column = lax.dynamic_slice_in_dim(transform, lax.axis_index("ens"), 1, 1)[:, 0]
    everyone = lax.all_gather(forecast[None], "ens", axis=0, tiled=True)
    blended = jnp.tensordot(column, everyone.astype(F32), axes=1, precision=lax.Precision.HIGHEST)
    return blended.astype(BF16).reshape(rows, nvar, cols).transpose(1, 0, 2)


def per_device(
    sample_quantities,
    conv_weight,
    conv_bias,
    out_weight,
    obs_index,
    obs_count,
    obs_value,
    obs_weight,
):
    x = sample_quantities[0]
    _, rows, cols = x.shape
    n_ens, n_lat, n_lon = (lax.axis_size(axis) for axis in ("ens", "lat", "lon"))
    down_lat = [(i, i + 1) for i in range(n_lat - 1)]
    up_lat = [(j, i) for i, j in down_lat]
    assert n_lon % 2 == 0
    odd_pairs = [(i, (i + 1) % n_lon) for i in range(1, n_lon, 2)]
    even_pairs = [(i, i + 1) for i in range(0, n_lon, 2)]

    first_rows, last_rows = edge_rows(x)
    north = lax.ppermute(last_rows, "lat", down_lat)
    south = lax.ppermute(first_rows, "lat", up_lat)
    fold = (obs_index.size // cols, cols)
    taps, own, conv, out_w, extra, chosen, *spot = spread(
        x,
        conv_weight,
        conv_bias,
        out_weight,
        obs_index.reshape(fold),
        obs_count,
        obs_value.reshape(fold),
        obs_weight.reshape(fold),
    )
    own_left, own_right, outer, inner = edge_columns(own, north, south, rows)
    between = lax.ppermute(outer, "lon", odd_pairs + [(j, i) for i, j in odd_pairs])
    within = lax.ppermute(inner, "lon", even_pairs + [(j, i) for i, j in even_pairs])
    forecast, notes = run_forecast(
        spot,
        taps,
        north,
        south,
        own_left,
        own_right,
        between,
        within,
        conv,
        out_w,
        chosen,
        extra,
        n_ens * n_lat * n_lon,
    )
    told = lax.all_to_all(notes, ("ens", "lat", "lon"), 0, 0, tiled=True)
    if n_ens == 2:
        other = lax.ppermute(forecast, "ens", [(0, 1), (1, 0)])
        return run_analysis(told, forecast, other, x.shape)[None]
    return many_members(told, forecast, x.shape)[None]


def solution(mesh):
    return jax.shard_map(
        per_device,
        mesh=mesh,
        in_specs=(
            P("ens", None, "lat", "lon"),
            P(),
            P(),
            P(),
            P("lat", "lon", None),
            P("lat", "lon"),
            P("lat", "lon", None),
            P("lat", "lon", None),
        ),
        out_specs=P("ens", None, "lat", "lon"),
        check_vma=False,
    )
```

```python
import functools
import math

import jax
import jax.numpy as jnp
from jax import lax
from jax.experimental import pallas as pl
from jax.experimental.pallas import tpu as pltpu
from jax.sharding import PartitionSpec as P

NS_ITERS = 20
GELU_A = math.sqrt(2.0 / math.pi)
GELU_B = GELU_A * 0.044715
F32 = jnp.float32
BF16 = jnp.bfloat16
PAD = 8
SMALL = 4 << 20
GROUP = 34


def lanes_of(shape):
    return lax.broadcasted_iota(jnp.int32, shape, len(shape) - 1)


def most_of(total, limit):
    return max(d for d in range(1, limit + 1) if total % d == 0)


def edge_rows(x):
    nvar, rows, cols = x.shape
    tile = 16

    def kernel(x_ref, near_ref, far_ref, part, stage, sems):
        copies = []
        for i, first in enumerate((0, rows - tile)):
            copies.append(pltpu.make_async_copy(x_ref.at[:, first : first + tile, :], part.at[i], sems.at[i]))
            copies[i].start()
        ends = []
        for i, first in enumerate((0, tile - 2)):
            copies[i].wait()
            stage[...] = part[i].reshape(nvar * tile, cols).astype(F32)
            both = [stage[pl.ds(first + j, nvar, stride=tile), :] for j in range(2)]
            ends.append(jnp.concatenate(both, axis=0))
        even = lax.axis_index("lat") % 2 == 0
        near_ref[...] = jnp.where(even, ends[1], ends[0]).astype(BF16)
        far_ref[...] = jnp.where(even, ends[0], ends[1]).astype(BF16)

    out = jax.ShapeDtypeStruct((2 * nvar, cols), BF16)
    return pl.pallas_call(
        kernel,
        out_shape=(out, out),
        in_specs=[pl.BlockSpec(memory_space=pltpu.HBM)],
        scratch_shapes=[
            pltpu.VMEM((2, nvar, tile, cols), BF16),
            pltpu.VMEM((nvar * tile, cols), F32),
            pltpu.SemaphoreType.DMA((2,)),
        ],
        compiler_params=pltpu.CompilerParams(vmem_limit_bytes=SMALL),
        name="edge_rows",
    )(pltpu.with_memory_space_constraint(x, pltpu.HBM))


def packed_rows(conv, bias, nvar):
    hid = bias.shape[1]
    high = bias.astype(BF16).astype(F32)
    middle = (bias - high).astype(BF16).astype(F32)
    low = (bias - high - middle).astype(BF16).astype(F32)
    rest = jnp.zeros((PAD - 3, hid), F32)
    pieces = []
    for a in range(3):
        for b in (1, 0, 2):
            at = (3 * a + b) * nvar
            pieces.append(conv[at : at + nvar, :].astype(F32))
        if a == 1:
            pieces.append(jnp.concatenate([high, middle, low, rest], axis=0))
        else:
            pieces.append(jnp.zeros((PAD, hid), F32))
    return jnp.concatenate(pieces, axis=0).T


def spread_kernel(
    x_hbm,
    conv_hbm,
    bias_hbm,
    out_hbm,
    index_hbm,
    count_ref,
    value_hbm,
    weight_hbm,
    taps_ref,
    own_ref,
    packed_ref,
    half_ref,
    extra_ref,
    chosen_ref,
    *rest,
):
    fold = extra_ref.shape[0]
    spot_refs = rest[:fold]
    x_ref, conv_ref, bias_ref, out_ref, index_ref, value_ref, weight_ref, stage, xf, sems = rest[fold:]
    nvar, rows, cols = x_ref.shape
    block = 3 * nvar + PAD
    small = [
        (conv_hbm, conv_ref),
        (bias_hbm, bias_ref),
        (out_hbm, out_ref),
        (index_hbm, index_ref),
        (value_hbm, value_ref),
        (weight_hbm, weight_ref),
    ]
    parts = sems.shape[0] - len(small)
    each = nvar // parts
    copies = []
    for i in range(parts):
        part = slice(i * each, (i + 1) * each)
        copies.append(pltpu.make_async_copy(x_hbm.at[part], x_ref.at[part], sems.at[i]))
    for i, (source, target) in enumerate(small):
        copies.append(pltpu.make_async_copy(source, target, sems.at[parts + i]))
    for copy in copies:
        copy.start()

    wanted = (0, 1, cols - 2, cols - 1)
    k = lax.broadcasted_iota(jnp.int32, (8, cols), 0)
    lane = lanes_of((8, cols))
    pick = jnp.zeros((8, cols), F32)
    for i, c in enumerate(wanted):
        pick = jnp.where((k == i) & (lane == c), 1.0, pick)
    pick = pick.astype(BF16)
    per = cols // rows
    for v in range(nvar):
        if v % each == 0:
            copies[v // each].wait()
        column = x_ref[v].astype(F32)
        for r in range(0, rows, 8):
            xf[pl.ds(r * nvar + v, 8, stride=nvar), :] = column[r : r + 8]
    flat = x_ref[...].reshape(nvar * rows, cols)
    taken = lax.dot_general(pick, flat, (((1,), (1,)), ((), ())), preferred_element_type=F32)
    for v in range(nvar):
        part = taken[:, (v // per) * cols : (v // per + 1) * cols]
        shift = (2 - (v % per) * rows) % cols
        stage[8 * v : 8 * v + 8, :] = pltpu.roll(part, shift, 1)
    for i in range(len(wanted)):
        own_ref[i * nvar : (i + 1) * nvar, :] = stage[pl.ds(i, nvar, stride=8), :]
    ones = jnp.ones((PAD, cols), F32)

    def fill(r, carry):
        row = xf[pl.ds(pl.multiple_of(r * nvar, 8), nvar), :]
        tap = jnp.concatenate([row, pltpu.roll(row, 1, 1), pltpu.roll(row, cols - 1, 1), ones], axis=0)
        at = pl.multiple_of(r * block, 16)
        taps_ref[pl.ds(at, block), :] = tap.astype(BF16)
        return carry

    lax.fori_loop(0, rows, fill, 0, unroll=8)

    for copy in copies[parts:]:
        copy.wait()
    packed_ref[...] = packed_rows(conv_ref[...], bias_ref[...], nvar).astype(BF16)
    half_ref[...] = (out_ref[...].astype(F32) * 0.5).astype(BF16)
    index = index_ref[...]
    row = index // cols % rows
    var = index // (rows * cols)
    spot = jnp.clip(row * nvar + var, 0, rows * nvar - 1)
    place = (index % cols).astype(F32)
    for i in range(fold):
        spot_refs[i][...] = spot[i : i + 1, :]
        across = jnp.broadcast_to(place[i : i + 1, :], (cols, cols)).T
        hot = across == lanes_of((cols, cols)).astype(F32)
        chosen_ref[i * cols : (i + 1) * cols, :] = jnp.where(hot, 1.0, 0.0).astype(BF16)
    slot = lanes_of((fold, cols)) + cols * lax.broadcasted_iota(jnp.int32, (fold, cols), 0)
    live = jnp.where(slot < count_ref[0, 0], weight_ref[...], 0.0)
    member = lax.axis_index("ens")
    extra_ref[...] = jnp.where(member == 0, value_ref[...], jnp.where(member == 1, live, 0.0))


def spread(x, conv_weight, conv_bias, out_weight, index, count, value, weight):
    nvar, rows, cols = x.shape
    fold, hid = index.shape[0], conv_bias.shape[0]
    block = 3 * nvar + PAD
    args = (x, conv_weight, conv_bias[None], out_weight.T, index, count, value, weight)
    shape = jax.ShapeDtypeStruct
    scratch = [pltpu.VMEM(arg.shape, arg.dtype) for arg in args]
    del scratch[5]
    in_specs = [pl.BlockSpec(memory_space=pltpu.HBM)] * len(args)
    in_specs[5] = pl.BlockSpec(memory_space=pltpu.SMEM)
    placed = [pltpu.with_memory_space_constraint(arg, pltpu.HBM) for arg in args]
    placed[5] = count
    return pl.pallas_call(
        spread_kernel,
        out_shape=(
            shape((rows * block, cols), BF16),
            shape((4 * nvar, cols), F32),
            shape((hid, 3 * block), BF16),
            shape((nvar, hid), BF16),
            shape((fold, cols), F32),
            shape((fold * cols, cols), BF16),
        )
        + (shape((1, cols), jnp.int32),) * fold,
        in_specs=in_specs,
        scratch_shapes=scratch
        + [
            pltpu.VMEM((8 * nvar, cols), F32),
            pltpu.VMEM((nvar * rows, cols), F32),
            pltpu.SemaphoreType.DMA((most_of(nvar, 4) + len(args) - 2,)),
        ],
        compiler_params=pltpu.CompilerParams(vmem_limit_bytes=SMALL),
        cost_estimate=pl.CostEstimate(flops=10**8, bytes_accessed=4 * 10**6, transcendentals=0),
        name="spread",
    )(*placed)


def bands(near_ref, far_ref):
    even = lax.axis_index("lat") % 2 == 0
    near, far = near_ref[...].astype(F32), far_ref[...].astype(F32)
    return jnp.where(even, far, near), jnp.where(even, near, far)


def edge_columns(own, near, far, rows):
    nvar, cols = own.shape[0] // 4, own.shape[1]
    wanted = (0, 1, cols - 2, cols - 1)

    def kernel(own_ref, near_ref, far_ref, left_ref, right_ref, between_ref, within_ref):
        lane = lanes_of((nvar, cols))
        halo = []
        for band, first in zip(bands(near_ref, far_ref), (0, rows + 2)):
            for i in range(2):
                halo.append((first + i, band[i * nvar : (i + 1) * nvar, :]))
        outs = []
        for i, c in enumerate(wanted):
            column = own_ref[i * nvar : (i + 1) * nvar, :]
            column = jnp.where(lane < rows + 2, column, 0.0)
            for at, row in halo:
                column = jnp.where(lane == at, pltpu.roll(row, (at - c) % cols, 1), column)
            outs.append(column)
        left, right = jnp.concatenate(outs[:2], axis=0), jnp.concatenate(outs[2:], axis=0)
        even = lax.axis_index("lon") % 2 == 0
        left_ref[...] = left.astype(BF16)
        right_ref[...] = right.astype(BF16)
        between_ref[...] = jnp.where(even, left, right).astype(BF16)
        within_ref[...] = jnp.where(even, right, left).astype(BF16)

    out = jax.ShapeDtypeStruct((2 * nvar, cols), BF16)
    return pl.pallas_call(
        kernel,
        out_shape=(out,) * 4,
        compiler_params=pltpu.CompilerParams(vmem_limit_bytes=SMALL),
        name="edge_columns",
    )(own, near, far)


def gelu2(pre):
    pre = pre.astype(BF16)
    inner = pre * (jnp.asarray(GELU_A, BF16) + jnp.asarray(GELU_B, BF16) * (pre * pre))
    return pre + pre * jnp.tanh(inner)


def forecast_kernel(
    fold,
    *refs,
):
    spot_refs = refs[:fold]
    (
    taps_ref,
    near_ref,
    far_ref,
    own_left_ref,
    own_right_ref,
    between_ref,
    within_ref,
    conv_ref,
    out_w_ref,
    chosen_ref,
    extra_ref,
    forecast_ref,
    notes_ref,
    first,
    second,
    final,
    hidden,
    seen,
    conv,
    out_w,
    ) = refs[fold:]
    nvar, cols = near_ref.shape[0] // 2, near_ref.shape[1]
    block = 3 * nvar + PAD
    rows = taps_ref.shape[0] // block
    deep = 3 * block
    lane = lanes_of((nvar, cols))
    ones = jnp.ones((PAD, cols), F32)

    def tap_rows(row, west, east, at):
        left = jnp.where(lane == 0, pltpu.roll(west, (cols - at) % cols, 1), pltpu.roll(row, 1, 1))
        right = jnp.where(
            lane == cols - 1, pltpu.roll(east, (2 * cols - 1 - at) % cols, 1), pltpu.roll(row, cols - 1, 1)
        )
        return jnp.concatenate([row, left, right, ones], axis=0).astype(BF16)

    def hidden_of(patches):
        return gelu2(jnp.dot(conv[...], patches, preferred_element_type=F32))

    def moved(centre, hidden):
        change = jnp.dot(out_w[...], hidden, preferred_element_type=F32)
        return (centre + change).astype(BF16).astype(F32)

    conv[...] = conv_ref[...]
    out_w[...] = out_w_ref[...]
    even = lax.axis_index("lon") % 2 == 0
    between = between_ref[...].astype(F32)
    within = within_ref[...].astype(F32)
    from_left = jnp.where(even, between, within)
    from_right = jnp.where(even, within, between)
    own_left = own_left_ref[...].astype(F32)
    own_right = own_right_ref[...].astype(F32)
    far_west, west = from_left[:nvar], from_left[nvar:]
    east, far_east = from_right[:nvar], from_right[nvar:]
    inner_west, inner_east = own_left[:nvar], own_right[nvar:]

    for band, start in zip(bands(near_ref, far_ref), (0, rows + 2)):
        for i in range(2):
            row = band[i * nvar : (i + 1) * nvar, :]
            first[(start + i) * block : (start + i + 1) * block, :] = tap_rows(row, west, east, start + i)

    group = lax.broadcasted_iota(jnp.int32, (block, cols), 0)
    wide = lanes_of((block, cols))
    is_left = (group >= nvar) & (group < 2 * nvar) & (wide == 0)
    is_right = (group >= 2 * nvar) & (group < 3 * nvar) & (wide == cols - 1)
    fix = jnp.where(is_left | is_right, 1.0, 0.0).astype(BF16) > 0
    nothing = jnp.zeros((nvar, cols), F32)
    source = jnp.concatenate([nothing, west, pltpu.roll(east, cols - 1, 1), jnp.zeros((PAD, cols), F32)], axis=0)
    source = source.astype(BF16)

    def fill(r, carry):
        at = pl.multiple_of(r * block, 16)
        mine = pltpu.roll(source, cols - 2 - r, 1)
        to = pl.multiple_of((r + 2) * block, 16)
        first[pl.ds(to, block), :] = jnp.where(fix, mine, taps_ref[pl.ds(at, block), :])
        return carry

    lax.fori_loop(0, rows, fill, 0, unroll=4)

    sides = []
    for mid, low, high in ((west, far_west, inner_west), (east, inner_east, far_east)):
        stack = []
        for a in range(3):
            for entry in (mid, low, high):
                stack.append(pltpu.roll(entry, (1 - a) % cols, 1) if a != 1 else entry)
            stack.append(ones)
        sides.append(jnp.concatenate(stack, axis=0).astype(BF16))
    patches = jnp.concatenate(sides, axis=1)
    beside = moved(jnp.concatenate([west, east], axis=1), hidden_of(patches))
    here = lax.axis_index("lat")
    north_in = (here > 0).astype(jnp.int32)
    south_in = (here < lax.axis_size("lat") - 1).astype(jnp.int32)
    keep = jnp.where(lane == 1, north_in, jnp.where(lane == rows + 2, south_in, 1)) > 0
    mid_west = jnp.where(keep, beside[:, :cols], 0.0)
    mid_east = jnp.where(keep, beside[:, cols:], 0.0)

    def ahead(source, at, slot):
        at = pl.multiple_of(at * block, 16)
        patches = jnp.concatenate(
            [source[pl.ds(at, deep), :], source[pl.ds(at + block, deep), :]], axis=1
        )
        hidden[slot] = hidden_of(patches)

    def finish(source, at, slot):
        at = pl.multiple_of(at * block, 16)
        centre = jnp.concatenate(
            [source[pl.ds(at + block, nvar), :], source[pl.ds(at + 2 * block, nvar), :]], axis=1
        ).astype(F32)
        return moved(centre, hidden[slot])

    def first_step(g, carry):
        for q in range(group1):
            ahead(first, 2 * (g * group1 + q), q)
        for q in range(group1):
            i = g * group1 + q
            both = finish(first, 2 * i, q)
            for half in range(2):
                m = 2 * i + half
                good = (jnp.where(m == 0, north_in, 1) * jnp.where(m == rows + 1, south_in, 1)) > 0
                row = both[:, half * cols : (half + 1) * cols]
                row = jnp.where(good, row, 0.0)
                at = pl.multiple_of(m * block, 16)
                second[pl.ds(at, block), :] = tap_rows(row, mid_west, mid_east, m + 1)
        return carry

    group1 = most_of(rows // 2 + 1, hidden.shape[0])
    lax.fori_loop(0, (rows // 2 + 1) // group1, first_step, 0)

    def second_step(g, carry):
        for q in range(group2):
            ahead(second, 2 * (g * group2 + q), q)
        for q in range(group2):
            j = g * group2 + q
            both = finish(second, 2 * j, q)
            both = jnp.concatenate([both[:, :cols], both[:, cols:]], axis=0)
            at = pl.multiple_of(j * 2 * nvar, 16)
            final[pl.ds(at, 2 * nvar), :] = both
            forecast_ref[pl.ds(at, 2 * nvar), :] = both.astype(BF16)
        return carry

    group2 = most_of(rows // 2, hidden.shape[0])
    lax.fori_loop(0, (rows // 2) // group2, second_step, 0)

    for half in range(fold):

        def look(o, carry, half=half):
            seen[pl.ds(half * cols + o, 1), :] = final[pl.ds(spot_refs[half][0, o], 1), :]
            return carry

        lax.fori_loop(0, cols, look, 0, unroll=32)
    masked = seen[...].astype(BF16) * chosen_ref[...]
    values = lax.dot_general(
        jnp.ones((8, cols), BF16), masked, (((1,), (1,)), ((), ())), preferred_element_type=F32
    )
    note = [values[0:1, i * cols : (i + 1) * cols] for i in range(fold)] + [extra_ref[...]]
    note = jnp.concatenate(note, axis=0).astype(BF16)
    for d in range(notes_ref.shape[0]):
        notes_ref[d] = note


def run_forecast(spot, taps, near, far, own_left, own_right, between, within, conv, out_w, chosen, extra, devices):
    nvar, cols = near.shape[0] // 2, near.shape[1]
    slots = len(spot) * cols
    block = 3 * nvar + PAD
    rows = taps.shape[0] // block
    smem = pl.BlockSpec(memory_space=pltpu.SMEM)
    vmem = pl.BlockSpec(memory_space=pltpu.VMEM)
    return pl.pallas_call(
        functools.partial(forecast_kernel, len(spot)),
        out_shape=(
            jax.ShapeDtypeStruct((rows * nvar, cols), BF16),
            jax.ShapeDtypeStruct((devices, 2 * extra.shape[0], cols), BF16),
        ),
        in_specs=[smem] * len(spot) + [vmem] * 11,
        out_specs=(vmem, vmem),
        scratch_shapes=[
            pltpu.VMEM(((rows + 4) * block, cols), BF16),
            pltpu.VMEM(((rows + 2) * block, cols), BF16),
            pltpu.VMEM((rows * nvar, cols), F32),
            pltpu.VMEM((GROUP, conv.shape[0], 2 * cols), BF16),
            pltpu.VMEM((slots, cols), F32),
            pltpu.VMEM(conv.shape, BF16),
            pltpu.VMEM(out_w.shape, BF16),
        ],
        compiler_params=pltpu.CompilerParams(vmem_limit_bytes=24 << 20),
        name="forecast",
    )(*spot, taps, near, far, own_left, own_right, between, within, conv, out_w, chosen, extra)


def pair_weights(gram, proj):
    count = len(proj)
    system = [[gram[k][m] + (float(count - 1) if k == m else 0.0) for m in range(count)] for k in range(count)]
    total = sum(entry * entry for line in system for entry in line)
    scale = jnp.sqrt(total)
    one = jnp.ones_like(scale)
    eye = [[one if k == m else 0.0 * one for m in range(count)] for k in range(count)]

    def times(left, right):
        return [
            [sum(left[k][j] * right[j][m] for j in range(count)) for m in range(count)] for k in range(count)
        ]

    current = [[entry / scale for entry in line] for line in system]
    inverse = eye
    for _ in range(NS_ITERS):
        both = times(inverse, current)
        factor = [[1.5 * eye[k][m] - 0.5 * both[k][m] for m in range(count)] for k in range(count)]
        current = times(current, factor)
        inverse = times(factor, inverse)
    root = jnp.sqrt(scale)
    root_inv = [[entry / root for entry in line] for line in inverse]
    half = [sum(root_inv[k][j] * proj[j] for j in range(count)) for k in range(count)]
    mean_w = [sum(root_inv[k][j] * half[j] for j in range(count)) for k in range(count)]
    span = math.sqrt(count - 1.0)
    full = [[mean_w[k] + span * root_inv[k][m] for m in range(count)] for k in range(count)]
    centre = [sum(full[k][m] for k in range(count)) / count for m in range(count)]
    return [[1.0 / count + full[k][m] - centre[m] for m in range(count)] for k in range(count)]


def analysis_kernel(told_ref, mine_ref, other_ref, out_ref, blended, packed, sems):
    count = lax.axis_size("ens")
    nvar, rows, cols = packed.shape[1], out_ref.shape[1], packed.shape[3]
    depth = told_ref.shape[1]
    told = told_ref[...].astype(F32).reshape(count, -1, cols)
    fold = depth // 2
    size = told.shape[1]
    hx = [told[k] for k in range(count)]
    value = pltpu.roll(told[0], size - fold, 0)
    weight = pltpu.roll(told[1], size - fold, 0)
    used = lax.broadcasted_iota(jnp.int32, (size, cols), 0) % depth < fold
    weight = jnp.where(used, weight, 0.0)
    mean = sum(hx) / count
    spread_of = [h - mean for h in hx]
    innov = value - mean
    tile = (8, cols)

    def total(term):
        return jnp.broadcast_to(jnp.sum(term, keepdims=True), tile)

    scaled = [part * weight for part in spread_of]
    gram = [[None] * count for _ in range(count)]
    for k in range(count):
        for m in range(k, count):
            gram[k][m] = gram[m][k] = total(scaled[k] * spread_of[m])
    weights = pair_weights(gram, [total(scaled[k] * innov) for k in range(count)])
    me = lax.axis_index("ens")
    mine = jnp.where(me == 0, weights[0][0], weights[1][1])[0:1, :]
    other = jnp.where(me == 0, weights[1][0], weights[0][1])[0:1, :]
    high = packed.shape[2]

    def copy_of(c):
        return pltpu.make_async_copy(packed.at[c], out_ref.at[:, pl.ds(c * high, high), :], sems.at[c])

    for c in range(rows // high):
        at = c * high * nvar
        part = slice(at, at + high * nvar)
        blended[c] = mine * mine_ref[part, :].astype(F32) + other * other_ref[part, :].astype(F32)
        for v in range(nvar):
            for r in range(0, high, 16):
                halves = [blended[c, pl.ds((r + 8 * i) * nvar + v, 8, stride=nvar), :] for i in range(2)]
                packed[c, v, r : r + 16, :] = jnp.concatenate(halves, axis=0).astype(BF16)
        copy_of(c).start()
    for c in range(rows // high):
        copy_of(c).wait()


def run_analysis(told, mine, other, shape):
    nvar, rows, cols = shape
    high = 16
    vmem = pl.BlockSpec(memory_space=pltpu.VMEM)
    return pl.pallas_call(
        analysis_kernel,
        out_shape=jax.ShapeDtypeStruct(shape, BF16),
        in_specs=[vmem, vmem, vmem],
        out_specs=pl.BlockSpec(memory_space=pltpu.HBM),
        scratch_shapes=[
            pltpu.VMEM((rows // high, high * nvar, cols), F32),
            pltpu.VMEM((rows // high, nvar, high, cols), BF16),
            pltpu.SemaphoreType.DMA((rows // high,)),
        ],
        compiler_params=pltpu.CompilerParams(vmem_limit_bytes=8 << 20),
        name="analysis",
    )(told, mine, other)


def blend_weights(gram, proj):
    entries_number = gram.shape[0]
    eye = jnp.eye(entries_number, dtype=gram.dtype)
    system = (entries_number - 1) * eye + gram
    scale = jnp.sqrt(jnp.sum(system * system))
    current = system / scale
    inverse = eye
    for _ in range(NS_ITERS):
        factor = 1.5 * eye - 0.5 * jnp.dot(inverse, current, precision=lax.Precision.HIGHEST)
        current = jnp.dot(current, factor, precision=lax.Precision.HIGHEST)
        inverse = jnp.dot(factor, inverse, precision=lax.Precision.HIGHEST)
    root_inv = inverse / jnp.sqrt(scale)
    half = jnp.dot(root_inv, proj, precision=lax.Precision.HIGHEST)
    mean_w = jnp.dot(root_inv, half, precision=lax.Precision.HIGHEST)
    full = mean_w[:, None] + math.sqrt(entries_number - 1.0) * root_inv
    return 1.0 / entries_number + full - jnp.mean(full, axis=0, keepdims=True)


def many_members(told, forecast, shape):
    nvar, rows, cols = shape
    fold = told.shape[1] // 2
    told = told.astype(F32).reshape(lax.axis_size("ens"), -1, *told.shape[1:])
    members = told[:, :, :fold, :].reshape(told.shape[0], -1)
    value = told[0, :, fold:, :].reshape(-1)
    weight = told[1, :, fold:, :].reshape(-1)
    mean = jnp.mean(members, axis=0)
    spread = members - mean[None, :]
    innov = value - mean
    weighted = spread * weight[None, :]
    gram = jnp.dot(weighted, spread.T, precision=lax.Precision.HIGHEST)
    proj = jnp.dot(weighted, innov, precision=lax.Precision.HIGHEST)
    transform = blend_weights(gram, proj)
    column = lax.dynamic_slice_in_dim(transform, lax.axis_index("ens"), 1, 1)[:, 0]
    everyone = lax.all_gather(forecast[None], "ens", axis=0, tiled=True)
    blended = jnp.tensordot(column, everyone.astype(F32), axes=1, precision=lax.Precision.HIGHEST)
    return blended.astype(BF16).reshape(rows, nvar, cols).transpose(1, 0, 2)


def per_device(
    sample_quantities,
    conv_weight,
    conv_bias,
    out_weight,
    obs_index,
    obs_count,
    obs_value,
    obs_weight,
):
    x = sample_quantities[0]
    _, rows, cols = x.shape
    n_ens, n_lat, n_lon = (lax.axis_size(axis) for axis in ("ens", "lat", "lon"))
    assert n_lon % 2 == 0
    first_bands = [(i, i + 1) for i in range(0, n_lat - 1, 2)]
    second_bands = [(i, i + 1) for i in range(1, n_lat - 1, 2)]
    odd_pairs = [(i, (i + 1) % n_lon) for i in range(1, n_lon, 2)]
    even_pairs = [(i, i + 1) for i in range(0, n_lon, 2)]

    near_rows, far_rows = edge_rows(x)
    near = lax.ppermute(near_rows, "lat", first_bands + [(j, i) for i, j in first_bands])
    far = lax.ppermute(far_rows, "lat", second_bands + [(j, i) for i, j in second_bands])
    fold = (obs_index.size // cols, cols)
    taps, own, conv, out_w, extra, chosen, *spot = spread(
        x,
        conv_weight,
        conv_bias,
        out_weight,
        obs_index.reshape(fold),
        obs_count,
        obs_value.reshape(fold),
        obs_weight.reshape(fold),
    )
    own_left, own_right, outer, inner = edge_columns(own, near, far, rows)
    between = lax.ppermute(outer, "lon", odd_pairs + [(j, i) for i, j in odd_pairs])
    within = lax.ppermute(inner, "lon", even_pairs + [(j, i) for i, j in even_pairs])
    forecast, notes = run_forecast(
        spot,
        taps,
        near,
        far,
        own_left,
        own_right,
        between,
        within,
        conv,
        out_w,
        chosen,
        extra,
        n_ens * n_lat * n_lon,
    )
    told = lax.all_to_all(notes, ("ens", "lat", "lon"), 0, 0, tiled=True)
    if n_ens == 2:
        other = lax.ppermute(forecast, "ens", [(0, 1), (1, 0)])
        return run_analysis(told, forecast, other, x.shape)[None]
    return many_members(told, forecast, x.shape)[None]


def solution(mesh):
    return jax.shard_map(
        per_device,
        mesh=mesh,
        in_specs=(
            P("ens", None, "lat", "lon"),
            P(),
            P(),
            P(),
            P("lat", "lon", None),
            P("lat", "lon"),
            P("lat", "lon", None),
            P("lat", "lon", None),
        ),
        out_specs=P("ens", None, "lat", "lon"),
        check_vma=False,
    )
```

```python
import functools
import math

import jax
import jax.numpy as jnp
from jax import lax
from jax.experimental import pallas as pl
from jax.experimental.pallas import tpu as pltpu
from jax.sharding import PartitionSpec as P

NS_ITERS = 20
GELU_A = math.sqrt(2.0 / math.pi)
GELU_B = GELU_A * 0.044715
F32 = jnp.float32
BF16 = jnp.bfloat16
PAD = 8
SMALL = 4 << 20
GROUP = 34


def lanes_of(shape):
    return lax.broadcasted_iota(jnp.int32, shape, len(shape) - 1)


def most_of(total, limit):
    return max(d for d in range(1, limit + 1) if total % d == 0)


def edge_rows(x):
    nvar, rows, cols = x.shape
    tile = 8

    def kernel(x_ref, near_ref, far_ref, part, stage, sems):
        copies = []
        for i, first in enumerate((0, rows - tile)):
            copies.append(pltpu.make_async_copy(x_ref.at[:, first : first + tile, :], part.at[i], sems.at[i]))
            copies[i].start()
        ends = []
        for i, first in enumerate((0, tile - 2)):
            copies[i].wait()
            stage[...] = part[i].reshape(nvar * tile, cols).astype(F32)
            both = [stage[pl.ds(first + j, nvar, stride=tile), :] for j in range(2)]
            ends.append(jnp.concatenate(both, axis=0))
        even = lax.axis_index("lat") % 2 == 0
        near_ref[...] = jnp.where(even, ends[1], ends[0]).astype(BF16)
        far_ref[...] = jnp.where(even, ends[0], ends[1]).astype(BF16)

    out = jax.ShapeDtypeStruct((2 * nvar, cols), BF16)
    return pl.pallas_call(
        kernel,
        out_shape=(out, out),
        in_specs=[pl.BlockSpec(memory_space=pltpu.HBM)],
        scratch_shapes=[
            pltpu.VMEM((2, nvar, tile, cols), BF16),
            pltpu.VMEM((nvar * tile, cols), F32),
            pltpu.SemaphoreType.DMA((2,)),
        ],
        compiler_params=pltpu.CompilerParams(vmem_limit_bytes=SMALL),
        name="edge_rows",
    )(pltpu.with_memory_space_constraint(x, pltpu.HBM))


def packed_rows(conv, bias, nvar):
    hid = bias.shape[1]
    high = bias.astype(BF16).astype(F32)
    middle = (bias - high).astype(BF16).astype(F32)
    low = (bias - high - middle).astype(BF16).astype(F32)
    rest = jnp.zeros((PAD - 3, hid), F32)
    pieces = []
    for a in range(3):
        for b in (1, 0, 2):
            at = (3 * a + b) * nvar
            pieces.append(conv[at : at + nvar, :].astype(F32))
        if a == 1:
            pieces.append(jnp.concatenate([high, middle, low, rest], axis=0))
        else:
            pieces.append(jnp.zeros((PAD, hid), F32))
    return jnp.concatenate(pieces, axis=0).T


def outer_kernel(count_ref, x_hbm, x_ref, own_ref, told_ref, stage, sem):
    nvar, rows, cols = x_ref.shape
    copy = pltpu.make_async_copy(x_hbm, x_ref, sem)
    copy.start()
    told_ref[...] = jnp.full(told_ref.shape, count_ref[0, 0], jnp.int32)
    wanted = (0, 1, cols - 2, cols - 1)
    k = lax.broadcasted_iota(jnp.int32, (8, cols), 0)
    lane = lanes_of((8, cols))
    pick = jnp.zeros((8, cols), F32)
    for i, c in enumerate(wanted):
        pick = jnp.where((k == i) & (lane == c), 1.0, pick)
    pick = pick.astype(BF16)
    per = cols // rows
    copy.wait()
    flat = x_ref[...].reshape(nvar * rows, cols)
    taken = lax.dot_general(pick, flat, (((1,), (1,)), ((), ())), preferred_element_type=F32)
    for v in range(nvar):
        part = taken[:, (v // per) * cols : (v // per + 1) * cols]
        shift = (2 - (v % per) * rows) % cols
        stage[8 * v : 8 * v + 8, :] = pltpu.roll(part, shift, 1)
    for i in range(len(wanted)):
        own_ref[i * nvar : (i + 1) * nvar, :] = stage[pl.ds(i, nvar, stride=8), :]


def outer_columns(x, count):
    nvar, _, cols = x.shape
    return pl.pallas_call(
        outer_kernel,
        out_shape=(
            jax.ShapeDtypeStruct(x.shape, BF16),
            jax.ShapeDtypeStruct((4 * nvar, cols), F32),
            jax.ShapeDtypeStruct((8, cols), jnp.int32),
        ),
        in_specs=[pl.BlockSpec(memory_space=pltpu.SMEM), pl.BlockSpec(memory_space=pltpu.HBM)],
        scratch_shapes=[pltpu.VMEM((8 * nvar, cols), F32), pltpu.SemaphoreType.DMA],
        compiler_params=pltpu.CompilerParams(vmem_limit_bytes=SMALL),
        cost_estimate=pl.CostEstimate(flops=10**7, bytes_accessed=2 * 10**6, transcendentals=0),
        name="outer_columns",
    )(count, pltpu.with_memory_space_constraint(x, pltpu.HBM))


def spread_kernel(
    x_ref,
    conv_hbm,
    bias_hbm,
    out_hbm,
    index_hbm,
    count_ref,
    value_hbm,
    weight_hbm,
    taps_ref,
    packed_ref,
    half_ref,
    extra_ref,
    chosen_ref,
    *rest,
):
    fold = extra_ref.shape[0]
    spot_refs = rest[:fold]
    conv_ref, bias_ref, out_ref, index_ref, value_ref, weight_ref, xf, sems = rest[fold:]
    nvar, rows, cols = x_ref.shape
    block = 3 * nvar + PAD
    small = [
        (conv_hbm, conv_ref),
        (bias_hbm, bias_ref),
        (out_hbm, out_ref),
        (index_hbm, index_ref),
        (value_hbm, value_ref),
        (weight_hbm, weight_ref),
    ]
    copies = []
    for i, (source, target) in enumerate(small):
        copies.append(pltpu.make_async_copy(source, target, sems.at[i]))
        copies[i].start()
    for v in range(nvar):
        column = x_ref[v].astype(F32)
        for r in range(0, rows, 8):
            xf[pl.ds(r * nvar + v, 8, stride=nvar), :] = column[r : r + 8]
    ones = jnp.ones((PAD, cols), F32)

    def fill(r, carry):
        row = xf[pl.ds(pl.multiple_of(r * nvar, 8), nvar), :]
        tap = jnp.concatenate([row, pltpu.roll(row, 1, 1), pltpu.roll(row, cols - 1, 1), ones], axis=0)
        at = pl.multiple_of(r * block, 16)
        taps_ref[pl.ds(at, block), :] = tap.astype(BF16)
        return carry

    lax.fori_loop(0, rows, fill, 0, unroll=8)

    for copy in copies:
        copy.wait()
    packed_ref[...] = packed_rows(conv_ref[...], bias_ref[...], nvar).astype(BF16)
    half_ref[...] = (out_ref[...].astype(F32) * 0.5).astype(BF16)
    index = index_ref[...]
    row = index // cols % rows
    var = index // (rows * cols)
    spot = jnp.clip(row * nvar + var, 0, rows * nvar - 1)
    place = (index % cols).astype(F32)
    for i in range(fold):
        spot_refs[i][...] = spot[i : i + 1, :]
        across = jnp.broadcast_to(place[i : i + 1, :], (cols, cols)).T
        hot = across == lanes_of((cols, cols)).astype(F32)
        chosen_ref[i * cols : (i + 1) * cols, :] = jnp.where(hot, 1.0, 0.0).astype(BF16)
    slot = lanes_of((fold, cols)) + cols * lax.broadcasted_iota(jnp.int32, (fold, cols), 0)
    live = jnp.where(slot < count_ref[0:1, :], weight_ref[...], 0.0)
    member = lax.axis_index("ens")
    extra_ref[...] = jnp.where(member == 0, value_ref[...], jnp.where(member == 1, live, 0.0))


def spread(x, conv_weight, conv_bias, out_weight, index, count, value, weight):
    nvar, rows, cols = x.shape
    fold, hid = index.shape[0], conv_bias.shape[0]
    block = 3 * nvar + PAD
    args = (x, conv_weight, conv_bias[None], out_weight.T, index, count, value, weight)
    shape = jax.ShapeDtypeStruct
    scratch = [pltpu.VMEM(arg.shape, arg.dtype) for arg in args[1:5] + args[6:]]
    in_specs = [pl.BlockSpec(memory_space=pltpu.HBM)] * len(args)
    in_specs[0] = pl.BlockSpec(memory_space=pltpu.VMEM)
    in_specs[5] = pl.BlockSpec(memory_space=pltpu.VMEM)
    placed = [pltpu.with_memory_space_constraint(arg, pltpu.HBM) for arg in args]
    placed[0], placed[5] = x, count
    return pl.pallas_call(
        spread_kernel,
        out_shape=(
            shape((rows * block, cols), BF16),
            shape((hid, 3 * block), BF16),
            shape((nvar, hid), BF16),
            shape((fold, cols), F32),
            shape((fold * cols, cols), BF16),
        )
        + (shape((1, cols), jnp.int32),) * fold,
        in_specs=in_specs,
        scratch_shapes=scratch
        + [
            pltpu.VMEM((nvar * rows, cols), F32),
            pltpu.SemaphoreType.DMA((len(args) - 2,)),
        ],
        compiler_params=pltpu.CompilerParams(vmem_limit_bytes=SMALL),
        cost_estimate=pl.CostEstimate(flops=10**8, bytes_accessed=4 * 10**6, transcendentals=0),
        name="spread",
    )(*placed)


def bands(near_ref, far_ref):
    even = lax.axis_index("lat") % 2 == 0
    near, far = near_ref[...].astype(F32), far_ref[...].astype(F32)
    return jnp.where(even, far, near), jnp.where(even, near, far)


def edge_columns(own, near, far, rows):
    nvar, cols = own.shape[0] // 4, own.shape[1]
    wanted = (0, 1, cols - 2, cols - 1)

    def kernel(own_ref, near_ref, far_ref, left_ref, right_ref, between_ref, within_ref):
        lane = lanes_of((nvar, cols))
        halo = []
        for band, first in zip(bands(near_ref, far_ref), (0, rows + 2)):
            for i in range(2):
                halo.append((first + i, band[i * nvar : (i + 1) * nvar, :]))
        outs = []
        for i, c in enumerate(wanted):
            column = own_ref[i * nvar : (i + 1) * nvar, :]
            column = jnp.where(lane < rows + 2, column, 0.0)
            for at, row in halo:
                column = jnp.where(lane == at, pltpu.roll(row, (at - c) % cols, 1), column)
            outs.append(column)
        left, right = jnp.concatenate(outs[:2], axis=0), jnp.concatenate(outs[2:], axis=0)
        even = lax.axis_index("lon") % 2 == 0
        left_ref[...] = left.astype(BF16)
        right_ref[...] = right.astype(BF16)
        between_ref[...] = jnp.where(even, left, right).astype(BF16)
        within_ref[...] = jnp.where(even, right, left).astype(BF16)

    out = jax.ShapeDtypeStruct((2 * nvar, cols), BF16)
    return pl.pallas_call(
        kernel,
        out_shape=(out,) * 4,
        compiler_params=pltpu.CompilerParams(vmem_limit_bytes=SMALL),
        name="edge_columns",
    )(own, near, far)


def gelu2(pre):
    pre = pre.astype(BF16)
    inner = pre * (jnp.asarray(GELU_A, BF16) + jnp.asarray(GELU_B, BF16) * (pre * pre))
    return pre + pre * jnp.tanh(inner)


def forecast_kernel(
    fold,
    *refs,
):
    spot_refs = refs[:fold]
    (
    taps_ref,
    near_ref,
    far_ref,
    own_left_ref,
    own_right_ref,
    between_ref,
    within_ref,
    conv_ref,
    out_w_ref,
    chosen_ref,
    extra_ref,
    forecast_ref,
    notes_ref,
    first,
    second,
    final,
    hidden,
    seen,
    conv,
    out_w,
    ) = refs[fold:]
    nvar, cols = near_ref.shape[0] // 2, near_ref.shape[1]
    block = 3 * nvar + PAD
    rows = taps_ref.shape[0] // block
    deep = 3 * block
    lane = lanes_of((nvar, cols))
    ones = jnp.ones((PAD, cols), F32)

    def tap_rows(row, west, east, at):
        left = jnp.where(lane == 0, pltpu.roll(west, (cols - at) % cols, 1), pltpu.roll(row, 1, 1))
        right = jnp.where(
            lane == cols - 1, pltpu.roll(east, (2 * cols - 1 - at) % cols, 1), pltpu.roll(row, cols - 1, 1)
        )
        return jnp.concatenate([row, left, right, ones], axis=0).astype(BF16)

    def hidden_of(patches):
        return gelu2(jnp.dot(conv[...], patches, preferred_element_type=F32))

    def moved(centre, hidden):
        change = jnp.dot(out_w[...], hidden, preferred_element_type=F32)
        return (centre + change).astype(BF16).astype(F32)

    conv[...] = conv_ref[...]
    out_w[...] = out_w_ref[...]
    even = lax.axis_index("lon") % 2 == 0
    between = between_ref[...].astype(F32)
    within = within_ref[...].astype(F32)
    from_left = jnp.where(even, between, within)
    from_right = jnp.where(even, within, between)
    own_left = own_left_ref[...].astype(F32)
    own_right = own_right_ref[...].astype(F32)
    far_west, west = from_left[:nvar], from_left[nvar:]
    east, far_east = from_right[:nvar], from_right[nvar:]
    inner_west, inner_east = own_left[:nvar], own_right[nvar:]

    for band, start in zip(bands(near_ref, far_ref), (0, rows + 2)):
        for i in range(2):
            row = band[i * nvar : (i + 1) * nvar, :]
            first[(start + i) * block : (start + i + 1) * block, :] = tap_rows(row, west, east, start + i)

    group = lax.broadcasted_iota(jnp.int32, (block, cols), 0)
    wide = lanes_of((block, cols))
    is_left = (group >= nvar) & (group < 2 * nvar) & (wide == 0)
    is_right = (group >= 2 * nvar) & (group < 3 * nvar) & (wide == cols - 1)
    fix = jnp.where(is_left | is_right, 1.0, 0.0).astype(BF16) > 0
    nothing = jnp.zeros((nvar, cols), F32)
    source = jnp.concatenate([nothing, west, pltpu.roll(east, cols - 1, 1), jnp.zeros((PAD, cols), F32)], axis=0)
    source = source.astype(BF16)

    def fill(r, carry):
        at = pl.multiple_of(r * block, 16)
        mine = pltpu.roll(source, cols - 2 - r, 1)
        to = pl.multiple_of((r + 2) * block, 16)
        first[pl.ds(to, block), :] = jnp.where(fix, mine, taps_ref[pl.ds(at, block), :])
        return carry

    lax.fori_loop(0, rows, fill, 0, unroll=4)

    sides = []
    for mid, low, high in ((west, far_west, inner_west), (east, inner_east, far_east)):
        stack = []
        for a in range(3):
            for entry in (mid, low, high):
                stack.append(pltpu.roll(entry, (1 - a) % cols, 1) if a != 1 else entry)
            stack.append(ones)
        sides.append(jnp.concatenate(stack, axis=0).astype(BF16))
    patches = jnp.concatenate(sides, axis=1)
    beside = moved(jnp.concatenate([west, east], axis=1), hidden_of(patches))
    here = lax.axis_index("lat")
    north_in = (here > 0).astype(jnp.int32)
    south_in = (here < lax.axis_size("lat") - 1).astype(jnp.int32)
    keep = jnp.where(lane == 1, north_in, jnp.where(lane == rows + 2, south_in, 1)) > 0
    mid_west = jnp.where(keep, beside[:, :cols], 0.0)
    mid_east = jnp.where(keep, beside[:, cols:], 0.0)

    def ahead(source, at, slot):
        at = pl.multiple_of(at * block, 16)
        patches = jnp.concatenate(
            [source[pl.ds(at, deep), :], source[pl.ds(at + block, deep), :]], axis=1
        )
        hidden[slot] = hidden_of(patches)

    def finish(source, at, slot):
        at = pl.multiple_of(at * block, 16)
        centre = jnp.concatenate(
            [source[pl.ds(at + block, nvar), :], source[pl.ds(at + 2 * block, nvar), :]], axis=1
        ).astype(F32)
        return moved(centre, hidden[slot])

    def first_step(g, carry):
        for q in range(group1):
            ahead(first, 2 * (g * group1 + q), q)
        for q in range(group1):
            i = g * group1 + q
            both = finish(first, 2 * i, q)
            for half in range(2):
                m = 2 * i + half
                good = (jnp.where(m == 0, north_in, 1) * jnp.where(m == rows + 1, south_in, 1)) > 0
                row = both[:, half * cols : (half + 1) * cols]
                row = jnp.where(good, row, 0.0)
                at = pl.multiple_of(m * block, 16)
                second[pl.ds(at, block), :] = tap_rows(row, mid_west, mid_east, m + 1)
        return carry

    group1 = most_of(rows // 2 + 1, hidden.shape[0])
    lax.fori_loop(0, (rows // 2 + 1) // group1, first_step, 0)

    def second_step(g, carry):
        for q in range(group2):
            ahead(second, 2 * (g * group2 + q), q)
        for q in range(group2):
            j = g * group2 + q
            both = finish(second, 2 * j, q)
            both = jnp.concatenate([both[:, :cols], both[:, cols:]], axis=0)
            at = pl.multiple_of(j * 2 * nvar, 16)
            final[pl.ds(at, 2 * nvar), :] = both
            forecast_ref[pl.ds(at, 2 * nvar), :] = both.astype(BF16)
        return carry

    group2 = most_of(rows // 2, hidden.shape[0])
    lax.fori_loop(0, (rows // 2) // group2, second_step, 0)

    for half in range(fold):

        def look(o, carry, half=half):
            seen[pl.ds(half * cols + o, 1), :] = final[pl.ds(spot_refs[half][0, o], 1), :]
            return carry

        lax.fori_loop(0, cols, look, 0, unroll=32)
    masked = seen[...].astype(BF16) * chosen_ref[...]
    values = lax.dot_general(
        jnp.ones((8, cols), BF16), masked, (((1,), (1,)), ((), ())), preferred_element_type=F32
    )
    note = [values[0:1, i * cols : (i + 1) * cols] for i in range(fold)] + [extra_ref[...]]
    note = jnp.concatenate(note, axis=0).astype(BF16)
    for d in range(notes_ref.shape[0]):
        notes_ref[d] = note


def run_forecast(spot, taps, near, far, own_left, own_right, between, within, conv, out_w, chosen, extra, devices):
    nvar, cols = near.shape[0] // 2, near.shape[1]
    slots = len(spot) * cols
    block = 3 * nvar + PAD
    rows = taps.shape[0] // block
    smem = pl.BlockSpec(memory_space=pltpu.SMEM)
    vmem = pl.BlockSpec(memory_space=pltpu.VMEM)
    return pl.pallas_call(
        functools.partial(forecast_kernel, len(spot)),
        out_shape=(
            jax.ShapeDtypeStruct((rows * nvar, cols), BF16),
            jax.ShapeDtypeStruct((devices, 2 * extra.shape[0], cols), BF16),
        ),
        in_specs=[smem] * len(spot) + [vmem] * 11,
        out_specs=(vmem, vmem),
        scratch_shapes=[
            pltpu.VMEM(((rows + 4) * block, cols), BF16),
            pltpu.VMEM(((rows + 2) * block, cols), BF16),
            pltpu.VMEM((rows * nvar, cols), F32),
            pltpu.VMEM((GROUP, conv.shape[0], 2 * cols), BF16),
            pltpu.VMEM((slots, cols), F32),
            pltpu.VMEM(conv.shape, BF16),
            pltpu.VMEM(out_w.shape, BF16),
        ],
        compiler_params=pltpu.CompilerParams(vmem_limit_bytes=24 << 20),
        name="forecast",
    )(*spot, taps, near, far, own_left, own_right, between, within, conv, out_w, chosen, extra)


def pair_weights(gram, proj):
    count = len(proj)
    system = [[gram[k][m] + (float(count - 1) if k == m else 0.0) for m in range(count)] for k in range(count)]
    total = sum(entry * entry for line in system for entry in line)
    scale = jnp.sqrt(total)
    one = jnp.ones_like(scale)
    eye = [[one if k == m else 0.0 * one for m in range(count)] for k in range(count)]

    def times(left, right):
        return [
            [sum(left[k][j] * right[j][m] for j in range(count)) for m in range(count)] for k in range(count)
        ]

    current = [[entry / scale for entry in line] for line in system]
    inverse = eye
    for _ in range(NS_ITERS):
        both = times(inverse, current)
        factor = [[1.5 * eye[k][m] - 0.5 * both[k][m] for m in range(count)] for k in range(count)]
        current = times(current, factor)
        inverse = times(factor, inverse)
    root = jnp.sqrt(scale)
    root_inv = [[entry / root for entry in line] for line in inverse]
    half = [sum(root_inv[k][j] * proj[j] for j in range(count)) for k in range(count)]
    mean_w = [sum(root_inv[k][j] * half[j] for j in range(count)) for k in range(count)]
    span = math.sqrt(count - 1.0)
    full = [[mean_w[k] + span * root_inv[k][m] for m in range(count)] for k in range(count)]
    centre = [sum(full[k][m] for k in range(count)) / count for m in range(count)]
    return [[1.0 / count + full[k][m] - centre[m] for m in range(count)] for k in range(count)]


def analysis_kernel(told_ref, mine_ref, other_ref, out_ref, blended, packed, sems):
    count = lax.axis_size("ens")
    nvar, rows, cols = packed.shape[1], out_ref.shape[1], packed.shape[3]
    depth = told_ref.shape[1]
    told = told_ref[...].astype(F32).reshape(count, -1, cols)
    fold = depth // 2
    size = told.shape[1]
    hx = [told[k] for k in range(count)]
    value = pltpu.roll(told[0], size - fold, 0)
    weight = pltpu.roll(told[1], size - fold, 0)
    used = lax.broadcasted_iota(jnp.int32, (size, cols), 0) % depth < fold
    weight = jnp.where(used, weight, 0.0)
    mean = sum(hx) / count
    spread_of = [h - mean for h in hx]
    innov = value - mean
    tile = (8, cols)

    def total(term):
        return jnp.broadcast_to(jnp.sum(term, keepdims=True), tile)

    scaled = [part * weight for part in spread_of]
    gram = [[None] * count for _ in range(count)]
    for k in range(count):
        for m in range(k, count):
            gram[k][m] = gram[m][k] = total(scaled[k] * spread_of[m])
    weights = pair_weights(gram, [total(scaled[k] * innov) for k in range(count)])
    me = lax.axis_index("ens")
    mine = jnp.where(me == 0, weights[0][0], weights[1][1])[0:1, :]
    other = jnp.where(me == 0, weights[1][0], weights[0][1])[0:1, :]
    high = packed.shape[2]

    def copy_of(c):
        return pltpu.make_async_copy(packed.at[c], out_ref.at[:, pl.ds(c * high, high), :], sems.at[c])

    for c in range(rows // high):
        at = c * high * nvar
        part = slice(at, at + high * nvar)
        blended[c] = mine * mine_ref[part, :].astype(F32) + other * other_ref[part, :].astype(F32)
        for v in range(nvar):
            for r in range(0, high, 16):
                halves = [blended[c, pl.ds((r + 8 * i) * nvar + v, 8, stride=nvar), :] for i in range(2)]
                packed[c, v, r : r + 16, :] = jnp.concatenate(halves, axis=0).astype(BF16)
        copy_of(c).start()
    for c in range(rows // high):
        copy_of(c).wait()


def run_analysis(told, mine, other, shape):
    nvar, rows, cols = shape
    high = 16
    vmem = pl.BlockSpec(memory_space=pltpu.VMEM)
    return pl.pallas_call(
        analysis_kernel,
        out_shape=jax.ShapeDtypeStruct(shape, BF16),
        in_specs=[vmem, vmem, vmem],
        out_specs=pl.BlockSpec(memory_space=pltpu.HBM),
        scratch_shapes=[
            pltpu.VMEM((rows // high, high * nvar, cols), F32),
            pltpu.VMEM((rows // high, nvar, high, cols), BF16),
            pltpu.SemaphoreType.DMA((rows // high,)),
        ],
        compiler_params=pltpu.CompilerParams(vmem_limit_bytes=8 << 20),
        name="analysis",
    )(told, mine, other)


def blend_weights(gram, proj):
    entries_number = gram.shape[0]
    eye = jnp.eye(entries_number, dtype=gram.dtype)
    system = (entries_number - 1) * eye + gram
    scale = jnp.sqrt(jnp.sum(system * system))
    current = system / scale
    inverse = eye
    for _ in range(NS_ITERS):
        factor = 1.5 * eye - 0.5 * jnp.dot(inverse, current, precision=lax.Precision.HIGHEST)
        current = jnp.dot(current, factor, precision=lax.Precision.HIGHEST)
        inverse = jnp.dot(factor, inverse, precision=lax.Precision.HIGHEST)
    root_inv = inverse / jnp.sqrt(scale)
    half = jnp.dot(root_inv, proj, precision=lax.Precision.HIGHEST)
    mean_w = jnp.dot(root_inv, half, precision=lax.Precision.HIGHEST)
    full = mean_w[:, None] + math.sqrt(entries_number - 1.0) * root_inv
    return 1.0 / entries_number + full - jnp.mean(full, axis=0, keepdims=True)


def many_members(told, forecast, shape):
    nvar, rows, cols = shape
    fold = told.shape[1] // 2
    told = told.astype(F32).reshape(lax.axis_size("ens"), -1, *told.shape[1:])
    members = told[:, :, :fold, :].reshape(told.shape[0], -1)
    value = told[0, :, fold:, :].reshape(-1)
    weight = told[1, :, fold:, :].reshape(-1)
    mean = jnp.mean(members, axis=0)
    spread = members - mean[None, :]
    innov = value - mean
    weighted = spread * weight[None, :]
    gram = jnp.dot(weighted, spread.T, precision=lax.Precision.HIGHEST)
    proj = jnp.dot(weighted, innov, precision=lax.Precision.HIGHEST)
    transform = blend_weights(gram, proj)
    column = lax.dynamic_slice_in_dim(transform, lax.axis_index("ens"), 1, 1)[:, 0]
    everyone = lax.all_gather(forecast[None], "ens", axis=0, tiled=True)
    blended = jnp.tensordot(column, everyone.astype(F32), axes=1, precision=lax.Precision.HIGHEST)
    return blended.astype(BF16).reshape(rows, nvar, cols).transpose(1, 0, 2)


def per_device(
    sample_quantities,
    conv_weight,
    conv_bias,
    out_weight,
    obs_index,
    obs_count,
    obs_value,
    obs_weight,
):
    x = sample_quantities[0]
    _, rows, cols = x.shape
    n_ens, n_lat, n_lon = (lax.axis_size(axis) for axis in ("ens", "lat", "lon"))
    assert n_lon % 2 == 0
    first_bands = [(i, i + 1) for i in range(0, n_lat - 1, 2)]
    second_bands = [(i, i + 1) for i in range(1, n_lat - 1, 2)]
    odd_pairs = [(i, (i + 1) % n_lon) for i in range(1, n_lon, 2)]
    even_pairs = [(i, i + 1) for i in range(0, n_lon, 2)]

    near_rows, far_rows = edge_rows(x)
    near = lax.ppermute(near_rows, "lat", first_bands + [(j, i) for i, j in first_bands])
    far = lax.ppermute(far_rows, "lat", second_bands + [(j, i) for i, j in second_bands])
    near_x, own, count = outer_columns(x, obs_count)
    own_left, own_right, outer, inner = edge_columns(own, near, far, rows)
    near_x, count, outer, inner = lax.optimization_barrier((near_x, count, outer, inner))
    fold = (obs_index.size // cols, cols)
    taps, conv, out_w, extra, chosen, *spot = spread(
        near_x,
        conv_weight,
        conv_bias,
        out_weight,
        obs_index.reshape(fold),
        count,
        obs_value.reshape(fold),
        obs_weight.reshape(fold),
    )
    between = lax.ppermute(outer, "lon", odd_pairs + [(j, i) for i, j in odd_pairs])
    within = lax.ppermute(inner, "lon", even_pairs + [(j, i) for i, j in even_pairs])
    forecast, notes = run_forecast(
        spot,
        taps,
        near,
        far,
        own_left,
        own_right,
        between,
        within,
        conv,
        out_w,
        chosen,
        extra,
        n_ens * n_lat * n_lon,
    )
    told = lax.all_to_all(notes, ("ens", "lat", "lon"), 0, 0, tiled=True)
    if n_ens == 2:
        other = lax.ppermute(forecast, "ens", [(0, 1), (1, 0)])
        return run_analysis(told, forecast, other, x.shape)[None]
    return many_members(told, forecast, x.shape)[None]


def solution(mesh):
    return jax.shard_map(
        per_device,
        mesh=mesh,
        in_specs=(
            P("ens", None, "lat", "lon"),
            P(),
            P(),
            P(),
            P("lat", "lon", None),
            P("lat", "lon"),
            P("lat", "lon", None),
            P("lat", "lon", None),
        ),
        out_specs=P("ens", None, "lat", "lon"),
        check_vma=False,
    )
```

```python
import functools
import math

import jax
import jax.numpy as jnp
from jax import lax
from jax.experimental import pallas as pl
from jax.experimental.pallas import tpu as pltpu
from jax.sharding import PartitionSpec as P

NS_ITERS = 20
GELU_A = math.sqrt(2.0 / math.pi)
GELU_B = GELU_A * 0.044715
F32 = jnp.float32
BF16 = jnp.bfloat16
PAD = 8
SMALL = 4 << 20
GROUP = 34


def lanes_of(shape):
    return lax.broadcasted_iota(jnp.int32, shape, len(shape) - 1)


def most_of(total, limit):
    return max(d for d in range(1, limit + 1) if total % d == 0)


def edge_rows(x):
    nvar, rows, cols = x.shape
    tile = 8

    def kernel(x_ref, near_ref, far_ref, part, stage, sems):
        copies = []
        for i, first in enumerate((0, rows - tile)):
            copies.append(pltpu.make_async_copy(x_ref.at[:, first : first + tile, :], part.at[i], sems.at[i]))
            copies[i].start()
        ends = []
        for i, first in enumerate((0, tile - 2)):
            copies[i].wait()
            stage[...] = part[i].reshape(nvar * tile, cols).astype(F32)
            both = [stage[pl.ds(first + j, nvar, stride=tile), :] for j in range(2)]
            ends.append(jnp.concatenate(both, axis=0))
        even = lax.axis_index("lat") % 2 == 0
        near_ref[...] = jnp.where(even, ends[1], ends[0]).astype(BF16)
        far_ref[...] = jnp.where(even, ends[0], ends[1]).astype(BF16)

    out = jax.ShapeDtypeStruct((2 * nvar, cols), BF16)
    return pl.pallas_call(
        kernel,
        out_shape=(out, out),
        in_specs=[pl.BlockSpec(memory_space=pltpu.HBM)],
        scratch_shapes=[
            pltpu.VMEM((2, nvar, tile, cols), BF16),
            pltpu.VMEM((nvar * tile, cols), F32),
            pltpu.SemaphoreType.DMA((2,)),
        ],
        compiler_params=pltpu.CompilerParams(vmem_limit_bytes=SMALL),
        name="edge_rows",
    )(pltpu.with_memory_space_constraint(x, pltpu.HBM))


def packed_rows(conv, bias, nvar):
    hid = bias.shape[1]
    high = bias.astype(BF16).astype(F32)
    middle = (bias - high).astype(BF16).astype(F32)
    low = (bias - high - middle).astype(BF16).astype(F32)
    rest = jnp.zeros((PAD - 3, hid), F32)
    pieces = []
    for a in range(3):
        for b in (1, 0, 2):
            at = (3 * a + b) * nvar
            pieces.append(conv[at : at + nvar, :].astype(F32))
        if a == 1:
            pieces.append(jnp.concatenate([high, middle, low, rest], axis=0))
        else:
            pieces.append(jnp.zeros((PAD, hid), F32))
    return jnp.concatenate(pieces, axis=0).T


def outer_kernel(x_hbm, x_ref, own_ref, stage, sem):
    nvar, rows, cols = x_ref.shape
    copy = pltpu.make_async_copy(x_hbm, x_ref, sem)
    copy.start()
    wanted = (0, 1, cols - 2, cols - 1)
    k = lax.broadcasted_iota(jnp.int32, (8, cols), 0)
    lane = lanes_of((8, cols))
    pick = jnp.zeros((8, cols), F32)
    for i, c in enumerate(wanted):
        pick = jnp.where((k == i) & (lane == c), 1.0, pick)
    pick = pick.astype(BF16)
    per = cols // rows
    copy.wait()
    flat = x_ref[...].reshape(nvar * rows, cols)
    taken = lax.dot_general(pick, flat, (((1,), (1,)), ((), ())), preferred_element_type=F32)
    for v in range(nvar):
        part = taken[:, (v // per) * cols : (v // per + 1) * cols]
        shift = (2 - (v % per) * rows) % cols
        stage[8 * v : 8 * v + 8, :] = pltpu.roll(part, shift, 1)
    for i in range(len(wanted)):
        own_ref[i * nvar : (i + 1) * nvar, :] = stage[pl.ds(i, nvar, stride=8), :]


def outer_columns(x):
    nvar, _, cols = x.shape
    return pl.pallas_call(
        outer_kernel,
        out_shape=(jax.ShapeDtypeStruct(x.shape, BF16), jax.ShapeDtypeStruct((4 * nvar, cols), F32)),
        in_specs=[pl.BlockSpec(memory_space=pltpu.HBM)],
        scratch_shapes=[pltpu.VMEM((8 * nvar, cols), F32), pltpu.SemaphoreType.DMA],
        compiler_params=pltpu.CompilerParams(vmem_limit_bytes=SMALL),
        cost_estimate=pl.CostEstimate(flops=10**7, bytes_accessed=2 * 10**6, transcendentals=0),
        name="outer_columns",
    )(pltpu.with_memory_space_constraint(x, pltpu.HBM))


def spread_kernel(
    x_ref,
    conv_hbm,
    bias_hbm,
    out_hbm,
    index_hbm,
    count_ref,
    value_hbm,
    weight_hbm,
    taps_ref,
    packed_ref,
    half_ref,
    extra_ref,
    chosen_ref,
    *rest,
):
    fold = extra_ref.shape[0]
    spot_refs = rest[:fold]
    conv_ref, bias_ref, out_ref, index_ref, value_ref, weight_ref, xf, sems = rest[fold:]
    nvar, rows, cols = x_ref.shape
    block = 3 * nvar + PAD
    small = [
        (conv_hbm, conv_ref),
        (bias_hbm, bias_ref),
        (out_hbm, out_ref),
        (index_hbm, index_ref),
        (value_hbm, value_ref),
        (weight_hbm, weight_ref),
    ]
    copies = []
    for i, (source, target) in enumerate(small):
        copies.append(pltpu.make_async_copy(source, target, sems.at[i]))
        copies[i].start()
    for v in range(nvar):
        column = x_ref[v].astype(F32)
        for r in range(0, rows, 8):
            xf[pl.ds(r * nvar + v, 8, stride=nvar), :] = column[r : r + 8]
    ones = jnp.ones((PAD, cols), F32)

    def fill(r, carry):
        row = xf[pl.ds(pl.multiple_of(r * nvar, 8), nvar), :]
        tap = jnp.concatenate([row, pltpu.roll(row, 1, 1), pltpu.roll(row, cols - 1, 1), ones], axis=0)
        at = pl.multiple_of(r * block, 16)
        taps_ref[pl.ds(at, block), :] = tap.astype(BF16)
        return carry

    lax.fori_loop(0, rows, fill, 0, unroll=8)

    for copy in copies:
        copy.wait()
    packed_ref[...] = packed_rows(conv_ref[...], bias_ref[...], nvar).astype(BF16)
    half_ref[...] = (out_ref[...].astype(F32) * 0.5).astype(BF16)
    index = index_ref[...]
    row = index // cols % rows
    var = index // (rows * cols)
    spot = jnp.clip(row * nvar + var, 0, rows * nvar - 1)
    place = (index % cols).astype(F32)
    for i in range(fold):
        spot_refs[i][...] = spot[i : i + 1, :]
        across = jnp.broadcast_to(place[i : i + 1, :], (cols, cols)).T
        hot = across == lanes_of((cols, cols)).astype(F32)
        chosen_ref[i * cols : (i + 1) * cols, :] = jnp.where(hot, 1.0, 0.0).astype(BF16)
    slot = lanes_of((fold, cols)) + cols * lax.broadcasted_iota(jnp.int32, (fold, cols), 0)
    live = jnp.where(slot < count_ref[0, 0], weight_ref[...], 0.0)
    member = lax.axis_index("ens")
    extra_ref[...] = jnp.where(member == 0, value_ref[...], jnp.where(member == 1, live, 0.0))


def spread(x, conv_weight, conv_bias, out_weight, index, count, value, weight):
    nvar, rows, cols = x.shape
    fold, hid = index.shape[0], conv_bias.shape[0]
    block = 3 * nvar + PAD
    args = (x, conv_weight, conv_bias[None], out_weight.T, index, count, value, weight)
    shape = jax.ShapeDtypeStruct
    scratch = [pltpu.VMEM(arg.shape, arg.dtype) for arg in args[1:5] + args[6:]]
    in_specs = [pl.BlockSpec(memory_space=pltpu.HBM)] * len(args)
    in_specs[0] = pl.BlockSpec(memory_space=pltpu.VMEM)
    in_specs[5] = pl.BlockSpec(memory_space=pltpu.SMEM)
    placed = [pltpu.with_memory_space_constraint(arg, pltpu.HBM) for arg in args]
    placed[0], placed[5] = x, count
    return pl.pallas_call(
        spread_kernel,
        out_shape=(
            shape((rows * block, cols), BF16),
            shape((hid, 3 * block), BF16),
            shape((nvar, hid), BF16),
            shape((fold, cols), F32),
            shape((fold * cols, cols), BF16),
        )
        + (shape((1, cols), jnp.int32),) * fold,
        in_specs=in_specs,
        scratch_shapes=scratch
        + [
            pltpu.VMEM((nvar * rows, cols), F32),
            pltpu.SemaphoreType.DMA((len(args) - 2,)),
        ],
        compiler_params=pltpu.CompilerParams(vmem_limit_bytes=SMALL),
        cost_estimate=pl.CostEstimate(flops=10**8, bytes_accessed=4 * 10**6, transcendentals=0),
        name="spread",
    )(*placed)


def bands(near_ref, far_ref):
    even = lax.axis_index("lat") % 2 == 0
    near, far = near_ref[...].astype(F32), far_ref[...].astype(F32)
    return jnp.where(even, far, near), jnp.where(even, near, far)


def edge_columns(own, near, far, rows):
    nvar, cols = own.shape[0] // 4, own.shape[1]
    wanted = (0, 1, cols - 2, cols - 1)

    def kernel(own_ref, near_ref, far_ref, left_ref, right_ref, between_ref, within_ref):
        lane = lanes_of((nvar, cols))
        halo = []
        for band, first in zip(bands(near_ref, far_ref), (0, rows + 2)):
            for i in range(2):
                halo.append((first + i, band[i * nvar : (i + 1) * nvar, :]))
        outs = []
        for i, c in enumerate(wanted):
            column = own_ref[i * nvar : (i + 1) * nvar, :]
            column = jnp.where(lane < rows + 2, column, 0.0)
            for at, row in halo:
                column = jnp.where(lane == at, pltpu.roll(row, (at - c) % cols, 1), column)
            outs.append(column)
        left, right = jnp.concatenate(outs[:2], axis=0), jnp.concatenate(outs[2:], axis=0)
        even = lax.axis_index("lon") % 2 == 0
        left_ref[...] = left.astype(BF16)
        right_ref[...] = right.astype(BF16)
        between_ref[...] = jnp.where(even, left, right).astype(BF16)
        within_ref[...] = jnp.where(even, right, left).astype(BF16)

    out = jax.ShapeDtypeStruct((2 * nvar, cols), BF16)
    return pl.pallas_call(
        kernel,
        out_shape=(out,) * 4,
        compiler_params=pltpu.CompilerParams(vmem_limit_bytes=SMALL),
        name="edge_columns",
    )(own, near, far)


def gelu2(pre):
    pre = pre.astype(BF16)
    inner = pre * (jnp.asarray(GELU_A, BF16) + jnp.asarray(GELU_B, BF16) * (pre * pre))
    return pre + pre * jnp.tanh(inner)


def forecast_kernel(
    fold,
    *refs,
):
    spot_refs = refs[:fold]
    (
    taps_ref,
    near_ref,
    far_ref,
    own_left_ref,
    own_right_ref,
    between_ref,
    within_ref,
    conv_ref,
    out_w_ref,
    chosen_ref,
    extra_ref,
    forecast_ref,
    notes_ref,
    first,
    second,
    final,
    hidden,
    seen,
    conv,
    out_w,
    ) = refs[fold:]
    nvar, cols = near_ref.shape[0] // 2, near_ref.shape[1]
    block = 3 * nvar + PAD
    rows = taps_ref.shape[0] // block
    deep = 3 * block
    lane = lanes_of((nvar, cols))
    ones = jnp.ones((PAD, cols), F32)

    def tap_rows(row, west, east, at):
        left = jnp.where(lane == 0, pltpu.roll(west, (cols - at) % cols, 1), pltpu.roll(row, 1, 1))
        right = jnp.where(
            lane == cols - 1, pltpu.roll(east, (2 * cols - 1 - at) % cols, 1), pltpu.roll(row, cols - 1, 1)
        )
        return jnp.concatenate([row, left, right, ones], axis=0).astype(BF16)

    def hidden_of(patches):
        return gelu2(jnp.dot(conv[...], patches, preferred_element_type=F32))

    def moved(centre, hidden):
        change = jnp.dot(out_w[...], hidden, preferred_element_type=F32)
        return (centre + change).astype(BF16).astype(F32)

    conv[...] = conv_ref[...]
    out_w[...] = out_w_ref[...]
    even = lax.axis_index("lon") % 2 == 0
    between = between_ref[...].astype(F32)
    within = within_ref[...].astype(F32)
    from_left = jnp.where(even, between, within)
    from_right = jnp.where(even, within, between)
    own_left = own_left_ref[...].astype(F32)
    own_right = own_right_ref[...].astype(F32)
    far_west, west = from_left[:nvar], from_left[nvar:]
    east, far_east = from_right[:nvar], from_right[nvar:]
    inner_west, inner_east = own_left[:nvar], own_right[nvar:]

    for band, start in zip(bands(near_ref, far_ref), (0, rows + 2)):
        for i in range(2):
            row = band[i * nvar : (i + 1) * nvar, :]
            first[(start + i) * block : (start + i + 1) * block, :] = tap_rows(row, west, east, start + i)

    group = lax.broadcasted_iota(jnp.int32, (block, cols), 0)
    wide = lanes_of((block, cols))
    is_left = (group >= nvar) & (group < 2 * nvar) & (wide == 0)
    is_right = (group >= 2 * nvar) & (group < 3 * nvar) & (wide == cols - 1)
    fix = jnp.where(is_left | is_right, 1.0, 0.0).astype(BF16) > 0
    nothing = jnp.zeros((nvar, cols), F32)
    source = jnp.concatenate([nothing, west, pltpu.roll(east, cols - 1, 1), jnp.zeros((PAD, cols), F32)], axis=0)
    source = source.astype(BF16)

    def fill(r, carry):
        at = pl.multiple_of(r * block, 16)
        mine = pltpu.roll(source, cols - 2 - r, 1)
        to = pl.multiple_of((r + 2) * block, 16)
        first[pl.ds(to, block), :] = jnp.where(fix, mine, taps_ref[pl.ds(at, block), :])
        return carry

    lax.fori_loop(0, rows, fill, 0, unroll=4)

    sides = []
    for mid, low, high in ((west, far_west, inner_west), (east, inner_east, far_east)):
        stack = []
        for a in range(3):
            for entry in (mid, low, high):
                stack.append(pltpu.roll(entry, (1 - a) % cols, 1) if a != 1 else entry)
            stack.append(ones)
        sides.append(jnp.concatenate(stack, axis=0).astype(BF16))
    patches = jnp.concatenate(sides, axis=1)
    beside = moved(jnp.concatenate([west, east], axis=1), hidden_of(patches))
    here = lax.axis_index("lat")
    north_in = (here > 0).astype(jnp.int32)
    south_in = (here < lax.axis_size("lat") - 1).astype(jnp.int32)
    keep = jnp.where(lane == 1, north_in, jnp.where(lane == rows + 2, south_in, 1)) > 0
    mid_west = jnp.where(keep, beside[:, :cols], 0.0)
    mid_east = jnp.where(keep, beside[:, cols:], 0.0)

    def ahead(source, at, slot):
        at = pl.multiple_of(at * block, 16)
        patches = jnp.concatenate(
            [source[pl.ds(at, deep), :], source[pl.ds(at + block, deep), :]], axis=1
        )
        hidden[slot] = hidden_of(patches)

    def finish(source, at, slot):
        at = pl.multiple_of(at * block, 16)
        centre = jnp.concatenate(
            [source[pl.ds(at + block, nvar), :], source[pl.ds(at + 2 * block, nvar), :]], axis=1
        ).astype(F32)
        return moved(centre, hidden[slot])

    def first_step(g, carry):
        for q in range(group1):
            ahead(first, 2 * (g * group1 + q), q)
        for q in range(group1):
            i = g * group1 + q
            both = finish(first, 2 * i, q)
            for half in range(2):
                m = 2 * i + half
                good = (jnp.where(m == 0, north_in, 1) * jnp.where(m == rows + 1, south_in, 1)) > 0
                row = both[:, half * cols : (half + 1) * cols]
                row = jnp.where(good, row, 0.0)
                at = pl.multiple_of(m * block, 16)
                second[pl.ds(at, block), :] = tap_rows(row, mid_west, mid_east, m + 1)
        return carry

    group1 = most_of(rows // 2 + 1, hidden.shape[0])
    lax.fori_loop(0, (rows // 2 + 1) // group1, first_step, 0)

    def second_step(g, carry):
        for q in range(group2):
            ahead(second, 2 * (g * group2 + q), q)
        for q in range(group2):
            j = g * group2 + q
            both = finish(second, 2 * j, q)
            both = jnp.concatenate([both[:, :cols], both[:, cols:]], axis=0)
            at = pl.multiple_of(j * 2 * nvar, 16)
            final[pl.ds(at, 2 * nvar), :] = both
            forecast_ref[pl.ds(at, 2 * nvar), :] = both.astype(BF16)
        return carry

    group2 = most_of(rows // 2, hidden.shape[0])
    lax.fori_loop(0, (rows // 2) // group2, second_step, 0)

    for half in range(fold):

        def look(o, carry, half=half):
            seen[pl.ds(half * cols + o, 1), :] = final[pl.ds(spot_refs[half][0, o], 1), :]
            return carry

        lax.fori_loop(0, cols, look, 0, unroll=32)
    masked = seen[...].astype(BF16) * chosen_ref[...]
    values = lax.dot_general(
        jnp.ones((8, cols), BF16), masked, (((1,), (1,)), ((), ())), preferred_element_type=F32
    )
    note = [values[0:1, i * cols : (i + 1) * cols] for i in range(fold)] + [extra_ref[...]]
    note = jnp.concatenate(note, axis=0).astype(BF16)
    for d in range(notes_ref.shape[0]):
        notes_ref[d] = note


def run_forecast(spot, taps, near, far, own_left, own_right, between, within, conv, out_w, chosen, extra, devices):
    nvar, cols = near.shape[0] // 2, near.shape[1]
    slots = len(spot) * cols
    block = 3 * nvar + PAD
    rows = taps.shape[0] // block
    smem = pl.BlockSpec(memory_space=pltpu.SMEM)
    vmem = pl.BlockSpec(memory_space=pltpu.VMEM)
    return pl.pallas_call(
        functools.partial(forecast_kernel, len(spot)),
        out_shape=(
            jax.ShapeDtypeStruct((rows * nvar, cols), BF16),
            jax.ShapeDtypeStruct((devices, 2 * extra.shape[0], cols), BF16),
        ),
        in_specs=[smem] * len(spot) + [vmem] * 11,
        out_specs=(vmem, vmem),
        scratch_shapes=[
            pltpu.VMEM(((rows + 4) * block, cols), BF16),
            pltpu.VMEM(((rows + 2) * block, cols), BF16),
            pltpu.VMEM((rows * nvar, cols), F32),
            pltpu.VMEM((GROUP, conv.shape[0], 2 * cols), BF16),
            pltpu.VMEM((slots, cols), F32),
            pltpu.VMEM(conv.shape, BF16),
            pltpu.VMEM(out_w.shape, BF16),
        ],
        compiler_params=pltpu.CompilerParams(vmem_limit_bytes=24 << 20),
        name="forecast",
    )(*spot, taps, near, far, own_left, own_right, between, within, conv, out_w, chosen, extra)


def pair_weights(gram, proj):
    count = len(proj)
    system = [[gram[k][m] + (float(count - 1) if k == m else 0.0) for m in range(count)] for k in range(count)]
    total = sum(entry * entry for line in system for entry in line)
    scale = jnp.sqrt(total)
    one = jnp.ones_like(scale)
    eye = [[one if k == m else 0.0 * one for m in range(count)] for k in range(count)]

    def times(left, right):
        return [
            [sum(left[k][j] * right[j][m] for j in range(count)) for m in range(count)] for k in range(count)
        ]

    current = [[entry / scale for entry in line] for line in system]
    inverse = eye
    for _ in range(NS_ITERS):
        both = times(inverse, current)
        factor = [[1.5 * eye[k][m] - 0.5 * both[k][m] for m in range(count)] for k in range(count)]
        current = times(current, factor)
        inverse = times(factor, inverse)
    root = jnp.sqrt(scale)
    root_inv = [[entry / root for entry in line] for line in inverse]
    half = [sum(root_inv[k][j] * proj[j] for j in range(count)) for k in range(count)]
    mean_w = [sum(root_inv[k][j] * half[j] for j in range(count)) for k in range(count)]
    span = math.sqrt(count - 1.0)
    full = [[mean_w[k] + span * root_inv[k][m] for m in range(count)] for k in range(count)]
    centre = [sum(full[k][m] for k in range(count)) / count for m in range(count)]
    return [[1.0 / count + full[k][m] - centre[m] for m in range(count)] for k in range(count)]


def analysis_kernel(told_ref, mine_ref, other_ref, out_ref, blended, packed, sems):
    count = lax.axis_size("ens")
    nvar, rows, cols = packed.shape[1], out_ref.shape[1], packed.shape[3]
    depth = told_ref.shape[1]
    told = told_ref[...].astype(F32).reshape(count, -1, cols)
    fold = depth // 2
    size = told.shape[1]
    hx = [told[k] for k in range(count)]
    value = pltpu.roll(told[0], size - fold, 0)
    weight = pltpu.roll(told[1], size - fold, 0)
    used = lax.broadcasted_iota(jnp.int32, (size, cols), 0) % depth < fold
    weight = jnp.where(used, weight, 0.0)
    mean = sum(hx) / count
    spread_of = [h - mean for h in hx]
    innov = value - mean
    tile = (8, cols)

    def total(term):
        return jnp.broadcast_to(jnp.sum(term, keepdims=True), tile)

    scaled = [part * weight for part in spread_of]
    gram = [[None] * count for _ in range(count)]
    for k in range(count):
        for m in range(k, count):
            gram[k][m] = gram[m][k] = total(scaled[k] * spread_of[m])
    weights = pair_weights(gram, [total(scaled[k] * innov) for k in range(count)])
    me = lax.axis_index("ens")
    mine = jnp.where(me == 0, weights[0][0], weights[1][1])[0:1, :]
    other = jnp.where(me == 0, weights[1][0], weights[0][1])[0:1, :]
    high = packed.shape[2]

    def copy_of(c):
        return pltpu.make_async_copy(packed.at[c], out_ref.at[:, pl.ds(c * high, high), :], sems.at[c])

    for c in range(rows // high):
        at = c * high * nvar
        part = slice(at, at + high * nvar)
        blended[c] = mine * mine_ref[part, :].astype(F32) + other * other_ref[part, :].astype(F32)
        for v in range(nvar):
            for r in range(0, high, 16):
                halves = [blended[c, pl.ds((r + 8 * i) * nvar + v, 8, stride=nvar), :] for i in range(2)]
                packed[c, v, r : r + 16, :] = jnp.concatenate(halves, axis=0).astype(BF16)
        copy_of(c).start()
    for c in range(rows // high):
        copy_of(c).wait()


def run_analysis(told, mine, other, shape):
    nvar, rows, cols = shape
    high = 16
    vmem = pl.BlockSpec(memory_space=pltpu.VMEM)
    return pl.pallas_call(
        analysis_kernel,
        out_shape=jax.ShapeDtypeStruct(shape, BF16),
        in_specs=[vmem, vmem, vmem],
        out_specs=pl.BlockSpec(memory_space=pltpu.HBM),
        scratch_shapes=[
            pltpu.VMEM((rows // high, high * nvar, cols), F32),
            pltpu.VMEM((rows // high, nvar, high, cols), BF16),
            pltpu.SemaphoreType.DMA((rows // high,)),
        ],
        compiler_params=pltpu.CompilerParams(vmem_limit_bytes=8 << 20),
        name="analysis",
    )(told, mine, other)


def blend_weights(gram, proj):
    entries_number = gram.shape[0]
    eye = jnp.eye(entries_number, dtype=gram.dtype)
    system = (entries_number - 1) * eye + gram
    scale = jnp.sqrt(jnp.sum(system * system))
    current = system / scale
    inverse = eye
    for _ in range(NS_ITERS):
        factor = 1.5 * eye - 0.5 * jnp.dot(inverse, current, precision=lax.Precision.HIGHEST)
        current = jnp.dot(current, factor, precision=lax.Precision.HIGHEST)
        inverse = jnp.dot(factor, inverse, precision=lax.Precision.HIGHEST)
    root_inv = inverse / jnp.sqrt(scale)
    half = jnp.dot(root_inv, proj, precision=lax.Precision.HIGHEST)
    mean_w = jnp.dot(root_inv, half, precision=lax.Precision.HIGHEST)
    full = mean_w[:, None] + math.sqrt(entries_number - 1.0) * root_inv
    return 1.0 / entries_number + full - jnp.mean(full, axis=0, keepdims=True)


def many_members(told, forecast, shape):
    nvar, rows, cols = shape
    fold = told.shape[1] // 2
    told = told.astype(F32).reshape(lax.axis_size("ens"), -1, *told.shape[1:])
    members = told[:, :, :fold, :].reshape(told.shape[0], -1)
    value = told[0, :, fold:, :].reshape(-1)
    weight = told[1, :, fold:, :].reshape(-1)
    mean = jnp.mean(members, axis=0)
    spread = members - mean[None, :]
    innov = value - mean
    weighted = spread * weight[None, :]
    gram = jnp.dot(weighted, spread.T, precision=lax.Precision.HIGHEST)
    proj = jnp.dot(weighted, innov, precision=lax.Precision.HIGHEST)
    transform = blend_weights(gram, proj)
    column = lax.dynamic_slice_in_dim(transform, lax.axis_index("ens"), 1, 1)[:, 0]
    everyone = lax.all_gather(forecast[None], "ens", axis=0, tiled=True)
    blended = jnp.tensordot(column, everyone.astype(F32), axes=1, precision=lax.Precision.HIGHEST)
    return blended.astype(BF16).reshape(rows, nvar, cols).transpose(1, 0, 2)


def per_device(
    sample_quantities,
    conv_weight,
    conv_bias,
    out_weight,
    obs_index,
    obs_count,
    obs_value,
    obs_weight,
):
    x = sample_quantities[0]
    _, rows, cols = x.shape
    n_ens, n_lat, n_lon = (lax.axis_size(axis) for axis in ("ens", "lat", "lon"))
    assert n_lon % 2 == 0
    first_bands = [(i, i + 1) for i in range(0, n_lat - 1, 2)]
    second_bands = [(i, i + 1) for i in range(1, n_lat - 1, 2)]
    odd_pairs = [(i, (i + 1) % n_lon) for i in range(1, n_lon, 2)]
    even_pairs = [(i, i + 1) for i in range(0, n_lon, 2)]

    near_rows, far_rows = edge_rows(x)
    near = lax.ppermute(near_rows, "lat", first_bands + [(j, i) for i, j in first_bands])
    far = lax.ppermute(far_rows, "lat", second_bands + [(j, i) for i, j in second_bands])
    near_x, own = outer_columns(x)
    own_left, own_right, outer, inner = edge_columns(own, near, far, rows)
    near_x, count, outer, inner = lax.optimization_barrier((near_x, obs_count, outer, inner))
    fold = (obs_index.size // cols, cols)
    taps, conv, out_w, extra, chosen, *spot = spread(
        near_x,
        conv_weight,
        conv_bias,
        out_weight,
        obs_index.reshape(fold),
        count,
        obs_value.reshape(fold),
        obs_weight.reshape(fold),
    )
    between = lax.ppermute(outer, "lon", odd_pairs + [(j, i) for i, j in odd_pairs])
    within = lax.ppermute(inner, "lon", even_pairs + [(j, i) for i, j in even_pairs])
    forecast, notes = run_forecast(
        spot,
        taps,
        near,
        far,
        own_left,
        own_right,
        between,
        within,
        conv,
        out_w,
        chosen,
        extra,
        n_ens * n_lat * n_lon,
    )
    told = lax.all_to_all(notes, ("ens", "lat", "lon"), 0, 0, tiled=True)
    if n_ens == 2:
        other = lax.ppermute(forecast, "ens", [(0, 1), (1, 0)])
        return run_analysis(told, forecast, other, x.shape)[None]
    return many_members(told, forecast, x.shape)[None]


def solution(mesh):
    return jax.shard_map(
        per_device,
        mesh=mesh,
        in_specs=(
            P("ens", None, "lat", "lon"),
            P(),
            P(),
            P(),
            P("lat", "lon", None),
            P("lat", "lon"),
            P("lat", "lon", None),
            P("lat", "lon", None),
        ),
        out_specs=P("ens", None, "lat", "lon"),
        check_vma=False,
    )
```
